128 devices in a mesh: sub: 32 (over x, y_hi, z), lib: 4 (over y_lo, core).
Axes of the slice: x: 4, y: 4 (y_hi: 2, y_lo: 2; y = y_hi * 2 + y_lo), z: 4, core: 2. Of those that a mesh axis runs over, the one named last changes fastest.
Arguments:
- snap_start: bfloat16 [4, 256, 128, 256], P(None, 'sub'), may hold values from -20 to 20
- snap_end: bfloat16 [4, 256, 128, 256], P(None, 'sub'), may hold values from -20 to 20
- exponents: int32 [512, 7], P('lib'), may hold values from 0 to 2, as said below
Outputs:
- coefficients: float32 [4, 512], P(None, 'lib')
- fitted: float32 [4, 16384], P(None, ('sub', 'lib'))
The draws below stay inside these ranges and needn't reach their ends.
Inputs may be any that keep to these rules, and one draw needn't show every extreme that they name: Each row holds four field exponents of 0 to 2 with total degree 1 to 3, then three derivative orders of 0 to 2; rows are distinct, each of the 30 such monomials appears in one row whose derivative orders are all zero, and each of the four fields to the first power alone appears with derivative orders (0, 0, 1) and with (0, 1, 1).
All inputs are finite; a program needn't handle non-finite values.
Results may differ from the reference program's by a relative error of at most 0.0024.
Values may be sent and summed in bfloat16 or wider, within the bound.
A program may use at most 64 MiB of HBM per device.

```python
import jax
import jax.numpy as jnp
from jax import lax

NY = 128
NZ = 256
TERMS = 512
STRIDE = 8
RADIUS = 8
POWER = 6
ITERS = 10
NX = 256


def depth_slope(values):
    return 0.5 * (jnp.roll(values, -1, axis=2) - jnp.roll(values, 1, axis=2))


def cross_slope(values):
    across = jnp.roll(values, -1, axis=1) - jnp.roll(values, 1, axis=1)
    return 0.25 * (jnp.roll(across, -1, axis=2) - jnp.roll(across, 1, axis=2))


def draw_fields(key):
    base_key = jax.random.fold_in(key, 11)
    grid_shape = (4, NX, NY, NZ)
    position = jnp.arange(NX, dtype=jnp.float32) / NX
    amplitude = jnp.exp(jnp.log(1.5) * position)[None, :, None, None]
    rough_part = jnp.clip(jax.random.normal(jax.random.fold_in(base_key, 1), grid_shape, jnp.float32), -4.0, 4.0)
    start_field = amplitude * rough_part
    noise_part = jnp.clip(jax.random.normal(jax.random.fold_in(base_key, 3), grid_shape, jnp.float32), -4.0, 4.0)
    forcing = jnp.stack([-start_field[1] * start_field[2] + 0.5 * start_field[3], start_field[0] * start_field[2] - 0.5 * start_field[0], -start_field[0] * start_field[1] + 0.3 * start_field[2] * start_field[2], start_field[0] * start_field[0] - start_field[1] * start_field[1]])
    transport = jnp.stack([1.2 * depth_slope(start_field[2]), 1.2 * depth_slope(start_field[0]), 3.0 * cross_slope(start_field[3]), 3.0 * cross_slope(start_field[1])])
    end_field = start_field + 0.25 * forcing + transport + 0.25 * noise_part
    end_field = jnp.clip(end_field, -19.5, 19.5)
    return (start_field, end_field)


def draw_snap_start(key, part):
    return draw_fields(key)[0].astype(jnp.bfloat16)


def draw_snap_end(key, part):
    return draw_fields(key)[1].astype(jnp.bfloat16)


def monomial_powers():
    power_rows = []
    for first in range(3):
        for second in range(3):
            for third in range(3):
                for fourth in range(3):
                    degree = first + second + third + fourth
                    if degree >= 1 and degree <= 3:
                        power_rows.append([first, second, third, fourth])
    return power_rows


def draw_exponents(key, part):
    power_rows = monomial_powers()
    monomials = len(power_rows)
    power_table = jnp.asarray(power_rows, dtype=jnp.int32)
    single_rows = [[1, 0, 0, 0], [0, 1, 0, 0], [0, 0, 1, 0], [0, 0, 0, 1]]
    forced_list = []
    for single in single_rows:
        position_here = power_rows.index(single)
        forced_list.append(position_here * 27 + 1)
        forced_list.append(position_here * 27 + 4)
    drawn_list = [index * 27 for index in range(monomials)]
    other_list = [index * 27 + order for index in range(monomials) for order in range(1, 27) if index * 27 + order not in forced_list]
    drawn_codes = jnp.asarray(drawn_list + forced_list, dtype=jnp.int32)
    other_codes = jnp.asarray(other_list, dtype=jnp.int32)
    chosen = jax.random.permutation(jax.random.fold_in(key, 21), other_codes)[:TERMS - len(drawn_list) - len(forced_list)]
    code_list = jnp.concatenate([drawn_codes, chosen])
    code_list = jax.random.permutation(jax.random.fold_in(key, 22), code_list)
    monomial_index = code_list // 27
    derivative = code_list % 27
    powers = power_table[monomial_index]
    orders = jnp.stack([derivative // 9, derivative // 3 % 3, derivative % 3], axis=1)
    return jnp.concatenate([powers, orders], axis=1).astype(jnp.int32)


def setup_inputs(seed: int = 0) -> dict:
    keys = jax.random.split(jax.random.key(seed), 4)
    return {
        "snap_start": draw_snap_start(jax.random.fold_in(keys[3], 71), 0),
        "snap_end": draw_snap_end(jax.random.fold_in(keys[3], 71), 0),
        "exponents": draw_exponents(jax.random.fold_in(keys[3], 71), 0),
    }


highest = lax.Precision.HIGHEST
ridge_term = 0.1
shrink = 0.05
epsilon = 1e-06

def tap_table(length, centers_count, offset):
    cell_pos = jnp.arange(length, dtype=jnp.float32)
    centers = STRIDE * jnp.arange(centers_count, dtype=jnp.float32) + offset
    scaled = (cell_pos[:, None] - centers[None, :]) / RADIUS
    inside = jnp.abs(scaled) <= 1.0
    bump_base = 1.0 - scaled * scaled
    zeroth = bump_base * bump_base * bump_base
    first_order = 6.0 * scaled * bump_base * bump_base
    second = -6.0 * bump_base * (1.0 - 5.0 * scaled * scaled)
    stacked = jnp.stack([zeroth, first_order, second])
    return jnp.where(inside[None], stacked, jnp.zeros_like(stacked))

def monomial(fields, powers):
    result = jnp.ones(fields.shape[1:], jnp.float32)
    for channel in range(4):
        values = fields[channel]
        power_here = powers[channel]
        factor = jnp.where(power_here == 0, jnp.ones_like(values), jnp.where(power_here == 1, values, values * values))
        result = result * factor
    return result

def weak_form(theta_field, x_taps, y_taps, z_taps):
    depth_x, height, width_z = theta_field.shape
    reduced = jnp.dot(theta_field.astype(jnp.bfloat16).reshape(-1, width_z), z_taps.astype(jnp.bfloat16), preferred_element_type=jnp.float32)
    reduced = reduced.reshape(depth_x, height, -1)
    reduced = jnp.einsum('xyc,yb->xbc', reduced, y_taps, precision=highest)
    reduced = jnp.einsum('xbc,xa->abc', reduced, x_taps, precision=highest)
    return reduced.reshape(-1)

def reference(snap_start, snap_end, exponents):
    start_field = snap_start.astype(jnp.float32)
    change = (snap_end.astype(jnp.float32) - start_field).astype(jnp.bfloat16)
    x_table = tap_table(NX, NX // STRIDE, 0)
    y_table = tap_table(NY, NY // STRIDE, 0)
    z_table = tap_table(NZ, NZ // STRIDE, 0)

    def one_term(term_row):
        theta_field = monomial(start_field, term_row[:4])
        return weak_form(theta_field, x_table[term_row[4]], y_table[term_row[5]], z_table[term_row[6]])

    def one_target(field_diff):
        return weak_form(field_diff, x_table[0], y_table[0], z_table[0])
    library = lax.map(one_term, exponents)
    targets = lax.map(one_target, change)
    gram_matrix = jnp.dot(library, library.T, precision=highest, preferred_element_type=jnp.float32)
    cross_terms = jnp.dot(library, targets.T, precision=highest, preferred_element_type=jnp.float32)
    squares = lax.optimization_barrier(jnp.sum(library * library, axis=1))
    target_squares = lax.optimization_barrier(jnp.sum(targets * targets, axis=1))
    total_rows = library.shape[1]
    column_scale = jnp.sqrt(squares / total_rows + epsilon)
    target_scale = jnp.sqrt(target_squares / total_rows + epsilon)
    normal_gram = gram_matrix / (total_rows * column_scale[:, None] * column_scale[None, :]) + ridge_term * jnp.eye(TERMS, dtype=jnp.float32)
    normal_cross = cross_terms / (total_rows * column_scale[:, None] * target_scale[None, :])
    vector = jnp.full((TERMS,), TERMS ** (-0.5), jnp.float32)
    magnitude = jnp.ones((), jnp.float32)
    for sweep_index in range(POWER):
        applied = jnp.dot(normal_gram, vector, precision=highest)
        magnitude = jnp.sqrt(jnp.sum(applied * applied))
        vector = applied / magnitude
    step_size = 1.0 / magnitude
    coeffs = jnp.zeros((4, TERMS), jnp.float32)
    for sweep_index in range(ITERS):
        gradient = jnp.dot(normal_gram, coeffs.T, precision=highest).T - normal_cross.T
        moved_coef = coeffs - step_size * gradient
        coeffs = jnp.sign(moved_coef) * jnp.maximum(jnp.abs(moved_coef) - step_size * shrink, 0.0)
    fitted = jnp.dot(coeffs / column_scale[None, :], library, precision=highest, preferred_element_type=jnp.float32)
    return (coeffs, fitted)
```

```python
import functools

import jax
import jax.numpy as jnp
import ml_dtypes
import numpy as np
from jax import lax
from jax.experimental import pallas as pl
from jax.experimental.pallas import tpu as pltpu
from jax.sharding import PartitionSpec as P

STRIDE = 8
RADIUS = 8
POWER = 6
ITERS = 10
TERMS = 512
ROWS = 16384
RIDGE = 0.1
SHRINK = 0.05
EPSILON = 1e-06

CELLS_X = 8
CELLS_Y = 40
CELLS_XY = CELLS_X * CELLS_Y
WIDTH_Z = 256
CENTERS_Y = 4
CENTERS_Z = 32
TESTS = CENTERS_Y * CENTERS_Z

POWERS = [
    (a, b, c, e)
    for a in range(3)
    for b in range(3)
    for c in range(3)
    for e in range(3)
    if 1 <= a + b + c + e <= 3
]
PRODUCTS = len(POWERS) + 4
PAD = 16
TABLE = PRODUCTS * PAD
KEYS = 3 * TABLE
PICKED = TERMS + 16
TARGET_CODE = 4000

CHUNK = 16
BLOCKS = (
    ((0, 0), (0, 1), (0, 2), (0, 3), (3, 3)),
    ((1, 1), (1, 2), (1, 3), (2, 2), (2, 3)),
)
CHUNKS = 8 * len(BLOCKS[0]) + 1
CHIPS = 64
SPREAD = 25
UNSPREAD = 41

MESH = pl.DeviceIdType.MESH
f32 = jnp.float32
bf16 = jnp.bfloat16


def tap(order, offset):
    s = np.asarray(offset, np.float64) / RADIUS
    base = 1.0 - s * s
    value = (base**3, 6.0 * s * base**2, -6.0 * base * (1.0 - 5.0 * s * s))[order]
    return np.where(np.abs(s) <= 1.0, value, 0.0)


def split_pieces(values):
    high = values.astype(ml_dtypes.bfloat16)
    low = (values - high.astype(np.float64)).astype(ml_dtypes.bfloat16)
    return high, low


def plane_weights():
    x = np.arange(CELLS_X)[:, None]
    y = np.arange(CELLS_Y)[None, :]
    both = []
    for shift in (0, STRIDE):
        full = np.zeros((2, CENTERS_Y, PAD, CELLS_X, CELLS_Y))
        for side in range(2):
            for center in range(CENTERS_Y):
                for order_x in range(3):
                    for order_y in range(3):
                        full[side, center, order_x * 3 + order_y] = tap(
                            order_x, x - STRIDE * side
                        ) * tap(order_y, y - STRIDE * center - shift)
        high, low = split_pieces(full.reshape(2 * CENTERS_Y * PAD, CELLS_XY))
        both.append(np.concatenate([high, low]))
    return np.stack(both)


def depth_weights():
    z = np.arange(WIDTH_Z)[:, None]
    centers = STRIDE * np.arange(CENTERS_Z)[None, :]
    full = np.zeros((CENTERS_Y, WIDTH_Z, 3, CENTERS_Y, CENTERS_Z))
    for order in range(3):
        for center in range(CENTERS_Y):
            full[center, :, order, center, :] = tap(order, z - centers)
    return full.reshape(CENTERS_Y * WIDTH_Z, 3 * TESTS).astype(ml_dtypes.bfloat16)


def column_codes():
    codes = np.full((3, PRODUCTS, PAD), -2.0, np.float32)
    for index, (a, b, c, e) in enumerate(POWERS):
        for order_z in range(3):
            for plane in range(9):
                codes[order_z, index, plane] = (
                    (((a * 3 + b) * 3 + c) * 3 + e) * 27 + plane * 3 + order_z
                )
    for field in range(4):
        codes[0, len(POWERS) + field, 0] = TARGET_CODE + field
    return codes.reshape(1, KEYS)


def code_weights():
    return np.array([[729, 243, 81, 27, 9, 3, 1]], np.float32)


def position():
    sub = lax.axis_index("sub")
    lib = lax.axis_index("lib")
    return sub // 8, (sub // 4) % 2 * 2 + lib // 2, sub % 4, lib % 2


def chip_device(chip, core):
    y = chip // 4 % 4
    return {"sub": (chip // 16 * 2 + y // 2) * 4 + chip % 4, "lib": y % 2 * 2 + core}


def products(fields_ref, later_ref, wide_ref, theta_ref):
    for field in range(4):
        for x in range(CELLS_X):
            wide_ref[field, x * CELLS_Y : (x + 1) * CELLS_Y, :] = fields_ref[field, x].astype(f32)
            wide_ref[4 + field, x * CELLS_Y : (x + 1) * CELLS_Y, :] = later_ref[field, x].astype(
                f32
            )

    def rows(step, carry):
        at = pl.multiple_of(step * 16, 16)
        value = [wide_ref[field, pl.ds(at, 16), :] for field in range(4)]
        square = [v * v for v in value]
        pairs = {}
        for index, powers in enumerate(POWERS):
            result = None
            key = ()
            for field, power in enumerate(powers):
                if power == 0:
                    continue
                factor = value[field] if power == 1 else square[field]
                key = key + ((field, power),)
                if result is None:
                    result = factor
                elif key in pairs:
                    result = pairs[key]
                else:
                    result = result * factor
                    pairs[key] = result
            theta_ref[index, pl.ds(at, 16), :] = result.astype(bf16)
        for field in range(4):
            change = wide_ref[4 + field, pl.ds(at, 16), :] - value[field]
            theta_ref[len(POWERS) + field, pl.ds(at, 16), :] = change.astype(bf16)
        return carry

    lax.fori_loop(0, CELLS_XY // 16, rows, 0)


def plane_sums(weights_ref, theta_ref, plane_ref):
    half = 2 * CENTERS_Y * PAD

    def one(index, carry):
        both = jnp.dot(weights_ref[...], theta_ref[index], preferred_element_type=f32)
        total = both[:half] + both[half:]
        high = total.astype(bf16)
        low = (total - high.astype(f32)).astype(bf16)
        at = pl.multiple_of(index * PAD, PAD)
        for side in range(2):
            for center in range(CENTERS_Y):
                row = (side * CENTERS_Y + center) * PAD
                lanes = slice(center * WIDTH_Z, (center + 1) * WIDTH_Z)
                plane_ref[side, 0, pl.ds(at, PAD), lanes] = high[row : row + PAD]
                plane_ref[side, 1, pl.ds(at, PAD), lanes] = low[row : row + PAD]
        return carry

    lax.fori_loop(0, PRODUCTS, one, 0)


def depth_sums(plane_ref, depth_ref, table_ref, side):
    size = 2 * PAD * 17 // 2
    for start in range(0, TABLE, size):
        high = jnp.dot(
            plane_ref[side, 0, start : start + size], depth_ref[...], preferred_element_type=f32
        )
        low = jnp.dot(
            plane_ref[side, 1, start : start + size], depth_ref[...], preferred_element_type=f32
        )
        total = high + low
        top = total.astype(bf16)
        rest = (total - top.astype(f32)).astype(bf16)
        for order in range(3):
            lanes = slice(order * TESTS, (order + 1) * TESTS)
            rows = slice(order * TABLE + start, order * TABLE + start + size)
            table_ref[rows, :TESTS] = top[:, lanes]
            table_ref[rows, TESTS:] = rest[:, lanes]


def pick_table(codes_ref, keys_ref, pick_ref):
    for row in range(0, PICKED, 16):
        code = codes_ref[row // 128, row % 128 : row % 128 + 16, :]
        for column in range(0, KEYS, 128):
            width = min(128, KEYS - column)
            same = code[:, :width] == keys_ref[:, column : column + width]
            pick_ref[row : row + 16, column : column + width] = jnp.where(same, 1.0, 0.0).astype(
                bf16
            )


def whole_dot(left, right, contract):
    return lax.dot_general(
        left,
        right,
        (((1,), (contract,)), ((), ())),
        precision=lax.Precision.HIGHEST,
        preferred_element_type=f32,
    )


def solve(gram_ref, normal_ref, lib_ref, cross, target_squares, lib, coef_ref, fit_ref, spot_ref):
    total = float(ROWS)
    diagonal_row = []
    diagonal_column = []
    same = lax.broadcasted_iota(jnp.int32, (128, 128), 0) == lax.broadcasted_iota(
        jnp.int32, (128, 128), 1
    )
    for block in range(4):
        at = slice(block * 128, block * 128 + 128)
        spread = jnp.where(same, gram_ref[at, at], 0.0)
        diagonal_row.append(jnp.sum(spread, axis=0, keepdims=True))
        diagonal_column.append(jnp.sum(spread, axis=1, keepdims=True))
    inverse_row = [1.0 / jnp.sqrt(d / total + EPSILON) for d in diagonal_row]
    inverse_column = [1.0 / jnp.sqrt(d / total + EPSILON) for d in diagonal_column]
    for i in range(4):
        for j in range(4):
            rows, lanes = slice(i * 128, i * 128 + 128), slice(j * 128, j * 128 + 128)
            block = gram_ref[rows, lanes] * (inverse_column[i] / total) * inverse_row[j]
            if i == j:
                block = block + jnp.where(same, RIDGE, 0.0)
            high = block.astype(bf16)
            normal_ref[rows, lanes] = high
            normal_ref[rows, slice(TERMS + j * 128, TERMS + j * 128 + 128)] = (
                block - high.astype(f32)
            ).astype(bf16)
    inverse = jnp.concatenate(inverse_row, axis=1)
    target_scale = 1.0 / jnp.sqrt(target_squares / total + EPSILON)
    normal_cross = cross * inverse * (target_scale / total)

    def apply(rows):
        high = rows.astype(bf16)
        low = (rows - high.astype(f32)).astype(bf16)
        stacked = jnp.concatenate([high, low], axis=0)
        both = jnp.dot(stacked, normal_ref[...], preferred_element_type=f32)
        return both[:8, :TERMS] + both[:8, TERMS:] + both[8:, :TERMS]

    vector = jnp.full((8, TERMS), TERMS**-0.5, f32)
    magnitude = None
    for _ in range(POWER):
        applied = apply(vector)
        magnitude = jnp.sqrt(jnp.sum(applied * applied, axis=1, keepdims=True))
        vector = applied / magnitude
    step_size = 1.0 / magnitude
    bound = step_size * SHRINK
    coeffs = None
    for sweep in range(ITERS):
        if sweep == 0:
            moved = step_size * normal_cross
        else:
            moved = coeffs - step_size * (apply(coeffs) - normal_cross)
        coeffs = jnp.maximum(moved - bound, 0.0) - jnp.maximum(-moved - bound, 0.0)
    spot_ref[...] = coeffs
    own = pl.multiple_of(lib * 128, 128)
    coef_ref[...] = spot_ref[:, pl.ds(own, 128)][:4]
    fit_ref[...] = whole_dot(coeffs * inverse, lib_ref[:TERMS], 0)[:4]


def kernel(
    exponents_ref,
    code_weight_ref,
    keys_ref,
    start_ref,
    end_ref,
    plane_weight_ref,
    depth_weight_ref,
    coef_ref,
    fit_ref,
    fields_ref,
    later_ref,
    weights_ref,
    depth_ref,
    wide_ref,
    theta_ref,
    plane_ref,
    table_ref,
    codes_ref,
    pick_ref,
    edge_out_ref,
    edge_in_ref,
    lib_ref,
    gram_ref,
    half_ref,
    half_in_ref,
    part_ref,
    parts_in_ref,
    done_ref,
    other_ref,
    normal_ref,
    spot_ref,
    local_sems,
    code_sems,
    edge_sems,
    core_sems,
    part_sems,
    done_sems,
    other_sems,
):
    sub = lax.axis_index("sub")
    lib = lax.axis_index("lib")
    x, y, z, core = position()
    chip = (x * 4 + y) * 4 + z
    next_sub = {"sub": (sub + 1) % 32, "lib": lib}
    last_sub = {"sub": (sub + 31) % 32, "lib": lib}
    other_core = {"sub": sub, "lib": lib + 1 - 2 * core}
    window = pl.ds(pl.multiple_of(jnp.maximum(lib * 32 - 8, 0), 8), CELLS_Y)
    loads = [
        pltpu.make_async_copy(start_ref.at[:, :, window, :], fields_ref, local_sems.at[0]),
        pltpu.make_async_copy(end_ref.at[:, :, window, :], later_ref, local_sems.at[1]),
        pltpu.make_async_copy(
            plane_weight_ref.at[jnp.minimum(lib, 1)], weights_ref, local_sems.at[2]
        ),
        pltpu.make_async_copy(depth_weight_ref, depth_ref, local_sems.at[3]),
    ]
    for load in loads:
        load.start()

    barrier = pltpu.get_barrier_semaphore()

    def greet(step, carry):
        pl.semaphore_signal(
            barrier,
            inc=1,
            device_id=chip_device((chip + step) % CHIPS, core),
            device_id_type=MESH,
        )
        return carry

    lax.fori_loop(1, CHIPS, greet, 0)
    for device in (
        next_sub,
        last_sub,
        {"sub": sub, "lib": (lib + 1) % 4},
        {"sub": sub, "lib": (lib + 2) % 4},
        {"sub": sub, "lib": (lib + 3) % 4},
    ):
        pl.semaphore_signal(barrier, inc=1, device_id=device, device_id_type=MESH)

    code = jnp.sum(
        exponents_ref[...].astype(f32) * code_weight_ref[...], axis=1, keepdims=True
    )
    codes_ref[lib] = jnp.broadcast_to(code, (128, 128))
    row = lax.broadcasted_iota(jnp.int32, (16, 128), 0)
    codes_ref[4, :16, :] = jnp.where(row < 4, TARGET_CODE + row, -1).astype(f32)

    pl.semaphore_wait(barrier, CHIPS - 1 + 5)
    code_copies = [
        pltpu.make_async_remote_copy(
            src_ref=codes_ref.at[lib],
            dst_ref=codes_ref.at[lib],
            send_sem=code_sems.at[step],
            recv_sem=code_sems.at[3 + step],
            device_id={"sub": sub, "lib": (lib + 1 + step) % 4},
            device_id_type=MESH,
        )
        for step in range(3)
    ]
    for copy in code_copies:
        copy.start()

    loads[0].wait()
    loads[1].wait()
    products(fields_ref, later_ref, wide_ref, theta_ref)
    loads[2].wait()
    plane_sums(weights_ref, theta_ref, plane_ref)
    loads[3].wait()
    depth_sums(plane_ref, depth_ref, table_ref.at[1], 1)
    for copy in code_copies:
        copy.wait()
    pick_table(codes_ref, keys_ref, pick_ref)
    both = jnp.dot(pick_ref[...], table_ref[1], preferred_element_type=f32)
    edge_out_ref[...] = (both[:, :TESTS] + both[:, TESTS:]).astype(bf16)
    edge = pltpu.make_async_remote_copy(
        src_ref=edge_out_ref,
        dst_ref=edge_in_ref,
        send_sem=edge_sems.at[0],
        recv_sem=edge_sems.at[1],
        device_id=next_sub,
        device_id_type=MESH,
    )
    edge.start()
    depth_sums(plane_ref, depth_ref, table_ref.at[0], 0)
    both = jnp.dot(pick_ref[...], table_ref[0], preferred_element_type=f32)
    lib_ref[...] = both[:, :TESTS] + both[:, TESTS:]
    edge.wait()
    keep = jnp.where(sub > 0, 1.0, 0.0).astype(f32)
    lib_ref[...] = lib_ref[...] + keep * edge_in_ref[...].astype(f32)

    library = lib_ref[:TERMS]
    gram_ref[...] = whole_dot(library, library, 1)
    target = lib_ref[TERMS : TERMS + 8]
    cross = whole_dot(target, library, 1)
    squares = jnp.broadcast_to(jnp.sum(target * target, axis=1, keepdims=True), (8, 128))

    for half in range(2):
        for number, (i, j) in enumerate(BLOCKS[half]):
            for part in range(8):
                half_ref[half, number * 8 + part] = gram_ref[
                    i * 128 + part * 16 : i * 128 + part * 16 + 16, j * 128 : j * 128 + 128
                ]
    for block in range(4):
        half_ref[0, CHUNKS - 1, block * 4 : block * 4 + 4, :] = cross[
            :4, block * 128 : block * 128 + 128
        ]
    half_ref[1, CHUNKS - 1, :8, :] = squares
    half_ref[1, CHUNKS - 1, 8:, :] = jnp.zeros((8, 128), f32)

    pair = pltpu.make_async_remote_copy(
        src_ref=half_ref.at[1 - core],
        dst_ref=half_in_ref,
        send_sem=core_sems.at[0],
        recv_sem=core_sems.at[1],
        device_id=other_core,
        device_id_type=MESH,
    )
    pair.start()
    pair.wait()
    part_ref[...] = half_ref[core] + half_in_ref[...]

    mine = (chip * UNSPREAD) % CHIPS
    owner = mine < CHUNKS

    def give(step, carry):
        chunk = (mine + step) % CHUNKS
        to = (chunk * SPREAD) % CHIPS

        @pl.when(to != chip)
        def _():
            pltpu.make_async_remote_copy(
                src_ref=part_ref.at[chunk],
                dst_ref=parts_in_ref.at[chip],
                send_sem=part_sems.at[0],
                recv_sem=part_sems.at[1],
                device_id=chip_device(to, core),
                device_id_type=MESH,
            ).start()

        return carry

    lax.fori_loop(0, CHUNKS, give, 0)

    @pl.when(owner)
    def _():
        own = parts_in_ref.at[pl.ds(0, CHIPS - 1)]
        pltpu.make_async_copy(own, own, part_sems.at[1]).wait()
        parts_in_ref[chip] = part_ref[mine]
        done_ref[mine] = jnp.sum(parts_in_ref[...], axis=0)

        def show(step, carry):
            pltpu.make_async_remote_copy(
                src_ref=done_ref.at[mine],
                dst_ref=done_ref.at[mine],
                send_sem=done_sems.at[0],
                recv_sem=done_sems.at[1],
                device_id=chip_device((chip + step) % CHIPS, core),
                device_id_type=MESH,
            ).start()
            return carry

        lax.fori_loop(1, CHIPS, show, 0)
        sent = parts_in_ref.at[pl.ds(0, CHIPS - 1)]
        pltpu.make_async_copy(sent, sent, done_sems.at[0]).wait()
        rest = part_ref.at[pl.ds(0, CHUNKS - 1)]
        pltpu.make_async_copy(rest, rest, part_sems.at[0]).wait()
        pltpu.make_async_copy(rest, rest, done_sems.at[1]).wait()

    @pl.when(jnp.logical_not(owner))
    def _():
        pltpu.make_async_copy(part_ref, part_ref, part_sems.at[0]).wait()
        pltpu.make_async_copy(part_ref, part_ref, done_sems.at[1]).wait()

    swap = pltpu.make_async_remote_copy(
        src_ref=done_ref,
        dst_ref=other_ref,
        send_sem=other_sems.at[0],
        recv_sem=other_sems.at[1],
        device_id=other_core,
        device_id_type=MESH,
    )
    swap.start()
    swap.wait()
    half_ref[core] = done_ref[...]
    half_ref[1 - core] = other_ref[...]

    for half in range(2):
        for number, (i, j) in enumerate(BLOCKS[half]):
            for part in range(8):
                gram_ref[
                    i * 128 + part * 16 : i * 128 + part * 16 + 16, j * 128 : j * 128 + 128
                ] = half_ref[half, number * 8 + part]
    for i in range(4):
        for j in range(i):
            gram_ref[i * 128 : i * 128 + 128, j * 128 : j * 128 + 128] = gram_ref[
                j * 128 : j * 128 + 128, i * 128 : i * 128 + 128
            ].T
    cross_sum = jnp.concatenate(
        [
            jnp.concatenate(
                [half_ref[0, CHUNKS - 1, block * 4 : block * 4 + 4, :] for block in range(4)],
                axis=1,
            ),
            jnp.zeros((4, TERMS), f32),
        ],
        axis=0,
    )
    square_sum = half_ref[1, CHUNKS - 1, :8, :1]
    solve(
        gram_ref, normal_ref, lib_ref, cross_sum, square_sum, lib, coef_ref, fit_ref, spot_ref
    )


def local(snap_start, snap_end, exponents):
    vmem = pl.BlockSpec(memory_space=pltpu.VMEM)
    anywhere = pl.BlockSpec(memory_space=pl.ANY)
    return pl.pallas_call(
        kernel,
        out_shape=(
            jax.ShapeDtypeStruct((4, TERMS // 4), f32),
            jax.ShapeDtypeStruct((4, TESTS), f32),
        ),
        in_specs=[vmem, vmem, vmem, anywhere, anywhere, anywhere, anywhere],
        out_specs=(vmem, vmem),
        scratch_shapes=[
            pltpu.VMEM((4, CELLS_X, CELLS_Y, WIDTH_Z), bf16),
            pltpu.VMEM((4, CELLS_X, CELLS_Y, WIDTH_Z), bf16),
            pltpu.VMEM((4 * CENTERS_Y * PAD, CELLS_XY), bf16),
            pltpu.VMEM((CENTERS_Y * WIDTH_Z, 3 * TESTS), bf16),
            pltpu.VMEM((8, CELLS_XY, WIDTH_Z), f32),
            pltpu.VMEM((PRODUCTS, CELLS_XY, WIDTH_Z), bf16),
            pltpu.VMEM((2, 2, TABLE, CENTERS_Y * WIDTH_Z), bf16),
            pltpu.VMEM((2, KEYS, 2 * TESTS), bf16),
            pltpu.VMEM((5, 128, 128), f32),
            pltpu.VMEM((PICKED, KEYS), bf16),
            pltpu.VMEM((PICKED, TESTS), bf16),
            pltpu.VMEM((PICKED, TESTS), bf16),
            pltpu.VMEM((PICKED, TESTS), f32),
            pltpu.VMEM((TERMS, TERMS), f32),
            pltpu.VMEM((2, CHUNKS, CHUNK, 128), f32),
            pltpu.VMEM((CHUNKS, CHUNK, 128), f32),
            pltpu.VMEM((CHUNKS, CHUNK, 128), f32),
            pltpu.VMEM((CHIPS, CHUNK, 128), f32),
            pltpu.VMEM((CHUNKS, CHUNK, 128), f32),
            pltpu.VMEM((CHUNKS, CHUNK, 128), f32),
            pltpu.VMEM((TERMS, 2 * TERMS), bf16),
            pltpu.VMEM((8, TERMS), f32),
            pltpu.SemaphoreType.DMA((4,)),
            pltpu.SemaphoreType.DMA((6,)),
            pltpu.SemaphoreType.DMA((2,)),
            pltpu.SemaphoreType.DMA((2,)),
            pltpu.SemaphoreType.DMA((2,)),
            pltpu.SemaphoreType.DMA((2,)),
            pltpu.SemaphoreType.DMA((2,)),
        ],
        compiler_params=pltpu.CompilerParams(
            collective_id=0, has_side_effects=True, vmem_limit_bytes=56 << 20
        ),
        name="weak_form_fit",
    )(
        exponents,
        jnp.asarray(code_weights()),
        jnp.asarray(column_codes()),
        snap_start,
        snap_end,
        jnp.asarray(plane_weights()),
        jnp.asarray(depth_weights()),
    )


def solution(mesh):
    placed = (P(None, "sub", None, None), P(None, "sub", None, None), P("lib", None))
    return jax.shard_map(
        local,
        mesh=mesh,
        in_specs=placed,
        out_specs=(P(None, "lib"), P(None, ("sub", "lib"))),
        check_vma=False,
    )
```

```python
import functools

import jax
import jax.numpy as jnp
import ml_dtypes
import numpy as np
from jax import lax
from jax.experimental import pallas as pl
from jax.experimental.pallas import tpu as pltpu
from jax.sharding import PartitionSpec as P

STRIDE = 8
RADIUS = 8
POWER = 6
ITERS = 10
TERMS = 512
ROWS = 16384
RIDGE = 0.1
SHRINK = 0.05
EPSILON = 1e-06

CELLS_X = 8
CELLS_Y = 40
CELLS_XY = CELLS_X * CELLS_Y
WIDTH_Z = 256
CENTERS_Y = 4
CENTERS_Z = 32
TESTS = CENTERS_Y * CENTERS_Z

POWERS = [
    (a, b, c, e)
    for a in range(3)
    for b in range(3)
    for c in range(3)
    for e in range(3)
    if 1 <= a + b + c + e <= 3
]
PRODUCTS = len(POWERS) + 4
PAD = 16
TABLE = PRODUCTS * PAD
KEYS = 3 * TABLE
PICKED = TERMS + 16
TARGET_CODE = 4000

CHUNK = 10
CHIPS = 64
BLOCKS = (
    ((0, 0), (0, 1), (0, 2), (0, 3), (3, 3)),
    ((1, 1), (1, 2), (1, 3), (2, 2), (2, 3)),
)
HOPS = (0, 1, 2, 1)
PARTNERS = sorted(
    range(1, CHIPS), key=lambda d: -(HOPS[d // 16] + HOPS[d // 4 % 4] + HOPS[d % 4])
)

MESH = pl.DeviceIdType.MESH
f32 = jnp.float32
bf16 = jnp.bfloat16


def tap(order, offset):
    s = np.asarray(offset, np.float64) / RADIUS
    base = 1.0 - s * s
    value = (base**3, 6.0 * s * base**2, -6.0 * base * (1.0 - 5.0 * s * s))[order]
    return np.where(np.abs(s) <= 1.0, value, 0.0)


def split_pieces(values):
    high = values.astype(ml_dtypes.bfloat16)
    low = (values - high.astype(np.float64)).astype(ml_dtypes.bfloat16)
    return high, low


def plane_weights():
    x = np.arange(CELLS_X)[:, None]
    y = np.arange(CELLS_Y)[None, :]
    both = []
    for shift in (0, STRIDE):
        full = np.zeros((2, CENTERS_Y, PAD, CELLS_X, CELLS_Y))
        for side in range(2):
            for center in range(CENTERS_Y):
                for order_x in range(3):
                    for order_y in range(3):
                        full[side, center, order_x * 3 + order_y] = tap(
                            order_x, x - STRIDE * side
                        ) * tap(order_y, y - STRIDE * center - shift)
        high, low = split_pieces(full.reshape(2, CENTERS_Y * PAD, CELLS_XY))
        both.append(np.concatenate([high, low], axis=1))
    return np.stack(both)


def depth_weights():
    z = np.arange(WIDTH_Z)[:, None]
    centers = STRIDE * np.arange(CENTERS_Z)[None, :]
    full = np.zeros((CENTERS_Y, WIDTH_Z, 3, CENTERS_Y, CENTERS_Z))
    for order in range(3):
        for center in range(CENTERS_Y):
            full[center, :, order, center, :] = tap(order, z - centers)
    return full.reshape(CENTERS_Y * WIDTH_Z, 3 * TESTS).astype(ml_dtypes.bfloat16)


def column_codes():
    codes = np.full((3, PRODUCTS, PAD), -2.0, np.float32)
    for index, (a, b, c, e) in enumerate(POWERS):
        for order_z in range(3):
            for plane in range(9):
                codes[order_z, index, plane] = (
                    (((a * 3 + b) * 3 + c) * 3 + e) * 27 + plane * 3 + order_z
                )
    for field in range(4):
        codes[0, len(POWERS) + field, 0] = TARGET_CODE + field
    return codes.reshape(1, KEYS)


def code_weights():
    return np.array([[729], [243], [81], [27], [9], [3], [1]], np.float32)


def others(value):
    return value, value + 1 - 2 * (value % 2), (value + 2) % 4, 3 - value


class Chips:
    def __init__(self):
        sub = lax.axis_index("sub")
        lib = lax.axis_index("lib")
        self.core = lib % 2
        self.x = others(sub // 8)
        self.y = others((sub // 4) % 2 * 2 + lib // 2)
        self.z = others(sub % 4)
        self.sub_x = [8 * v for v in self.x]
        self.sub_y = [v // 2 * 4 for v in self.y]
        self.lib_y = [v % 2 * 2 + self.core for v in self.y]
        self.chip_xy = [[16 * v + 4 * w for w in self.y] for v in self.x]

    def chip(self, d):
        return self.chip_xy[d // 16][d // 4 % 4] + self.z[d % 4]

    def device(self, d):
        return {
            "sub": self.sub_x[d // 16] + self.sub_y[d // 4 % 4] + self.z[d % 4],
            "lib": self.lib_y[d // 4 % 4],
        }


def products(fields_ref, later_ref, wide_ref, theta_ref):
    for field in range(4):
        for x in range(CELLS_X):
            wide_ref[field, x * CELLS_Y : (x + 1) * CELLS_Y, :] = fields_ref[field, x].astype(f32)
            wide_ref[4 + field, x * CELLS_Y : (x + 1) * CELLS_Y, :] = later_ref[field, x].astype(
                f32
            )

    def rows(step, carry):
        at = pl.multiple_of(step * 16, 16)
        for half in range(2):
            some(at, slice(half * 128, half * 128 + 128))
        return carry

    def some(at, lanes):
        value = [wide_ref[field, pl.ds(at, 16), lanes] for field in range(4)]
        square = [v * v for v in value]
        pairs = {}
        for index, powers in enumerate(POWERS):
            result = None
            key = ()
            for field, power in enumerate(powers):
                if power == 0:
                    continue
                factor = value[field] if power == 1 else square[field]
                key = key + ((field, power),)
                if result is None:
                    result = factor
                elif key in pairs:
                    result = pairs[key]
                else:
                    result = result * factor
                    pairs[key] = result
            theta_ref[index, pl.ds(at, 16), lanes] = result.astype(bf16)
        for field in range(4):
            change = wide_ref[4 + field, pl.ds(at, 16), lanes] - value[field]
            theta_ref[len(POWERS) + field, pl.ds(at, 16), lanes] = change.astype(bf16)

    lax.fori_loop(0, CELLS_XY // 16, rows, 0)


def plane_sums(weights_ref, theta_ref, plane_ref, side):
    half = CENTERS_Y * PAD

    def one(index, carry):
        both = jnp.dot(weights_ref[side], theta_ref[index], preferred_element_type=f32)
        total = both[:half] + both[half:]
        high = total.astype(bf16)
        low = (total - high.astype(f32)).astype(bf16)
        at = pl.multiple_of(index * PAD, PAD)
        for center in range(CENTERS_Y):
            row = center * PAD
            lanes = slice(center * WIDTH_Z, (center + 1) * WIDTH_Z)
            plane_ref[side, 0, pl.ds(at, PAD), lanes] = high[row : row + PAD]
            plane_ref[side, 1, pl.ds(at, PAD), lanes] = low[row : row + PAD]
        return carry

    lax.fori_loop(0, PRODUCTS, one, 0, unroll=2)


def depth_sums(plane_ref, depth_ref, table_ref, side):
    size = 2 * PAD * 17 // 2
    for start in range(0, TABLE, size):
        high = jnp.dot(
            plane_ref[side, 0, start : start + size], depth_ref[...], preferred_element_type=f32
        )
        low = jnp.dot(
            plane_ref[side, 1, start : start + size], depth_ref[...], preferred_element_type=f32
        )
        total = high + low
        top = total.astype(bf16)
        rest = (total - top.astype(f32)).astype(bf16)
        for order in range(3):
            lanes = slice(order * TESTS, (order + 1) * TESTS)
            rows = slice(order * TABLE + start, order * TABLE + start + size)
            table_ref[rows, :TESTS] = top[:, lanes]
            table_ref[rows, TESTS:] = rest[:, lanes]


def pick_table(codes_ref, keys_ref, pick_ref):
    for row in range(0, PICKED, 16):
        code = codes_ref[row // 128, row % 128 : row % 128 + 16, :]
        for column in range(0, KEYS, 128):
            width = min(128, KEYS - column)
            same = code[:, :width] == keys_ref[:, column : column + width]
            pick_ref[row : row + 16, column : column + width] = jnp.where(same, 1.0, 0.0).astype(
                bf16
            )


def whole_dot(left, right, contract):
    return lax.dot_general(
        left,
        right,
        (((1,), (contract,)), ((), ())),
        precision=lax.Precision.HIGHEST,
        preferred_element_type=f32,
    )


def solve(gram_ref, normal_ref, lib_ref, cross, target_squares, lib, result_ref, spot_ref):
    total = float(ROWS)
    diagonal_row = []
    diagonal_column = []
    same = lax.broadcasted_iota(jnp.int32, (128, 128), 0) == lax.broadcasted_iota(
        jnp.int32, (128, 128), 1
    )
    for block in range(4):
        at = slice(block * 128, block * 128 + 128)
        spread = jnp.where(same, gram_ref[at, at], 0.0)
        diagonal_row.append(jnp.sum(spread, axis=0, keepdims=True))
        diagonal_column.append(jnp.sum(spread, axis=1, keepdims=True))
    inverse_row = [1.0 / jnp.sqrt(d / total + EPSILON) for d in diagonal_row]
    inverse_column = [1.0 / jnp.sqrt(d / total + EPSILON) for d in diagonal_column]
    for i in range(4):
        for j in range(4):
            rows, lanes = slice(i * 128, i * 128 + 128), slice(j * 128, j * 128 + 128)
            block = gram_ref[rows, lanes] * (inverse_column[i] / total) * inverse_row[j]
            if i == j:
                block = block + jnp.where(same, RIDGE, 0.0)
            high = block.astype(bf16)
            normal_ref[rows, lanes] = high
            normal_ref[rows, slice(TERMS + j * 128, TERMS + j * 128 + 128)] = (
                block - high.astype(f32)
            ).astype(bf16)
    inverse = jnp.concatenate(inverse_row, axis=1)
    target_scale = 1.0 / jnp.sqrt(target_squares / total + EPSILON)
    normal_cross = cross * inverse * (target_scale / total)

    def apply(rows):
        high = rows.astype(bf16)
        low = (rows - high.astype(f32)).astype(bf16)
        stacked = jnp.concatenate([high, low], axis=0)
        both = jnp.dot(stacked, normal_ref[...], preferred_element_type=f32)
        return both[:8, :TERMS] + both[:8, TERMS:] + both[8:, :TERMS]

    vector = jnp.full((8, TERMS), TERMS**-0.5, f32)
    for _ in range(POWER - 1):
        vector = apply(vector)
    applied = apply(vector)
    before = jnp.sum(vector * vector, axis=1, keepdims=True)
    after = jnp.sum(applied * applied, axis=1, keepdims=True)
    step_size = jnp.sqrt(before) / jnp.sqrt(after)
    bound = step_size * SHRINK
    coeffs = None
    for sweep in range(ITERS):
        if sweep == 0:
            moved = step_size * normal_cross
        else:
            moved = coeffs - step_size * (apply(coeffs) - normal_cross)
        coeffs = jnp.maximum(moved - bound, 0.0) - jnp.maximum(-moved - bound, 0.0)
    spot_ref[...] = coeffs
    own = pl.multiple_of(lib * 128, 128)
    result_ref[:8, :] = spot_ref[:, pl.ds(own, 128)]
    result_ref[8:, :] = whole_dot(coeffs * inverse, lib_ref[:TERMS], 0)


def kernel(
    exponents_ref,
    code_weight_ref,
    keys_ref,
    start_ref,
    end_ref,
    plane_weight_ref,
    depth_weight_ref,
    result_ref,
    fields_ref,
    later_ref,
    weights_ref,
    depth_ref,
    wide_ref,
    theta_ref,
    plane_ref,
    table_ref,
    codes_ref,
    pick_ref,
    edge_out_ref,
    edge_in_ref,
    lib_ref,
    gram_ref,
    half_ref,
    half_in_ref,
    parts_in_ref,
    done_ref,
    normal_ref,
    spot_ref,
    local_sems,
    code_sems,
    edge_sems,
    core_sems,
    part_sems,
    done_sems,
    other_sems,
):
    sub = lax.axis_index("sub")
    lib = lax.axis_index("lib")
    chips = Chips()
    core = chips.core
    next_sub = {"sub": (sub + 1) % 32, "lib": lib}
    last_sub = {"sub": (sub + 31) % 32, "lib": lib}
    other_core = {"sub": sub, "lib": lib + 1 - 2 * core}
    window = pl.ds(pl.multiple_of(jnp.maximum(lib * 32 - 8, 0), 8), CELLS_Y)
    loads = [
        pltpu.make_async_copy(start_ref.at[:, :, window, :], fields_ref, local_sems.at[0]),
        pltpu.make_async_copy(end_ref.at[:, :, window, :], later_ref, local_sems.at[1]),
        pltpu.make_async_copy(
            plane_weight_ref.at[jnp.minimum(lib, 1)], weights_ref, local_sems.at[2]
        ),
        pltpu.make_async_copy(depth_weight_ref, depth_ref, local_sems.at[3]),
    ]
    for load in loads:
        load.start()

    barrier = pltpu.get_barrier_semaphore()

    for d in PARTNERS:
        pl.semaphore_signal(barrier, inc=1, device_id=chips.device(d), device_id_type=MESH)
    for device in (
        next_sub,
        last_sub,
        {"sub": sub, "lib": (lib + 1) % 4},
        {"sub": sub, "lib": (lib + 2) % 4},
        {"sub": sub, "lib": (lib + 3) % 4},
    ):
        pl.semaphore_signal(barrier, inc=1, device_id=device, device_id_type=MESH)

    code = jnp.sum(
        exponents_ref[...].astype(f32) * code_weight_ref[...], axis=0, keepdims=True
    )
    codes_ref[lib] = jnp.broadcast_to(code, (128, 128)).T
    row = lax.broadcasted_iota(jnp.int32, (16, 128), 0)
    codes_ref[4, :16, :] = jnp.where(row < 4, TARGET_CODE + row, -1).astype(f32)

    loads[0].wait()
    loads[1].wait()
    products(fields_ref, later_ref, wide_ref, theta_ref)
    pl.semaphore_wait(barrier, CHIPS - 1 + 5)
    code_copies = [
        pltpu.make_async_remote_copy(
            src_ref=codes_ref.at[lib],
            dst_ref=codes_ref.at[lib],
            send_sem=code_sems.at[step],
            recv_sem=code_sems.at[3 + step],
            device_id={"sub": sub, "lib": (lib + 1 + step) % 4},
            device_id_type=MESH,
        )
        for step in range(3)
    ]
    for copy in code_copies:
        copy.start()
    loads[2].wait()
    plane_sums(weights_ref, theta_ref, plane_ref, 1)
    for copy in code_copies:
        copy.wait()
    pick_table(codes_ref, keys_ref, pick_ref)
    loads[3].wait()
    depth_sums(plane_ref, depth_ref, table_ref.at[1], 1)
    both = jnp.dot(pick_ref[...], table_ref[1], preferred_element_type=f32)
    edge_out_ref[...] = (both[:, :TESTS] + both[:, TESTS:]).astype(bf16)
    edge = pltpu.make_async_remote_copy(
        src_ref=edge_out_ref,
        dst_ref=edge_in_ref,
        send_sem=edge_sems.at[0],
        recv_sem=edge_sems.at[1],
        device_id=next_sub,
        device_id_type=MESH,
    )
    edge.start()
    plane_sums(weights_ref, theta_ref, plane_ref, 0)
    depth_sums(plane_ref, depth_ref, table_ref.at[0], 0)
    both = jnp.dot(pick_ref[...], table_ref[0], preferred_element_type=f32)
    lib_ref[...] = both[:, :TESTS] + both[:, TESTS:]
    edge.wait()
    keep = jnp.where(sub > 0, 1.0, 0.0).astype(f32)
    lib_ref[...] = lib_ref[...] + keep * edge_in_ref[...].astype(f32)

    library = lib_ref[:TERMS]
    gram_ref[...] = whole_dot(library, library, 1)
    target = lib_ref[TERMS : TERMS + 8]
    cross = whole_dot(target, library, 1)
    squares = jnp.broadcast_to(jnp.sum(target * target, axis=1, keepdims=True), (8, 128))

    for piece in range(8):
        gram_ref[64 + piece * 4 : 68 + piece * 4, :64] = cross[:4, piece * 64 : piece * 64 + 64]
    gram_ref[96:100, :64] = squares[:4, :64]

    for half in range(2):
        for number, (i, j) in enumerate(BLOCKS[half][:4]):
            lanes = slice(j * 128, j * 128 + 128)
            for part in range(16):
                row = i * 128 + part * 8
                half_ref[half, number * 16 + part, :8, :] = gram_ref[row : row + 8, lanes]
        i, j = BLOCKS[half][4]
        for part in range(CHIPS):
            row = i * 128 + part * 2
            half_ref[half, part, 8:, :] = gram_ref[row : row + 2, j * 128 : j * 128 + 128]
    pair = pltpu.make_async_remote_copy(
        src_ref=half_ref.at[1 - core],
        dst_ref=half_in_ref,
        send_sem=core_sems.at[0],
        recv_sem=core_sems.at[1],
        device_id=other_core,
        device_id_type=MESH,
    )
    pair.start()
    pair.wait()
    half_in_ref[...] = half_in_ref[...] + half_ref[core]
    own = chips.chip(0)
    for d in PARTNERS:
        pltpu.make_async_remote_copy(
            src_ref=half_in_ref.at[chips.chip(d)],
            dst_ref=parts_in_ref.at[d],
            send_sem=part_sems.at[0],
            recv_sem=part_sems.at[1],
            device_id=chips.device(d),
            device_id_type=MESH,
        ).start()
    parts_in_ref[0] = half_in_ref[own]
    received = parts_in_ref.at[pl.ds(1, CHIPS - 1)]
    pltpu.make_async_copy(received, received, part_sems.at[1]).wait()
    done_ref[core, own] = jnp.sum(parts_in_ref[...], axis=0)
    for d in PARTNERS:
        pltpu.make_async_remote_copy(
            src_ref=done_ref.at[core, own],
            dst_ref=done_ref.at[core, own],
            send_sem=done_sems.at[0],
            recv_sem=done_sems.at[1],
            device_id=chips.device(d),
            device_id_type=MESH,
        ).start()
    pltpu.make_async_copy(received, received, part_sems.at[0]).wait()
    pltpu.make_async_copy(received, received, done_sems.at[1]).wait()
    pltpu.make_async_copy(received, received, done_sems.at[0]).wait()
    swap = pltpu.make_async_remote_copy(
        src_ref=done_ref.at[core],
        dst_ref=done_ref.at[core],
        send_sem=other_sems.at[0],
        recv_sem=other_sems.at[1],
        device_id=other_core,
        device_id_type=MESH,
    )
    swap.start()
    swap.wait()
    for half in range(2):
        for number, (i, j) in enumerate(BLOCKS[half][:4]):
            lanes = slice(j * 128, j * 128 + 128)
            for part in range(16):
                row = i * 128 + part * 8
                gram_ref[row : row + 8, lanes] = done_ref[half, number * 16 + part, :8, :]
        i, j = BLOCKS[half][4]
        for part in range(CHIPS):
            row = i * 128 + part * 2
            gram_ref[row : row + 2, j * 128 : j * 128 + 128] = done_ref[half, part, 8:, :]
    cross_sum = jnp.concatenate(
        [
            jnp.concatenate(
                [gram_ref[64 + piece * 4 : 68 + piece * 4, :64] for piece in range(8)], axis=1
            ),
            jnp.zeros((4, TERMS), f32),
        ],
        axis=0,
    )
    square_sum = jnp.concatenate([gram_ref[96:100, :1], jnp.zeros((4, 1), f32)], axis=0)
    gram_ref[64:128, :64] = gram_ref[:64, 64:128].T
    for i in range(4):
        for j in range(i):
            gram_ref[i * 128 : i * 128 + 128, j * 128 : j * 128 + 128] = gram_ref[
                j * 128 : j * 128 + 128, i * 128 : i * 128 + 128
            ].T
    solve(
        gram_ref, normal_ref, lib_ref, cross_sum, square_sum, lib, result_ref, spot_ref
    )


def split_result(result_ref, coef_ref, fit_ref):
    coef_ref[...] = result_ref[:4]
    fit_ref[...] = result_ref[8:12]


def local(snap_start, snap_end, exponents):
    vmem = pl.BlockSpec(memory_space=pltpu.VMEM)
    anywhere = pl.BlockSpec(memory_space=pl.ANY)
    result = pl.pallas_call(
        kernel,
        out_shape=jax.ShapeDtypeStruct((16, TESTS), f32),
        in_specs=[vmem, vmem, vmem, anywhere, anywhere, anywhere, anywhere],
        out_specs=vmem,
        scratch_shapes=[
            pltpu.VMEM((4, CELLS_X, CELLS_Y, WIDTH_Z), bf16),
            pltpu.VMEM((4, CELLS_X, CELLS_Y, WIDTH_Z), bf16),
            pltpu.VMEM((2, 2 * CENTERS_Y * PAD, CELLS_XY), bf16),
            pltpu.VMEM((CENTERS_Y * WIDTH_Z, 3 * TESTS), bf16),
            pltpu.VMEM((8, CELLS_XY, WIDTH_Z), f32),
            pltpu.VMEM((PRODUCTS, CELLS_XY, WIDTH_Z), bf16),
            pltpu.VMEM((2, 2, TABLE, CENTERS_Y * WIDTH_Z), bf16),
            pltpu.VMEM((2, KEYS, 2 * TESTS), bf16),
            pltpu.VMEM((5, 128, 128), f32),
            pltpu.VMEM((PICKED, KEYS), bf16),
            pltpu.VMEM((PICKED, TESTS), bf16),
            pltpu.VMEM((PICKED, TESTS), bf16),
            pltpu.VMEM((PICKED, TESTS), f32),
            pltpu.VMEM((TERMS, TERMS), f32),
            pltpu.VMEM((2, CHIPS, CHUNK, 128), f32),
            pltpu.VMEM((CHIPS, CHUNK, 128), f32),
            pltpu.VMEM((CHIPS, CHUNK, 128), f32),
            pltpu.VMEM((2, CHIPS, CHUNK, 128), f32),
            pltpu.VMEM((TERMS, 2 * TERMS), bf16),
            pltpu.VMEM((8, TERMS), f32),
            pltpu.SemaphoreType.DMA((4,)),
            pltpu.SemaphoreType.DMA((6,)),
            pltpu.SemaphoreType.DMA((2,)),
            pltpu.SemaphoreType.DMA((2,)),
            pltpu.SemaphoreType.DMA((2,)),
            pltpu.SemaphoreType.DMA((2,)),
            pltpu.SemaphoreType.DMA((2,)),
        ],
        compiler_params=pltpu.CompilerParams(
            collective_id=0, has_side_effects=True, vmem_limit_bytes=56 << 20
        ),
        name="weak_form_fit",
    )(
        exponents.T,
        jnp.asarray(code_weights()),
        jnp.asarray(column_codes()),
        snap_start,
        snap_end,
        jnp.asarray(plane_weights()),
        jnp.asarray(depth_weights()),
    )
    return pl.pallas_call(
        split_result,
        out_shape=(
            jax.ShapeDtypeStruct((4, TERMS // 4), f32),
            jax.ShapeDtypeStruct((4, TESTS), f32),
        ),
        in_specs=[vmem],
        out_specs=(vmem, vmem),
        name="split_result",
    )(result)


def solution(mesh):
    placed = (P(None, "sub", None, None), P(None, "sub", None, None), P("lib", None))
    return jax.shard_map(
        local,
        mesh=mesh,
        in_specs=placed,
        out_specs=(P(None, "lib"), P(None, ("sub", "lib"))),
        check_vma=False,
    )
```

```python
import functools

import jax
import jax.numpy as jnp
import ml_dtypes
import numpy as np
from jax import lax
from jax.experimental import pallas as pl
from jax.experimental.pallas import tpu as pltpu
from jax.sharding import PartitionSpec as P

STRIDE = 8
RADIUS = 8
POWER = 6
ITERS = 10
TERMS = 512
ROWS = 16384
RIDGE = 0.1
SHRINK = 0.05
EPSILON = 1e-06

CELLS_X = 8
CELLS_Y = 40
CELLS_XY = CELLS_X * CELLS_Y
MAIN_Y = 32
MAIN = CELLS_X * MAIN_Y
REST = CELLS_XY - MAIN
WIDTH_Z = 256
CENTERS_Y = 4
CENTERS_Z = 32
TESTS = CENTERS_Y * CENTERS_Z

POWERS = [
    (a, b, c, e)
    for a in range(3)
    for b in range(3)
    for c in range(3)
    for e in range(3)
    if 1 <= a + b + c + e <= 3
]
PRODUCTS = len(POWERS) + 4
PAD = 16
TABLE = PRODUCTS * PAD
KEYS = 3 * TABLE
PICKED = TERMS + 16
TARGET_CODE = 4000

CHUNK = 10
CHIPS = 64
BLOCKS = (
    ((0, 0), (0, 1), (0, 2), (0, 3), (3, 3)),
    ((1, 1), (1, 2), (1, 3), (2, 2), (2, 3)),
)
HOPS = (0, 1, 2, 1)
PARTNERS = sorted(
    range(1, CHIPS), key=lambda d: -(HOPS[d // 16] + HOPS[d // 4 % 4] + HOPS[d % 4])
)

MESH = pl.DeviceIdType.MESH
f32 = jnp.float32
bf16 = jnp.bfloat16


def tap(order, offset):
    s = np.asarray(offset, np.float64) / RADIUS
    base = 1.0 - s * s
    value = (base**3, 6.0 * s * base**2, -6.0 * base * (1.0 - 5.0 * s * s))[order]
    return np.where(np.abs(s) <= 1.0, value, 0.0)


def split_pieces(values):
    high = values.astype(ml_dtypes.bfloat16)
    low = (values - high.astype(np.float64)).astype(ml_dtypes.bfloat16)
    return high, low


def plane_weights():
    x = np.arange(CELLS_X)[:, None]
    y = np.arange(CELLS_Y)[None, :]
    both = []
    for shift in (0, STRIDE):
        full = np.zeros((2, CENTERS_Y, PAD, CELLS_X, CELLS_Y))
        for side in range(2):
            for center in range(CENTERS_Y):
                for order_x in range(3):
                    for order_y in range(3):
                        full[side, center, order_x * 3 + order_y] = tap(
                            order_x, x - STRIDE * side
                        ) * tap(order_y, y - STRIDE * center - shift)
        wide = full[..., :MAIN_Y].reshape(2, CENTERS_Y * PAD, MAIN)
        edge = full[:, CENTERS_Y - 1, :, :, MAIN_Y:].reshape(2, PAD, REST)
        apart = np.zeros((2, 4, PAD, 4, REST))
        for member in range(4):
            apart[:, member, :, member, :] = edge
        groups = (wide, apart.reshape(2, 4 * PAD, 4 * REST))
        both.append(np.stack([np.concatenate(split_pieces(g), axis=1) for g in groups]))
    return np.stack(both)


def depth_weights():
    z = np.arange(WIDTH_Z)[:, None]
    centers = STRIDE * np.arange(CENTERS_Z)[None, :]
    full = np.zeros((CENTERS_Y, WIDTH_Z, 3, CENTERS_Y, CENTERS_Z))
    for order in range(3):
        for center in range(CENTERS_Y):
            full[center, :, order, center, :] = tap(order, z - centers)
    return full.reshape(CENTERS_Y * WIDTH_Z, 3 * TESTS).astype(ml_dtypes.bfloat16)


def column_codes():
    codes = np.full((3, PRODUCTS, PAD), -2.0, np.float32)
    for index, (a, b, c, e) in enumerate(POWERS):
        for order_z in range(3):
            for plane in range(9):
                codes[order_z, index, plane] = (
                    (((a * 3 + b) * 3 + c) * 3 + e) * 27 + plane * 3 + order_z
                )
    for field in range(4):
        codes[0, len(POWERS) + field, 0] = TARGET_CODE + field
    return codes.reshape(1, KEYS)


def code_weights():
    return np.array([[729], [243], [81], [27], [9], [3], [1]], np.float32)


def others(value):
    return value, value + 1 - 2 * (value % 2), (value + 2) % 4, 3 - value


class Chips:
    def __init__(self):
        sub = lax.axis_index("sub")
        lib = lax.axis_index("lib")
        self.core = lib % 2
        self.x = others(sub // 8)
        self.y = others((sub // 4) % 2 * 2 + lib // 2)
        self.z = others(sub % 4)
        self.sub_x = [8 * v for v in self.x]
        self.sub_y = [v // 2 * 4 for v in self.y]
        self.lib_y = [v % 2 * 2 + self.core for v in self.y]
        self.chip_xy = [[16 * v + 4 * w for w in self.y] for v in self.x]

    def chip(self, d):
        return self.chip_xy[d // 16][d // 4 % 4] + self.z[d % 4]

    def device(self, d):
        return {
            "sub": self.sub_x[d // 16] + self.sub_y[d // 4 % 4] + self.z[d % 4],
            "lib": self.lib_y[d // 4 % 4],
        }


def products(fields_ref, later_ref, wide_ref, theta_ref, rest_ref):
    for field in range(4):
        for x in range(CELLS_X):
            for base, source in ((0, fields_ref), (4, later_ref)):
                plane = source[field, x].astype(f32)
                wide_ref[base + field, x * MAIN_Y : x * MAIN_Y + MAIN_Y, :] = plane[:MAIN_Y]
                wide_ref[base + field, MAIN + x * 8 : MAIN + x * 8 + 8, :] = plane[MAIN_Y:]

    def some(at, lanes, put):
        value = [wide_ref[field, pl.ds(at, 16), lanes] for field in range(4)]
        square = [v * v for v in value]
        pairs = {}
        for index, powers in enumerate(POWERS):
            result = None
            key = ()
            for field, power in enumerate(powers):
                if power == 0:
                    continue
                factor = value[field] if power == 1 else square[field]
                key = key + ((field, power),)
                if result is None:
                    result = factor
                elif key in pairs:
                    result = pairs[key]
                else:
                    result = result * factor
                    pairs[key] = result
            put(index, result.astype(bf16))
        for field in range(4):
            change = wide_ref[4 + field, pl.ds(at, 16), lanes] - value[field]
            put(len(POWERS) + field, change.astype(bf16))

    def main_rows(step, carry):
        at = pl.multiple_of(step * 16, 16)
        for half in range(2):

            def put(index, value, half=half):
                lane = index % 2 * WIDTH_Z + half * 128
                theta_ref[index // 2, pl.ds(at, 16), lane : lane + 128] = value

            some(at, slice(half * 128, half * 128 + 128), put)
        return carry

    def rest_rows(step, carry):
        at = pl.multiple_of(step * 16, 16)
        for half in range(2):
            lanes = slice(half * 128, half * 128 + 128)

            def put(index, value, lanes=lanes):
                rest_ref[index // 4, pl.ds(index % 4 * REST + at, 16), lanes] = value

            some(MAIN + at, lanes, put)
        return carry

    lax.fori_loop(0, MAIN // 16, main_rows, 0)
    lax.fori_loop(0, REST // 16, rest_rows, 0)
    used = PRODUCTS % 4 * REST
    rest_ref[PRODUCTS // 4, used:, :] = jnp.zeros((4 * REST - used, WIDTH_Z), bf16)


def plane_sums(weights_ref, theta_ref, rest_ref, rest_sum_ref, plane_ref, side, pieces):
    half = CENTERS_Y * PAD

    def leftover(index, carry):
        both = jnp.dot(weights_ref[1, side], rest_ref[index], preferred_element_type=f32)
        at = pl.multiple_of(index * half, half)
        rest_sum_ref[pl.ds(at, half), :] = both[:half] + both[half:]
        return carry

    def pair(index, carry):
        both = jnp.dot(weights_ref[0, side], theta_ref[index], preferred_element_type=f32)
        total = both[:half] + both[half:]
        for member in range(2):
            at = pl.multiple_of((index * 2 + member) * PAD, PAD)
            for center in range(CENTERS_Y):
                part = total[center * PAD : center * PAD + PAD, member * WIDTH_Z :][:, :WIDTH_Z]
                if center == CENTERS_Y - 1:
                    part = part + rest_sum_ref[pl.ds(at, PAD), :]
                lanes = slice(center * WIDTH_Z, (center + 1) * WIDTH_Z)
                high = part.astype(bf16)
                plane_ref[0, pl.ds(at, PAD), lanes] = high
                if pieces == 2:
                    plane_ref[1, pl.ds(at, PAD), lanes] = (part - high.astype(f32)).astype(bf16)
        return carry

    lax.fori_loop(0, PRODUCTS // 4 + 1, leftover, 0, unroll=9)
    lax.fori_loop(0, PRODUCTS // 2, pair, 0, unroll=PRODUCTS // 2)


def depth_sums(plane_ref, depth_ref, table_ref, pieces):
    size = TABLE // 2
    for start in range(0, TABLE, size):
        total = jnp.dot(
            plane_ref[0, start : start + size], depth_ref[...], preferred_element_type=f32
        )
        if pieces == 2:
            total = total + jnp.dot(
                plane_ref[1, start : start + size], depth_ref[...], preferred_element_type=f32
            )
        top = total.astype(bf16)
        rest = (total - top.astype(f32)).astype(bf16)
        for order in range(3):
            lanes = slice(order * TESTS, (order + 1) * TESTS)
            rows = slice(order * TABLE + start, order * TABLE + start + size)
            table_ref[rows, :TESTS] = top[:, lanes]
            if pieces == 2:
                table_ref[rows, TESTS:] = rest[:, lanes]


def pick_table(codes_ref, keys_ref, pick_ref):
    spread = [jnp.broadcast_to(codes_ref[part, :1, :], (128, 128)).T for part in range(5)]
    for row in range(0, PICKED, 16):
        code = spread[row // 128][row % 128 : row % 128 + 16, :]
        for column in range(0, KEYS, 128):
            width = min(128, KEYS - column)
            same = code[:, :width] == keys_ref[:, column : column + width]
            pick_ref[row : row + 16, column : column + width] = jnp.where(same, 1.0, 0.0).astype(
                bf16
            )


def whole_dot(left, right, contract):
    return lax.dot_general(
        left,
        right,
        (((1,), (contract,)), ((), ())),
        precision=lax.Precision.HIGHEST,
        preferred_element_type=f32,
    )


def solve(gram_ref, normal_ref, lib_ref, cross, target_squares, lib, result_ref, spot_ref):
    total = float(ROWS)
    diagonal_row = []
    diagonal_column = []
    same = lax.broadcasted_iota(jnp.int32, (128, 128), 0) == lax.broadcasted_iota(
        jnp.int32, (128, 128), 1
    )
    for block in range(4):
        at = slice(block * 128, block * 128 + 128)
        spread = jnp.where(same, gram_ref[at, at], 0.0)
        diagonal_row.append(jnp.sum(spread, axis=0, keepdims=True))
        diagonal_column.append(jnp.sum(spread, axis=1, keepdims=True))
    inverse_row = [1.0 / jnp.sqrt(d / total + EPSILON) for d in diagonal_row]
    inverse_column = [1.0 / jnp.sqrt(d / total + EPSILON) for d in diagonal_column]
    for i in range(4):
        for j in range(4):
            rows, lanes = slice(i * 128, i * 128 + 128), slice(j * 128, j * 128 + 128)
            block = gram_ref[rows, lanes] * (inverse_column[i] / total) * inverse_row[j]
            if i == j:
                block = block + jnp.where(same, RIDGE, 0.0)
            high = block.astype(bf16)
            normal_ref[rows, lanes] = high
            normal_ref[rows, slice(TERMS + j * 128, TERMS + j * 128 + 128)] = (
                block - high.astype(f32)
            ).astype(bf16)
    inverse = jnp.concatenate(inverse_row, axis=1)
    target_scale = 1.0 / jnp.sqrt(target_squares / total + EPSILON)
    normal_cross = cross * inverse * (target_scale / total)

    def apply(rows):
        high = rows.astype(bf16)
        low = (rows - high.astype(f32)).astype(bf16)
        stacked = jnp.concatenate([high, low], axis=0)
        both = jnp.dot(stacked, normal_ref[...], preferred_element_type=f32)
        return both[:8, :TERMS] + both[:8, TERMS:] + both[8:, :TERMS]

    vector = jnp.full((8, TERMS), TERMS**-0.5, f32)
    for _ in range(POWER - 1):
        vector = apply(vector)
    applied = apply(vector)
    before = jnp.sum(vector * vector, axis=1, keepdims=True)
    after = jnp.sum(applied * applied, axis=1, keepdims=True)
    step_size = jnp.sqrt(before) / jnp.sqrt(after)
    bound = step_size * SHRINK
    coeffs = None
    for sweep in range(ITERS):
        if sweep == 0:
            moved = step_size * normal_cross
        else:
            moved = coeffs - step_size * (apply(coeffs) - normal_cross)
        coeffs = jnp.maximum(moved - bound, 0.0) - jnp.maximum(-moved - bound, 0.0)
    spot_ref[...] = coeffs
    own = pl.multiple_of(lib * 128, 128)
    result_ref[:8, :] = spot_ref[:, pl.ds(own, 128)]
    result_ref[8:, :] = whole_dot(coeffs * inverse, lib_ref[:TERMS], 0)


def kernel(
    exponents_ref,
    code_weight_ref,
    keys_ref,
    start_ref,
    end_ref,
    plane_weight_ref,
    depth_weight_ref,
    result_ref,
    fields_ref,
    later_ref,
    weights_ref,
    depth_ref,
    wide_ref,
    theta_ref,
    rest_ref,
    rest_sum_ref,
    plane_ref,
    table_ref,
    codes_ref,
    pick_ref,
    edge_out_ref,
    edge_in_ref,
    lib_ref,
    gram_ref,
    half_ref,
    half_in_ref,
    parts_in_ref,
    done_ref,
    normal_ref,
    spot_ref,
    local_sems,
    code_sems,
    edge_sems,
    core_sems,
    part_sems,
    done_sems,
    other_sems,
):
    sub = lax.axis_index("sub")
    lib = lax.axis_index("lib")
    chips = Chips()
    core = chips.core
    next_sub = {"sub": (sub + 1) % 32, "lib": lib}
    last_sub = {"sub": (sub + 31) % 32, "lib": lib}
    other_core = {"sub": sub, "lib": lib + 1 - 2 * core}
    window = pl.ds(pl.multiple_of(jnp.maximum(lib * 32 - 8, 0), 8), CELLS_Y)
    loads = [
        pltpu.make_async_copy(start_ref.at[:, :, window, :], fields_ref, local_sems.at[0]),
        pltpu.make_async_copy(end_ref.at[:, :, window, :], later_ref, local_sems.at[1]),
        pltpu.make_async_copy(
            plane_weight_ref.at[jnp.minimum(lib, 1)], weights_ref, local_sems.at[2]
        ),
        pltpu.make_async_copy(depth_weight_ref, depth_ref, local_sems.at[3]),
    ]
    for load in loads:
        load.start()

    barrier = pltpu.get_barrier_semaphore()

    for d in PARTNERS:
        pl.semaphore_signal(barrier, inc=1, device_id=chips.device(d), device_id_type=MESH)
    for device in (
        next_sub,
        last_sub,
        {"sub": sub, "lib": (lib + 1) % 4},
        {"sub": sub, "lib": (lib + 2) % 4},
        {"sub": sub, "lib": (lib + 3) % 4},
    ):
        pl.semaphore_signal(barrier, inc=1, device_id=device, device_id_type=MESH)

    code = jnp.sum(
        exponents_ref[...].astype(f32) * code_weight_ref[...], axis=0, keepdims=True
    )
    codes_ref[lib] = jnp.broadcast_to(code, (8, 128))
    lane = lax.broadcasted_iota(jnp.int32, (8, 128), 1)
    codes_ref[4] = jnp.where(lane < 4, TARGET_CODE + lane, -1).astype(f32)

    loads[0].wait()
    loads[1].wait()
    products(fields_ref, later_ref, wide_ref, theta_ref, rest_ref)
    pl.semaphore_wait(barrier, CHIPS - 1 + 5)
    code_copies = [
        pltpu.make_async_remote_copy(
            src_ref=codes_ref.at[lib],
            dst_ref=codes_ref.at[lib],
            send_sem=code_sems.at[step],
            recv_sem=code_sems.at[3 + step],
            device_id={"sub": sub, "lib": (lib + 1 + step) % 4},
            device_id_type=MESH,
        )
        for step in range(3)
    ]
    for copy in code_copies:
        copy.start()
    loads[2].wait()
    plane_sums(weights_ref, theta_ref, rest_ref, rest_sum_ref, plane_ref, 1, 2)
    loads[3].wait()
    depth_sums(plane_ref, depth_ref, table_ref, 2)
    for copy in code_copies:
        copy.wait()
    pick_table(codes_ref, keys_ref, pick_ref)
    both = jnp.dot(pick_ref[...], table_ref[...], preferred_element_type=f32)
    edge_out_ref[...] = (both[:, :TESTS] + both[:, TESTS:]).astype(bf16)
    edge = pltpu.make_async_remote_copy(
        src_ref=edge_out_ref,
        dst_ref=edge_in_ref,
        send_sem=edge_sems.at[0],
        recv_sem=edge_sems.at[1],
        device_id=next_sub,
        device_id_type=MESH,
    )
    edge.start()
    plane_sums(weights_ref, theta_ref, rest_ref, rest_sum_ref, plane_ref, 0, 2)
    depth_sums(plane_ref, depth_ref, table_ref, 2)
    both = jnp.dot(pick_ref[...], table_ref[...], preferred_element_type=f32)
    lib_ref[...] = both[:, :TESTS] + both[:, TESTS:]
    edge.wait()
    keep = jnp.where(sub > 0, 1.0, 0.0).astype(f32)
    lib_ref[...] = lib_ref[...] + keep * edge_in_ref[...].astype(f32)

    high = lib_ref[...].astype(bf16)
    low = (lib_ref[...] - high.astype(f32)).astype(bf16)
    product = lax.dot_general(
        jnp.concatenate([high, low, high], axis=1),
        jnp.concatenate([high[:TERMS], high[:TERMS], low[:TERMS]], axis=1),
        (((1,), (1,)), ((), ())),
        preferred_element_type=f32,
    )
    gram_ref[...] = product[:TERMS]
    cross = product[TERMS : TERMS + 8]
    target = lib_ref[TERMS : TERMS + 8]
    squares = jnp.broadcast_to(jnp.sum(target * target, axis=1, keepdims=True), (8, 128))

    for piece in range(8):
        gram_ref[64 + piece * 4 : 68 + piece * 4, :64] = cross[:4, piece * 64 : piece * 64 + 64]
    gram_ref[96:100, :64] = squares[:4, :64]

    for half in range(2):
        for number, (i, j) in enumerate(BLOCKS[half][:4]):
            lanes = slice(j * 128, j * 128 + 128)
            for part in range(16):
                row = i * 128 + part * 8
                half_ref[half, number * 16 + part, :8, :] = gram_ref[row : row + 8, lanes]
        i, j = BLOCKS[half][4]
        for part in range(CHIPS):
            row = i * 128 + part * 2
            half_ref[half, part, 8:, :] = gram_ref[row : row + 2, j * 128 : j * 128 + 128]
    pair = pltpu.make_async_remote_copy(
        src_ref=half_ref.at[1 - core],
        dst_ref=half_in_ref,
        send_sem=core_sems.at[0],
        recv_sem=core_sems.at[1],
        device_id=other_core,
        device_id_type=MESH,
    )
    pair.start()
    pair.wait()
    half_in_ref[...] = half_in_ref[...] + half_ref[core]
    own = chips.chip(0)
    for d in PARTNERS:
        pltpu.make_async_remote_copy(
            src_ref=half_in_ref.at[chips.chip(d)],
            dst_ref=parts_in_ref.at[d],
            send_sem=part_sems.at[0],
            recv_sem=part_sems.at[1],
            device_id=chips.device(d),
            device_id_type=MESH,
        ).start()
    parts_in_ref[0] = half_in_ref[own]
    received = parts_in_ref.at[pl.ds(1, CHIPS - 1)]
    pltpu.make_async_copy(received, received, part_sems.at[1]).wait()
    done_ref[core, own] = jnp.sum(parts_in_ref[...], axis=0)
    for d in PARTNERS:
        pltpu.make_async_remote_copy(
            src_ref=done_ref.at[core, own],
            dst_ref=done_ref.at[core, own],
            send_sem=done_sems.at[0],
            recv_sem=done_sems.at[1],
            device_id=chips.device(d),
            device_id_type=MESH,
        ).start()
    pltpu.make_async_copy(received, received, part_sems.at[0]).wait()
    pltpu.make_async_copy(received, received, done_sems.at[1]).wait()
    pltpu.make_async_copy(received, received, done_sems.at[0]).wait()
    swap = pltpu.make_async_remote_copy(
        src_ref=done_ref.at[core],
        dst_ref=done_ref.at[core],
        send_sem=other_sems.at[0],
        recv_sem=other_sems.at[1],
        device_id=other_core,
        device_id_type=MESH,
    )
    swap.start()
    swap.wait()
    for half in range(2):
        for number, (i, j) in enumerate(BLOCKS[half][:4]):
            lanes = slice(j * 128, j * 128 + 128)
            for part in range(16):
                row = i * 128 + part * 8
                gram_ref[row : row + 8, lanes] = done_ref[half, number * 16 + part, :8, :]
        i, j = BLOCKS[half][4]
        for part in range(CHIPS):
            row = i * 128 + part * 2
            gram_ref[row : row + 2, j * 128 : j * 128 + 128] = done_ref[half, part, 8:, :]
    cross_sum = jnp.concatenate(
        [
            jnp.concatenate(
                [gram_ref[64 + piece * 4 : 68 + piece * 4, :64] for piece in range(8)], axis=1
            ),
            jnp.zeros((4, TERMS), f32),
        ],
        axis=0,
    )
    square_sum = jnp.concatenate([gram_ref[96:100, :1], jnp.zeros((4, 1), f32)], axis=0)
    gram_ref[64:128, :64] = gram_ref[:64, 64:128].T
    for i in range(4):
        for j in range(i):
            gram_ref[i * 128 : i * 128 + 128, j * 128 : j * 128 + 128] = gram_ref[
                j * 128 : j * 128 + 128, i * 128 : i * 128 + 128
            ].T
    solve(
        gram_ref, normal_ref, lib_ref, cross_sum, square_sum, lib, result_ref, spot_ref
    )


def split_result(result_ref, coef_ref, fit_ref):
    coef_ref[...] = result_ref[:4]
    fit_ref[...] = result_ref[8:12]


def local(snap_start, snap_end, exponents):
    vmem = pl.BlockSpec(memory_space=pltpu.VMEM)
    anywhere = pl.BlockSpec(memory_space=pl.ANY)
    result = pl.pallas_call(
        kernel,
        out_shape=jax.ShapeDtypeStruct((16, TESTS), f32),
        in_specs=[vmem, vmem, vmem, anywhere, anywhere, anywhere, anywhere],
        out_specs=vmem,
        scratch_shapes=[
            pltpu.VMEM((4, CELLS_X, CELLS_Y, WIDTH_Z), bf16),
            pltpu.VMEM((4, CELLS_X, CELLS_Y, WIDTH_Z), bf16),
            pltpu.VMEM((2, 2, 2 * CENTERS_Y * PAD, MAIN), bf16),
            pltpu.VMEM((CENTERS_Y * WIDTH_Z, 3 * TESTS), bf16),
            pltpu.VMEM((8, CELLS_XY, WIDTH_Z), f32),
            pltpu.VMEM((PRODUCTS // 2, MAIN, 2 * WIDTH_Z), bf16),
            pltpu.VMEM((PRODUCTS // 4 + 1, 4 * REST, WIDTH_Z), bf16),
            pltpu.VMEM(((PRODUCTS // 4 + 1) * 4 * PAD, WIDTH_Z), f32),
            pltpu.VMEM((2, TABLE, CENTERS_Y * WIDTH_Z), bf16),
            pltpu.VMEM((KEYS, 2 * TESTS), bf16),
            pltpu.VMEM((5, 8, 128), f32),
            pltpu.VMEM((PICKED, KEYS), bf16),
            pltpu.VMEM((PICKED, TESTS), bf16),
            pltpu.VMEM((PICKED, TESTS), bf16),
            pltpu.VMEM((PICKED, TESTS), f32),
            pltpu.VMEM((TERMS, TERMS), f32),
            pltpu.VMEM((2, CHIPS, CHUNK, 128), f32),
            pltpu.VMEM((CHIPS, CHUNK, 128), f32),
            pltpu.VMEM((CHIPS, CHUNK, 128), f32),
            pltpu.VMEM((2, CHIPS, CHUNK, 128), f32),
            pltpu.VMEM((TERMS, 2 * TERMS), bf16),
            pltpu.VMEM((8, TERMS), f32),
            pltpu.SemaphoreType.DMA((4,)),
            pltpu.SemaphoreType.DMA((6,)),
            pltpu.SemaphoreType.DMA((2,)),
            pltpu.SemaphoreType.DMA((2,)),
            pltpu.SemaphoreType.DMA((2,)),
            pltpu.SemaphoreType.DMA((2,)),
            pltpu.SemaphoreType.DMA((2,)),
        ],
        compiler_params=pltpu.CompilerParams(
            collective_id=0, has_side_effects=True, vmem_limit_bytes=56 << 20
        ),
        name="weak_form_fit",
    )(
        exponents.T,
        jnp.asarray(code_weights()),
        jnp.asarray(column_codes()),
        snap_start,
        snap_end,
        jnp.asarray(plane_weights()),
        jnp.asarray(depth_weights()),
    )
    return pl.pallas_call(
        split_result,
        out_shape=(
            jax.ShapeDtypeStruct((4, TERMS // 4), f32),
            jax.ShapeDtypeStruct((4, TESTS), f32),
        ),
        in_specs=[vmem],
        out_specs=(vmem, vmem),
        name="split_result",
    )(result)


def solution(mesh):
    placed = (P(None, "sub", None, None), P(None, "sub", None, None), P("lib", None))
    return jax.shard_map(
        local,
        mesh=mesh,
        in_specs=placed,
        out_specs=(P(None, "lib"), P(None, ("sub", "lib"))),
        check_vma=False,
    )
```

```python
import functools

import jax
import jax.numpy as jnp
import ml_dtypes
import numpy as np
from jax import lax
from jax.experimental import pallas as pl
from jax.experimental.pallas import tpu as pltpu
from jax.sharding import PartitionSpec as P

STRIDE = 8
RADIUS = 8
POWER = 6
ITERS = 10
TERMS = 512
ROWS = 16384
RIDGE = 0.1
SHRINK = 0.05
EPSILON = 1e-06

CELLS_X = 8
CELLS_Y = 40
CELLS_XY = CELLS_X * CELLS_Y
MAIN_Y = 32
MAIN = CELLS_X * MAIN_Y
REST = CELLS_XY - MAIN
WIDTH_Z = 256
CENTERS_Y = 4
CENTERS_Z = 32
TESTS = CENTERS_Y * CENTERS_Z

POWERS = [
    (a, b, c, e)
    for a in range(3)
    for b in range(3)
    for c in range(3)
    for e in range(3)
    if 1 <= a + b + c + e <= 3
]
PRODUCTS = len(POWERS) + 4
PAD = 16
TABLE = PRODUCTS * PAD
KEYS = 3 * TABLE
PICKED = TERMS + 16
TARGET_CODE = 4000

CHUNK = 10
CHIPS = 64
BLOCKS = (
    ((0, 0), (0, 1), (0, 2), (0, 3), (3, 3)),
    ((1, 1), (1, 2), (1, 3), (2, 2), (2, 3)),
)
HOPS = (0, 1, 2, 1)
PARTNERS = sorted(
    range(1, CHIPS), key=lambda d: -(HOPS[d // 16] + HOPS[d // 4 % 4] + HOPS[d % 4])
)

MESH = pl.DeviceIdType.MESH
f32 = jnp.float32
bf16 = jnp.bfloat16


def tap(order, offset):
    s = np.asarray(offset, np.float64) / RADIUS
    base = 1.0 - s * s
    value = (base**3, 6.0 * s * base**2, -6.0 * base * (1.0 - 5.0 * s * s))[order]
    return np.where(np.abs(s) <= 1.0, value, 0.0)


def split_pieces(values):
    high = values.astype(ml_dtypes.bfloat16)
    low = (values - high.astype(np.float64)).astype(ml_dtypes.bfloat16)
    return high, low


def plane_weights():
    x = np.arange(CELLS_X)[:, None]
    y = np.arange(CELLS_Y)[None, :]
    both = []
    for shift in (0, STRIDE):
        full = np.zeros((2, CENTERS_Y, PAD, CELLS_X, CELLS_Y))
        for side in range(2):
            for center in range(CENTERS_Y):
                for order_x in range(3):
                    for order_y in range(3):
                        full[side, center, order_x * 3 + order_y] = tap(
                            order_x, x - STRIDE * side
                        ) * tap(order_y, y - STRIDE * center - shift)
        wide = full[..., :MAIN_Y].reshape(2, CENTERS_Y * PAD, MAIN)
        edge = full[:, CENTERS_Y - 1, :, :, MAIN_Y:].reshape(2, PAD, REST)
        apart = np.zeros((2, 4, PAD, 4, REST))
        for member in range(4):
            apart[:, member, :, member, :] = edge
        groups = (wide, apart.reshape(2, 4 * PAD, 4 * REST))
        both.append(np.stack([np.concatenate(split_pieces(g), axis=1) for g in groups]))
    return np.stack(both)


def depth_weights():
    z = np.arange(WIDTH_Z)[:, None]
    centers = STRIDE * np.arange(CENTERS_Z)[None, :]
    full = np.zeros((CENTERS_Y, WIDTH_Z, 3, CENTERS_Y, CENTERS_Z))
    for order in range(3):
        for center in range(CENTERS_Y):
            full[center, :, order, center, :] = tap(order, z - centers)
    return full.reshape(CENTERS_Y * WIDTH_Z, 3 * TESTS).astype(ml_dtypes.bfloat16)


def column_codes():
    codes = np.full((3, PRODUCTS, PAD), -2.0, np.float32)
    for index, (a, b, c, e) in enumerate(POWERS):
        for order_z in range(3):
            for plane in range(9):
                codes[order_z, index, plane] = (
                    (((a * 3 + b) * 3 + c) * 3 + e) * 27 + plane * 3 + order_z
                )
    for field in range(4):
        codes[0, len(POWERS) + field, 0] = TARGET_CODE + field
    return codes.reshape(1, KEYS)


def code_weights():
    return np.array([[729], [243], [81], [27], [9], [3], [1]], np.float32)


def others(value):
    return value, value + 1 - 2 * (value % 2), (value + 2) % 4, 3 - value


class Chips:
    def __init__(self):
        sub = lax.axis_index("sub")
        lib = lax.axis_index("lib")
        self.core = lib % 2
        self.x = others(sub // 8)
        self.y = others((sub // 4) % 2 * 2 + lib // 2)
        self.z = others(sub % 4)
        self.sub_x = [8 * v for v in self.x]
        self.sub_y = [v // 2 * 4 for v in self.y]
        self.lib_y = [v % 2 * 2 + self.core for v in self.y]
        self.chip_xy = [[16 * v + 4 * w for w in self.y] for v in self.x]

    def chip(self, d):
        return self.chip_xy[d // 16][d // 4 % 4] + self.z[d % 4]

    def device(self, d):
        return {
            "sub": self.sub_x[d // 16] + self.sub_y[d // 4 % 4] + self.z[d % 4],
            "lib": self.lib_y[d // 4 % 4],
        }


def products(fields_ref, later_ref, wide_ref, theta_ref, rest_ref):
    for field in range(4):
        for x in range(CELLS_X):
            for base, source in ((0, fields_ref), (4, later_ref)):
                plane = source[field, x].astype(f32)
                wide_ref[base + field, x * MAIN_Y : x * MAIN_Y + MAIN_Y, :] = plane[:MAIN_Y]
                wide_ref[base + field, MAIN + x * 8 : MAIN + x * 8 + 8, :] = plane[MAIN_Y:]

    def some(at, lanes, put):
        value = [wide_ref[field, pl.ds(at, 16), lanes] for field in range(4)]
        square = [v * v for v in value]
        pairs = {}
        for index, powers in enumerate(POWERS):
            result = None
            key = ()
            for field, power in enumerate(powers):
                if power == 0:
                    continue
                factor = value[field] if power == 1 else square[field]
                key = key + ((field, power),)
                if result is None:
                    result = factor
                elif key in pairs:
                    result = pairs[key]
                else:
                    result = result * factor
                    pairs[key] = result
            put(index, result.astype(bf16))
        for field in range(4):
            change = wide_ref[4 + field, pl.ds(at, 16), lanes] - value[field]
            put(len(POWERS) + field, change.astype(bf16))

    def main_rows(step, carry):
        at = pl.multiple_of(step * 16, 16)
        for half in range(2):

            def put(index, value, half=half):
                lane = index % 2 * WIDTH_Z + half * 128
                theta_ref[index // 2, pl.ds(at, 16), lane : lane + 128] = value

            some(at, slice(half * 128, half * 128 + 128), put)
        return carry

    def rest_rows(step, carry):
        at = pl.multiple_of(step * 16, 16)
        for half in range(2):
            lanes = slice(half * 128, half * 128 + 128)

            def put(index, value, lanes=lanes):
                rest_ref[index // 4, pl.ds(index % 4 * REST + at, 16), lanes] = value

            some(MAIN + at, lanes, put)
        return carry

    lax.fori_loop(0, MAIN // 16, main_rows, 0)
    lax.fori_loop(0, REST // 16, rest_rows, 0)
    used = PRODUCTS % 4 * REST
    rest_ref[PRODUCTS // 4, used:, :] = jnp.zeros((4 * REST - used, WIDTH_Z), bf16)


def plane_sums(weights_ref, theta_ref, rest_ref, rest_sum_ref, plane_ref, side, pieces):
    half = CENTERS_Y * PAD

    def leftover(index, carry):
        both = jnp.dot(weights_ref[1, side], rest_ref[index], preferred_element_type=f32)
        at = pl.multiple_of(index * half, half)
        rest_sum_ref[pl.ds(at, half), :] = both[:half] + both[half:]
        return carry

    def pair(index, carry):
        both = jnp.dot(weights_ref[0, side], theta_ref[index], preferred_element_type=f32)
        total = both[:half] + both[half:]
        for member in range(2):
            at = pl.multiple_of((index * 2 + member) * PAD, PAD)
            for center in range(CENTERS_Y):
                part = total[center * PAD : center * PAD + PAD, member * WIDTH_Z :][:, :WIDTH_Z]
                if center == CENTERS_Y - 1:
                    part = part + rest_sum_ref[pl.ds(at, PAD), :]
                lanes = slice(center * WIDTH_Z, (center + 1) * WIDTH_Z)
                high = part.astype(bf16)
                plane_ref[0, pl.ds(at, PAD), lanes] = high
                if pieces == 2:
                    plane_ref[1, pl.ds(at, PAD), lanes] = (part - high.astype(f32)).astype(bf16)
        return carry

    lax.fori_loop(0, PRODUCTS // 4 + 1, leftover, 0, unroll=9)
    lax.fori_loop(0, PRODUCTS // 2, pair, 0, unroll=PRODUCTS // 2)


def depth_sums(plane_ref, depth_ref, table_ref, pieces):
    size = TABLE // 2
    for start in range(0, TABLE, size):
        total = jnp.dot(
            plane_ref[0, start : start + size], depth_ref[...], preferred_element_type=f32
        )
        if pieces == 2:
            total = total + jnp.dot(
                plane_ref[1, start : start + size], depth_ref[...], preferred_element_type=f32
            )
        top = total.astype(bf16)
        rest = (total - top.astype(f32)).astype(bf16)
        for order in range(3):
            lanes = slice(order * TESTS, (order + 1) * TESTS)
            rows = slice(order * TABLE + start, order * TABLE + start + size)
            table_ref[rows, :TESTS] = top[:, lanes]
            if pieces == 2:
                table_ref[rows, TESTS:] = rest[:, lanes]


def pick_table(codes_ref, keys_ref, pick_ref):
    spread = [jnp.broadcast_to(codes_ref[part, :1, :], (128, 128)).T for part in range(5)]
    for row in range(0, PICKED, 16):
        code = spread[row // 128][row % 128 : row % 128 + 16, :]
        for column in range(0, KEYS, 128):
            width = min(128, KEYS - column)
            same = code[:, :width] == keys_ref[:, column : column + width]
            pick_ref[row : row + 16, column : column + width] = jnp.where(same, 1.0, 0.0).astype(
                bf16
            )


def whole_dot(left, right, contract):
    return lax.dot_general(
        left,
        right,
        (((1,), (contract,)), ((), ())),
        precision=lax.Precision.HIGHEST,
        preferred_element_type=f32,
    )


def solve(gram_ref, normal_ref, lib_ref, cross, target_squares, lib, result_ref, spot_ref):
    total = float(ROWS)
    diagonal_row = []
    diagonal_column = []
    same = lax.broadcasted_iota(jnp.int32, (128, 128), 0) == lax.broadcasted_iota(
        jnp.int32, (128, 128), 1
    )
    for block in range(4):
        at = slice(block * 128, block * 128 + 128)
        spread = jnp.where(same, gram_ref[at, at], 0.0)
        diagonal_row.append(jnp.sum(spread, axis=0, keepdims=True))
        diagonal_column.append(jnp.sum(spread, axis=1, keepdims=True))
    inverse_row = [1.0 / jnp.sqrt(d / total + EPSILON) for d in diagonal_row]
    inverse_column = [1.0 / jnp.sqrt(d / total + EPSILON) for d in diagonal_column]
    for i in range(4):
        for j in range(4):
            rows, lanes = slice(i * 128, i * 128 + 128), slice(j * 128, j * 128 + 128)
            block = gram_ref[rows, lanes] * (inverse_column[i] / total) * inverse_row[j]
            if i == j:
                block = block + jnp.where(same, RIDGE, 0.0)
            gram_ref[rows, lanes] = block
            high = block.astype(bf16)
            normal_ref[rows, lanes] = high
            normal_ref[rows, slice(TERMS + j * 128, TERMS + j * 128 + 128)] = (
                block - high.astype(f32)
            ).astype(bf16)
    inverse = jnp.concatenate(inverse_row, axis=1)
    target_scale = 1.0 / jnp.sqrt(target_squares / total + EPSILON)
    normal_cross = cross * inverse * (target_scale / total)

    def apply(rows):
        high = rows.astype(bf16)
        low = (rows - high.astype(f32)).astype(bf16)
        stacked = jnp.concatenate([high, low], axis=0)
        both = jnp.dot(stacked, normal_ref[...], preferred_element_type=f32)
        return both[:8, :TERMS] + both[:8, TERMS:] + both[8:, :TERMS]

    def fold(column):
        sums = [jnp.zeros((8, TERMS), f32) for _ in range(4)]
        for tile in range(TERMS // 8):
            rows = gram_ref[tile * 8 : tile * 8 + 8, :]
            if column is not None:
                rows = rows * column[tile]
            sums[tile % 4] = sums[tile % 4] + rows
        return jnp.sum((sums[0] + sums[1]) + (sums[2] + sums[3]), axis=0, keepdims=True)

    def spread(row):
        row = jnp.broadcast_to(row, (8, TERMS))
        return [
            jnp.sum(gram_ref[tile * 8 : tile * 8 + 8, :] * row, axis=1, keepdims=True)
            for tile in range(TERMS // 8)
        ]

    column = None
    for sweep in range(POWER // 2):
        row = fold(column)
        if sweep == 0:
            row = row * TERMS**-0.5
        column = spread(row)
    before = jnp.sum(row * row, axis=1, keepdims=True)
    after = column[0] * column[0]
    for tile in range(1, TERMS // 8):
        after = after + column[tile] * column[tile]
    after = jnp.sum(after, axis=0, keepdims=True)
    step_size = jnp.sqrt(before) / jnp.sqrt(after)
    bound = step_size * SHRINK
    coeffs = None
    for sweep in range(ITERS):
        if sweep == 0:
            moved = step_size * normal_cross
        else:
            moved = coeffs - step_size * (apply(coeffs) - normal_cross)
        coeffs = jnp.maximum(moved - bound, 0.0) - jnp.maximum(-moved - bound, 0.0)
    spot_ref[...] = coeffs
    own = pl.multiple_of(lib * 128, 128)
    result_ref[:8, :] = spot_ref[:, pl.ds(own, 128)]
    result_ref[8:, :] = whole_dot(coeffs * inverse, lib_ref[:TERMS], 0)


def kernel(
    exponents_ref,
    code_weight_ref,
    keys_ref,
    start_ref,
    end_ref,
    plane_weight_ref,
    depth_weight_ref,
    result_ref,
    fields_ref,
    later_ref,
    weights_ref,
    depth_ref,
    wide_ref,
    theta_ref,
    rest_ref,
    rest_sum_ref,
    plane_ref,
    table_ref,
    codes_ref,
    pick_ref,
    edge_out_ref,
    edge_in_ref,
    lib_ref,
    gram_ref,
    half_ref,
    half_in_ref,
    parts_in_ref,
    done_ref,
    normal_ref,
    spot_ref,
    local_sems,
    code_sems,
    edge_sems,
    core_sems,
    part_sems,
    done_sems,
    other_sems,
    ready_sems,
):
    sub = lax.axis_index("sub")
    lib = lax.axis_index("lib")
    chips = Chips()
    core = chips.core
    next_sub = {"sub": (sub + 1) % 32, "lib": lib}
    last_sub = {"sub": (sub + 31) % 32, "lib": lib}
    other_core = {"sub": sub, "lib": lib + 1 - 2 * core}
    window = pl.ds(pl.multiple_of(jnp.maximum(lib * 32 - 8, 0), 8), CELLS_Y)
    loads = [
        pltpu.make_async_copy(start_ref.at[:, :, window, :], fields_ref, local_sems.at[0]),
        pltpu.make_async_copy(end_ref.at[:, :, window, :], later_ref, local_sems.at[1]),
        pltpu.make_async_copy(
            plane_weight_ref.at[jnp.minimum(lib, 1)], weights_ref, local_sems.at[2]
        ),
        pltpu.make_async_copy(depth_weight_ref, depth_ref, local_sems.at[3]),
    ]
    for load in loads:
        load.start()

    barrier = pltpu.get_barrier_semaphore()

    near = [chips.device(d) for d in (1, 2, 3, 4, 8, 12, 16, 32, 48)]
    near += [{"sub": sub, "lib": (lib + step) % 4} for step in (1, 2, 3)]
    near += [next_sub, last_sub]
    for device in near:
        pl.semaphore_signal(barrier, inc=1, device_id=device, device_id_type=MESH)

    code = jnp.sum(
        exponents_ref[...].astype(f32) * code_weight_ref[...], axis=0, keepdims=True
    )
    codes_ref[lib] = jnp.broadcast_to(code, (8, 128))
    lane = lax.broadcasted_iota(jnp.int32, (8, 128), 1)
    codes_ref[4] = jnp.where(lane < 4, TARGET_CODE + lane, -1).astype(f32)

    loads[0].wait()
    loads[1].wait()
    products(fields_ref, later_ref, wide_ref, theta_ref, rest_ref)
    pl.semaphore_wait(barrier, len(near))
    for device in near[6:9]:
        pl.semaphore_signal(ready_sems.at[0], inc=1, device_id=device, device_id_type=MESH)
    code_copies = [
        pltpu.make_async_remote_copy(
            src_ref=codes_ref.at[lib],
            dst_ref=codes_ref.at[lib],
            send_sem=code_sems.at[step],
            recv_sem=code_sems.at[3 + step],
            device_id={"sub": sub, "lib": (lib + 1 + step) % 4},
            device_id_type=MESH,
        )
        for step in range(3)
    ]
    for copy in code_copies:
        copy.start()
    loads[2].wait()
    plane_sums(weights_ref, theta_ref, rest_ref, rest_sum_ref, plane_ref, 1, 2)
    pl.semaphore_wait(ready_sems.at[0], 3)
    for device in near[3:6]:
        pl.semaphore_signal(ready_sems.at[1], inc=1, device_id=device, device_id_type=MESH)
    loads[3].wait()
    depth_sums(plane_ref, depth_ref, table_ref, 2)
    for copy in code_copies:
        copy.wait()
    pick_table(codes_ref, keys_ref, pick_ref)
    both = jnp.dot(pick_ref[...], table_ref[...], preferred_element_type=f32)
    edge_out_ref[...] = (both[:, :TESTS] + both[:, TESTS:]).astype(bf16)
    edge = pltpu.make_async_remote_copy(
        src_ref=edge_out_ref,
        dst_ref=edge_in_ref,
        send_sem=edge_sems.at[0],
        recv_sem=edge_sems.at[1],
        device_id=next_sub,
        device_id_type=MESH,
    )
    edge.start()
    plane_sums(weights_ref, theta_ref, rest_ref, rest_sum_ref, plane_ref, 0, 2)
    depth_sums(plane_ref, depth_ref, table_ref, 2)
    both = jnp.dot(pick_ref[...], table_ref[...], preferred_element_type=f32)
    lib_ref[...] = both[:, :TESTS] + both[:, TESTS:]
    edge.wait()
    keep = jnp.where(sub > 0, 1.0, 0.0).astype(f32)
    lib_ref[...] = lib_ref[...] + keep * edge_in_ref[...].astype(f32)

    high = lib_ref[...].astype(bf16)
    low = (lib_ref[...] - high.astype(f32)).astype(bf16)
    product = lax.dot_general(
        jnp.concatenate([high, low, high], axis=1),
        jnp.concatenate([high[:TERMS], high[:TERMS], low[:TERMS]], axis=1),
        (((1,), (1,)), ((), ())),
        preferred_element_type=f32,
    )
    gram_ref[...] = product[:TERMS]
    cross = product[TERMS : TERMS + 8]
    target = lib_ref[TERMS : TERMS + 8]
    squares = jnp.broadcast_to(jnp.sum(target * target, axis=1, keepdims=True), (8, 128))

    for piece in range(8):
        gram_ref[64 + piece * 4 : 68 + piece * 4, :64] = cross[:4, piece * 64 : piece * 64 + 64]
    gram_ref[96:100, :64] = squares[:4, :64]

    for half in range(2):
        for number, (i, j) in enumerate(BLOCKS[half][:4]):
            lanes = slice(j * 128, j * 128 + 128)
            for part in range(16):
                row = i * 128 + part * 8
                half_ref[half, number * 16 + part, :8, :] = gram_ref[row : row + 8, lanes]
        i, j = BLOCKS[half][4]
        for part in range(CHIPS):
            row = i * 128 + part * 2
            half_ref[half, part, 8:, :] = gram_ref[row : row + 2, j * 128 : j * 128 + 128]
    pair = pltpu.make_async_remote_copy(
        src_ref=half_ref.at[1 - core],
        dst_ref=half_in_ref,
        send_sem=core_sems.at[0],
        recv_sem=core_sems.at[1],
        device_id=other_core,
        device_id_type=MESH,
    )
    pair.start()
    pair.wait()
    half_in_ref[...] = half_in_ref[...] + half_ref[core]
    pl.semaphore_wait(ready_sems.at[1], 3)
    own = chips.chip(0)
    for d in PARTNERS:
        pltpu.make_async_remote_copy(
            src_ref=half_in_ref.at[chips.chip(d)],
            dst_ref=parts_in_ref.at[d],
            send_sem=part_sems.at[0],
            recv_sem=part_sems.at[1],
            device_id=chips.device(d),
            device_id_type=MESH,
        ).start()
    parts_in_ref[0] = half_in_ref[own]
    received = parts_in_ref.at[pl.ds(1, CHIPS - 1)]
    pltpu.make_async_copy(received, received, part_sems.at[1]).wait()
    done_ref[core, own] = jnp.sum(parts_in_ref[...], axis=0)
    for d in PARTNERS:
        pltpu.make_async_remote_copy(
            src_ref=done_ref.at[core, own],
            dst_ref=done_ref.at[core, own],
            send_sem=done_sems.at[0],
            recv_sem=done_sems.at[1],
            device_id=chips.device(d),
            device_id_type=MESH,
        ).start()
    pltpu.make_async_copy(received, received, part_sems.at[0]).wait()
    pltpu.make_async_copy(received, received, done_sems.at[1]).wait()
    pltpu.make_async_copy(received, received, done_sems.at[0]).wait()
    swap = pltpu.make_async_remote_copy(
        src_ref=done_ref.at[core],
        dst_ref=done_ref.at[core],
        send_sem=other_sems.at[0],
        recv_sem=other_sems.at[1],
        device_id=other_core,
        device_id_type=MESH,
    )
    swap.start()
    swap.wait()
    for half in range(2):
        for number, (i, j) in enumerate(BLOCKS[half][:4]):
            lanes = slice(j * 128, j * 128 + 128)
            for part in range(16):
                row = i * 128 + part * 8
                gram_ref[row : row + 8, lanes] = done_ref[half, number * 16 + part, :8, :]
        i, j = BLOCKS[half][4]
        for part in range(CHIPS):
            row = i * 128 + part * 2
            gram_ref[row : row + 2, j * 128 : j * 128 + 128] = done_ref[half, part, 8:, :]
    cross_sum = jnp.concatenate(
        [
            jnp.concatenate(
                [gram_ref[64 + piece * 4 : 68 + piece * 4, :64] for piece in range(8)], axis=1
            ),
            jnp.zeros((4, TERMS), f32),
        ],
        axis=0,
    )
    square_sum = jnp.concatenate([gram_ref[96:100, :1], jnp.zeros((4, 1), f32)], axis=0)
    gram_ref[64:128, :64] = gram_ref[:64, 64:128].T
    for i in range(4):
        for j in range(i):
            gram_ref[i * 128 : i * 128 + 128, j * 128 : j * 128 + 128] = gram_ref[
                j * 128 : j * 128 + 128, i * 128 : i * 128 + 128
            ].T
    solve(
        gram_ref, normal_ref, lib_ref, cross_sum, square_sum, lib, result_ref, spot_ref
    )


def split_result(result_ref, coef_ref, fit_ref):
    coef_ref[...] = result_ref[:4]
    fit_ref[...] = result_ref[8:12]


def local(snap_start, snap_end, exponents):
    vmem = pl.BlockSpec(memory_space=pltpu.VMEM)
    anywhere = pl.BlockSpec(memory_space=pl.ANY)
    result = pl.pallas_call(
        kernel,
        out_shape=jax.ShapeDtypeStruct((16, TESTS), f32),
        in_specs=[vmem, vmem, vmem, anywhere, anywhere, anywhere, anywhere],
        out_specs=vmem,
        scratch_shapes=[
            pltpu.VMEM((4, CELLS_X, CELLS_Y, WIDTH_Z), bf16),
            pltpu.VMEM((4, CELLS_X, CELLS_Y, WIDTH_Z), bf16),
            pltpu.VMEM((2, 2, 2 * CENTERS_Y * PAD, MAIN), bf16),
            pltpu.VMEM((CENTERS_Y * WIDTH_Z, 3 * TESTS), bf16),
            pltpu.VMEM((8, CELLS_XY, WIDTH_Z), f32),
            pltpu.VMEM((PRODUCTS // 2, MAIN, 2 * WIDTH_Z), bf16),
            pltpu.VMEM((PRODUCTS // 4 + 1, 4 * REST, WIDTH_Z), bf16),
            pltpu.VMEM(((PRODUCTS // 4 + 1) * 4 * PAD, WIDTH_Z), f32),
            pltpu.VMEM((2, TABLE, CENTERS_Y * WIDTH_Z), bf16),
            pltpu.VMEM((KEYS, 2 * TESTS), bf16),
            pltpu.VMEM((5, 8, 128), f32),
            pltpu.VMEM((PICKED, KEYS), bf16),
            pltpu.VMEM((PICKED, TESTS), bf16),
            pltpu.VMEM((PICKED, TESTS), bf16),
            pltpu.VMEM((PICKED, TESTS), f32),
            pltpu.VMEM((TERMS, TERMS), f32),
            pltpu.VMEM((2, CHIPS, CHUNK, 128), f32),
            pltpu.VMEM((CHIPS, CHUNK, 128), f32),
            pltpu.VMEM((CHIPS, CHUNK, 128), f32),
            pltpu.VMEM((2, CHIPS, CHUNK, 128), f32),
            pltpu.VMEM((TERMS, 2 * TERMS), bf16),
            pltpu.VMEM((8, TERMS), f32),
            pltpu.SemaphoreType.DMA((4,)),
            pltpu.SemaphoreType.DMA((6,)),
            pltpu.SemaphoreType.DMA((2,)),
            pltpu.SemaphoreType.DMA((2,)),
            pltpu.SemaphoreType.DMA((2,)),
            pltpu.SemaphoreType.DMA((2,)),
            pltpu.SemaphoreType.DMA((2,)),
            pltpu.SemaphoreType.REGULAR((2,)),
        ],
        compiler_params=pltpu.CompilerParams(
            collective_id=0, has_side_effects=True, vmem_limit_bytes=56 << 20
        ),
        name="weak_form_fit",
    )(
        exponents.T,
        jnp.asarray(code_weights()),
        jnp.asarray(column_codes()),
        snap_start,
        snap_end,
        jnp.asarray(plane_weights()),
        jnp.asarray(depth_weights()),
    )
    return pl.pallas_call(
        split_result,
        out_shape=(
            jax.ShapeDtypeStruct((4, TERMS // 4), f32),
            jax.ShapeDtypeStruct((4, TESTS), f32),
        ),
        in_specs=[vmem],
        out_specs=(vmem, vmem),
        name="split_result",
    )(result)


def solution(mesh):
    placed = (P(None, "sub", None, None), P(None, "sub", None, None), P("lib", None))
    return jax.shard_map(
        local,
        mesh=mesh,
        in_specs=placed,
        out_specs=(P(None, "lib"), P(None, ("sub", "lib"))),
        check_vma=False,
    )
```

```python
import functools

import jax
import jax.numpy as jnp
import ml_dtypes
import numpy as np
from jax import lax
from jax.experimental import pallas as pl
from jax.experimental.pallas import tpu as pltpu
from jax.sharding import PartitionSpec as P

STRIDE = 8
RADIUS = 8
POWER = 6
ITERS = 10
TERMS = 512
ROWS = 16384
RIDGE = 0.1
SHRINK = 0.05
EPSILON = 1e-06

CELLS_X = 8
CELLS_Y = 40
CELLS_XY = CELLS_X * CELLS_Y
MAIN_Y = 32
MAIN = CELLS_X * MAIN_Y
REST = CELLS_XY - MAIN
WIDTH_Z = 256
CENTERS_Y = 4
CENTERS_Z = 32
TESTS = CENTERS_Y * CENTERS_Z

POWERS = [
    (a, b, c, e)
    for a in range(3)
    for b in range(3)
    for c in range(3)
    for e in range(3)
    if 1 <= a + b + c + e <= 3
]
PRODUCTS = len(POWERS) + 4
PAD = 16
TABLE = PRODUCTS * PAD
KEYS = 3 * TABLE
PICKED = TERMS + 16
TARGET_CODE = 4000

CHUNK = 10
CHIPS = 64
BLOCKS = (
    ((0, 0), (0, 1), (0, 2), (0, 3), (3, 3)),
    ((1, 1), (1, 2), (1, 3), (2, 2), (2, 3)),
)
HOPS = (0, 1, 2, 1)
PARTNERS = sorted(
    range(1, CHIPS), key=lambda d: -(HOPS[d // 16] + HOPS[d // 4 % 4] + HOPS[d % 4])
)

MESH = pl.DeviceIdType.MESH
f32 = jnp.float32
bf16 = jnp.bfloat16


def tap(order, offset):
    s = np.asarray(offset, np.float64) / RADIUS
    base = 1.0 - s * s
    value = (base**3, 6.0 * s * base**2, -6.0 * base * (1.0 - 5.0 * s * s))[order]
    return np.where(np.abs(s) <= 1.0, value, 0.0)


def split_pieces(values):
    high = values.astype(ml_dtypes.bfloat16)
    low = (values - high.astype(np.float64)).astype(ml_dtypes.bfloat16)
    return high, low


def plane_weights():
    x = np.arange(CELLS_X)[:, None]
    y = np.arange(CELLS_Y)[None, :]
    both = []
    for shift in (0, STRIDE):
        full = np.zeros((2, CENTERS_Y, PAD, CELLS_X, CELLS_Y))
        for side in range(2):
            for center in range(CENTERS_Y):
                for order_x in range(3):
                    for order_y in range(3):
                        full[side, center, order_x * 3 + order_y] = tap(
                            order_x, x - STRIDE * side
                        ) * tap(order_y, y - STRIDE * center - shift)
        wide = full[..., :MAIN_Y].reshape(2, CENTERS_Y * PAD, MAIN)
        edge = full[:, CENTERS_Y - 1, :, :, MAIN_Y:].reshape(2, PAD, REST)
        apart = np.zeros((2, 4, PAD, 4, REST))
        for member in range(4):
            apart[:, member, :, member, :] = edge
        groups = (wide, apart.reshape(2, 4 * PAD, 4 * REST))
        both.append(np.stack([np.concatenate(split_pieces(g), axis=1) for g in groups]))
    return np.stack(both)


def depth_weights():
    z = np.arange(WIDTH_Z)[:, None]
    centers = STRIDE * np.arange(CENTERS_Z)[None, :]
    full = np.zeros((CENTERS_Y, WIDTH_Z, 3, CENTERS_Y, CENTERS_Z))
    for order in range(3):
        for center in range(CENTERS_Y):
            full[center, :, order, center, :] = tap(order, z - centers)
    return full.reshape(CENTERS_Y * WIDTH_Z, 3 * TESTS).astype(ml_dtypes.bfloat16)


def column_codes():
    codes = np.full((3, PRODUCTS, PAD), -2.0, np.float32)
    for index, (a, b, c, e) in enumerate(POWERS):
        for order_z in range(3):
            for plane in range(9):
                codes[order_z, index, plane] = (
                    (((a * 3 + b) * 3 + c) * 3 + e) * 27 + plane * 3 + order_z
                )
    for field in range(4):
        codes[0, len(POWERS) + field, 0] = TARGET_CODE + field
    return codes.reshape(1, KEYS)


def others(value):
    return value, value + 1 - 2 * (value % 2), (value + 2) % 4, 3 - value


class Chips:
    def __init__(self):
        sub = lax.axis_index("sub")
        lib = lax.axis_index("lib")
        self.core = lib % 2
        self.x = others(sub // 8)
        self.y = others((sub // 4) % 2 * 2 + lib // 2)
        self.z = others(sub % 4)
        self.sub_x = [8 * v for v in self.x]
        self.sub_y = [v // 2 * 4 for v in self.y]
        self.lib_y = [v % 2 * 2 + self.core for v in self.y]
        self.chip_xy = [[16 * v + 4 * w for w in self.y] for v in self.x]

    def chip(self, d):
        return self.chip_xy[d // 16][d // 4 % 4] + self.z[d % 4]

    def device(self, d):
        return {
            "sub": self.sub_x[d // 16] + self.sub_y[d // 4 % 4] + self.z[d % 4],
            "lib": self.lib_y[d // 4 % 4],
        }


def products(fields_ref, later_ref, wide_ref, theta_ref, rest_ref):
    for field in range(4):
        for x in range(CELLS_X):
            for base, source in ((0, fields_ref), (4, later_ref)):
                plane = source[field, x].astype(f32)
                wide_ref[base + field, x * MAIN_Y : x * MAIN_Y + MAIN_Y, :] = plane[:MAIN_Y]
                wide_ref[base + field, MAIN + x * 8 : MAIN + x * 8 + 8, :] = plane[MAIN_Y:]

    def some(at, lanes, put):
        value = [wide_ref[field, pl.ds(at, 16), lanes] for field in range(4)]
        square = [v * v for v in value]
        pairs = {}
        for index, powers in enumerate(POWERS):
            result = None
            key = ()
            for field, power in enumerate(powers):
                if power == 0:
                    continue
                factor = value[field] if power == 1 else square[field]
                key = key + ((field, power),)
                if result is None:
                    result = factor
                elif key in pairs:
                    result = pairs[key]
                else:
                    result = result * factor
                    pairs[key] = result
            put(index, result.astype(bf16))
        for field in range(4):
            change = wide_ref[4 + field, pl.ds(at, 16), lanes] - value[field]
            put(len(POWERS) + field, change.astype(bf16))

    def main_rows(step, carry):
        at = pl.multiple_of(step * 16, 16)
        for half in range(2):

            def put(index, value, half=half):
                lane = index % 2 * WIDTH_Z + half * 128
                theta_ref[index // 2, pl.ds(at, 16), lane : lane + 128] = value

            some(at, slice(half * 128, half * 128 + 128), put)
        return carry

    def rest_rows(step, carry):
        at = pl.multiple_of(step * 16, 16)
        for half in range(2):
            lanes = slice(half * 128, half * 128 + 128)

            def put(index, value, lanes=lanes):
                rest_ref[index // 4, pl.ds(index % 4 * REST + at, 16), lanes] = value

            some(MAIN + at, lanes, put)
        return carry

    lax.fori_loop(0, MAIN // 16, main_rows, 0)
    lax.fori_loop(0, REST // 16, rest_rows, 0)
    used = PRODUCTS % 4 * REST
    rest_ref[PRODUCTS // 4, used:, :] = jnp.zeros((4 * REST - used, WIDTH_Z), bf16)


def plane_sums(weights_ref, theta_ref, rest_ref, rest_sum_ref, plane_ref, side, pieces):
    half = CENTERS_Y * PAD

    def leftover(index, carry):
        both = jnp.dot(weights_ref[1, side], rest_ref[index], preferred_element_type=f32)
        at = pl.multiple_of(index * half, half)
        rest_sum_ref[pl.ds(at, half), :] = both[:half] + both[half:]
        return carry

    def pair(index, carry):
        both = jnp.dot(weights_ref[0, side], theta_ref[index], preferred_element_type=f32)
        total = both[:half] + both[half:]
        for member in range(2):
            at = pl.multiple_of((index * 2 + member) * PAD, PAD)
            for center in range(CENTERS_Y):
                part = total[center * PAD : center * PAD + PAD, member * WIDTH_Z :][:, :WIDTH_Z]
                if center == CENTERS_Y - 1:
                    part = part + rest_sum_ref[pl.ds(at, PAD), :]
                lanes = slice(center * WIDTH_Z, (center + 1) * WIDTH_Z)
                high = part.astype(bf16)
                plane_ref[0, pl.ds(at, PAD), lanes] = high
                if pieces == 2:
                    plane_ref[1, pl.ds(at, PAD), lanes] = (part - high.astype(f32)).astype(bf16)
        return carry

    lax.fori_loop(0, PRODUCTS // 4 + 1, leftover, 0, unroll=9)
    lax.fori_loop(0, PRODUCTS // 2, pair, 0, unroll=PRODUCTS // 2)


def depth_sums(plane_ref, depth_ref, table_ref, pieces):
    size = TABLE // 2
    for start in range(0, TABLE, size):
        total = jnp.dot(
            plane_ref[0, start : start + size], depth_ref[...], preferred_element_type=f32
        )
        if pieces == 2:
            total = total + jnp.dot(
                plane_ref[1, start : start + size], depth_ref[...], preferred_element_type=f32
            )
        top = total.astype(bf16)
        rest = (total - top.astype(f32)).astype(bf16)
        for order in range(3):
            lanes = slice(order * TESTS, (order + 1) * TESTS)
            rows = slice(order * TABLE + start, order * TABLE + start + size)
            table_ref[rows, :TESTS] = top[:, lanes]
            if pieces == 2:
                table_ref[rows, TESTS:] = rest[:, lanes]


def pick_rows(code, keys_ref, pick_ref, start, count):
    spread = jnp.broadcast_to(code, (128, 128)).T
    for row in range(0, count, 16):
        for column in range(0, KEYS, 128):
            width = min(128, KEYS - column)
            same = spread[row : row + 16, :width] == keys_ref[:, column : column + width]
            pick_ref[pl.ds(start + row, 16), column : column + width] = jnp.where(
                same, 1.0, 0.0
            ).astype(bf16)


def whole_dot(left, right, contract):
    return lax.dot_general(
        left,
        right,
        (((1,), (contract,)), ((), ())),
        precision=lax.Precision.HIGHEST,
        preferred_element_type=f32,
    )


def solve(gram_ref, normal_ref, lib_ref, cross, target_squares, lib, result_ref, spot_ref):
    total = float(ROWS)
    diagonal_row = []
    diagonal_column = []
    same = lax.broadcasted_iota(jnp.int32, (128, 128), 0) == lax.broadcasted_iota(
        jnp.int32, (128, 128), 1
    )
    for block in range(4):
        at = slice(block * 128, block * 128 + 128)
        spread = jnp.where(same, gram_ref[at, at], 0.0)
        diagonal_row.append(jnp.sum(spread, axis=0, keepdims=True))
        diagonal_column.append(jnp.sum(spread, axis=1, keepdims=True))
    inverse_row = [1.0 / jnp.sqrt(d / total + EPSILON) for d in diagonal_row]
    inverse_column = [1.0 / jnp.sqrt(d / total + EPSILON) for d in diagonal_column]
    for i in range(4):
        for j in range(4):
            rows, lanes = slice(i * 128, i * 128 + 128), slice(j * 128, j * 128 + 128)
            block = gram_ref[rows, lanes] * (inverse_column[i] / total) * inverse_row[j]
            if i == j:
                block = block + jnp.where(same, RIDGE, 0.0)
            gram_ref[rows, lanes] = block
            high = block.astype(bf16)
            normal_ref[rows, lanes] = high
            normal_ref[rows, slice(TERMS + j * 128, TERMS + j * 128 + 128)] = (
                block - high.astype(f32)
            ).astype(bf16)
    inverse = jnp.concatenate(inverse_row, axis=1)
    target_scale = 1.0 / jnp.sqrt(target_squares / total + EPSILON)
    normal_cross = cross * inverse * (target_scale / total)

    def apply(rows):
        high = rows.astype(bf16)
        low = (rows - high.astype(f32)).astype(bf16)
        stacked = jnp.concatenate([high, low], axis=0)
        both = jnp.dot(stacked, normal_ref[...], preferred_element_type=f32)
        return both[:8, :TERMS] + both[:8, TERMS:] + both[8:, :TERMS]

    def fold(column):
        sums = [jnp.zeros((8, TERMS), f32) for _ in range(4)]
        for tile in range(TERMS // 8):
            rows = gram_ref[tile * 8 : tile * 8 + 8, :]
            if column is not None:
                rows = rows * column[tile]
            sums[tile % 4] = sums[tile % 4] + rows
        return jnp.sum((sums[0] + sums[1]) + (sums[2] + sums[3]), axis=0, keepdims=True)

    def spread(row):
        row = jnp.broadcast_to(row, (8, TERMS))
        return [
            jnp.sum(gram_ref[tile * 8 : tile * 8 + 8, :] * row, axis=1, keepdims=True)
            for tile in range(TERMS // 8)
        ]

    column = None
    for sweep in range(POWER // 2):
        row = fold(column)
        if sweep == 0:
            row = row * TERMS**-0.5
        column = spread(row)
    before = jnp.sum(row * row, axis=1, keepdims=True)
    after = column[0] * column[0]
    for tile in range(1, TERMS // 8):
        after = after + column[tile] * column[tile]
    after = jnp.sum(after, axis=0, keepdims=True)
    step_size = jnp.sqrt(before) / jnp.sqrt(after)
    bound = step_size * SHRINK
    coeffs = None
    for sweep in range(ITERS):
        if sweep == 0:
            moved = step_size * normal_cross
        else:
            moved = coeffs - step_size * (apply(coeffs) - normal_cross)
        coeffs = jnp.maximum(moved - bound, 0.0) - jnp.maximum(-moved - bound, 0.0)
    spot_ref[...] = coeffs
    own = pl.multiple_of(lib * 128, 128)
    result_ref[:8, :] = spot_ref[:, pl.ds(own, 128)]
    result_ref[8:, :] = whole_dot(coeffs * inverse, lib_ref[:TERMS], 0)


def kernel(
    exponents_hbm_ref,
    keys_hbm_ref,
    start_ref,
    end_ref,
    plane_weight_ref,
    depth_weight_ref,
    result_ref,
    exponents_ref,
    keys_ref,
    fields_ref,
    later_ref,
    weights_ref,
    depth_ref,
    wide_ref,
    theta_ref,
    rest_ref,
    rest_sum_ref,
    plane_ref,
    table_ref,
    codes_ref,
    pick_ref,
    edge_out_ref,
    edge_in_ref,
    lib_ref,
    gram_ref,
    half_ref,
    half_in_ref,
    parts_in_ref,
    done_ref,
    normal_ref,
    spot_ref,
    local_sems,
    code_sems,
    edge_sems,
    core_sems,
    part_sems,
    done_sems,
    other_sems,
    ready_sems,
):
    sub = lax.axis_index("sub")
    lib = lax.axis_index("lib")
    chips = Chips()
    core = chips.core
    next_sub = {"sub": (sub + 1) % 32, "lib": lib}
    last_sub = {"sub": (sub + 31) % 32, "lib": lib}
    other_core = {"sub": sub, "lib": lib + 1 - 2 * core}
    window = pl.ds(pl.multiple_of(jnp.maximum(lib * 32 - 8, 0), 8), CELLS_Y)
    load_exponents = pltpu.make_async_copy(exponents_hbm_ref, exponents_ref, local_sems.at[4])
    load_exponents.start()
    for field in range(4):
        for number, (source, target) in enumerate(
            ((start_ref, fields_ref), (end_ref, later_ref))
        ):
            pltpu.make_async_copy(
                source.at[field, :, window, :], target.at[field], local_sems.at[number]
            ).start()
    load_weights = pltpu.make_async_copy(
        plane_weight_ref.at[jnp.minimum(lib, 1)], weights_ref, local_sems.at[2]
    )
    load_depth = pltpu.make_async_copy(depth_weight_ref, depth_ref, local_sems.at[3])
    load_keys = pltpu.make_async_copy(keys_hbm_ref, keys_ref, local_sems.at[5])

    barrier = pltpu.get_barrier_semaphore()

    near = [chips.device(d) for d in (1, 2, 3, 4, 8, 12, 16, 32, 48)]
    near += [{"sub": sub, "lib": (lib + step) % 4} for step in (1, 2, 3)]
    near += [next_sub, last_sub]
    for device in near:
        pl.semaphore_signal(barrier, inc=1, device_id=device, device_id_type=MESH)

    load_weights.start()
    load_depth.start()
    load_keys.start()
    load_exponents.wait()
    code = jnp.zeros((1, 128), f32)
    for place in range(7):
        code = code * 3.0 + exponents_ref[place : place + 1, :].astype(f32)
    codes_ref[lib] = jnp.broadcast_to(code, (8, 128))
    lane = lax.broadcasted_iota(jnp.int32, (8, 128), 1)
    codes_ref[4] = jnp.where(lane < 4, TARGET_CODE + lane, -1).astype(f32)

    pltpu.make_async_copy(fields_ref, fields_ref, local_sems.at[0]).wait()
    pltpu.make_async_copy(later_ref, later_ref, local_sems.at[1]).wait()
    products(fields_ref, later_ref, wide_ref, theta_ref, rest_ref)
    pl.semaphore_wait(barrier, len(near))
    for device in near[6:9]:
        pl.semaphore_signal(ready_sems.at[0], inc=1, device_id=device, device_id_type=MESH)
    code_copies = [
        pltpu.make_async_remote_copy(
            src_ref=codes_ref.at[lib],
            dst_ref=codes_ref.at[lib],
            send_sem=code_sems.at[step],
            recv_sem=code_sems.at[3 + step],
            device_id={"sub": sub, "lib": (lib + 1 + step) % 4},
            device_id_type=MESH,
        )
        for step in range(3)
    ]
    for copy in code_copies:
        copy.start()
    load_weights.wait()
    plane_sums(weights_ref, theta_ref, rest_ref, rest_sum_ref, plane_ref, 1, 2)
    pl.semaphore_wait(ready_sems.at[0], 3)
    for device in near[3:6]:
        pl.semaphore_signal(ready_sems.at[1], inc=1, device_id=device, device_id_type=MESH)
    load_depth.wait()
    load_keys.wait()
    depth_sums(plane_ref, depth_ref, table_ref, 2)
    edges = []

    def send_edge(number, code_row, start, count):
        rows = pl.ds(start, count)
        pick_rows(code_row, keys_ref, pick_ref, start, count)
        both = jnp.dot(pick_ref[rows, :], table_ref[...], preferred_element_type=f32)
        edge_out_ref[rows, :] = (both[:, :TESTS] + both[:, TESTS:]).astype(bf16)
        edge = pltpu.make_async_remote_copy(
            src_ref=edge_out_ref.at[rows],
            dst_ref=edge_in_ref.at[rows],
            send_sem=edge_sems.at[number],
            recv_sem=edge_sems.at[5 + number],
            device_id=next_sub,
            device_id_type=MESH,
        )
        edge.start()
        edges.append(edge)

    send_edge(0, code, pl.multiple_of(lib * 128, 128), 128)
    send_edge(1, codes_ref[4, :1, :], TERMS, 16)
    for step, copy in enumerate(code_copies):
        copy.wait()
        part = (lib + 3 - step) % 4
        send_edge(2 + step, codes_ref[part, :1, :], pl.multiple_of(part * 128, 128), 128)
    plane_sums(weights_ref, theta_ref, rest_ref, rest_sum_ref, plane_ref, 0, 2)
    depth_sums(plane_ref, depth_ref, table_ref, 2)
    both = jnp.dot(pick_ref[...], table_ref[...], preferred_element_type=f32)
    lib_ref[...] = both[:, :TESTS] + both[:, TESTS:]
    for edge in edges:
        edge.wait()
    keep = jnp.where(sub > 0, 1.0, 0.0).astype(f32)
    lib_ref[...] = lib_ref[...] + keep * edge_in_ref[...].astype(f32)

    high = lib_ref[...].astype(bf16)
    low = (lib_ref[...] - high.astype(f32)).astype(bf16)
    product = lax.dot_general(
        jnp.concatenate([high, low, high], axis=1),
        jnp.concatenate([high[:TERMS], high[:TERMS], low[:TERMS]], axis=1),
        (((1,), (1,)), ((), ())),
        preferred_element_type=f32,
    )
    gram_ref[...] = product[:TERMS]
    cross = product[TERMS : TERMS + 8]
    target = lib_ref[TERMS : TERMS + 8]
    squares = jnp.broadcast_to(jnp.sum(target * target, axis=1, keepdims=True), (8, 128))

    for piece in range(8):
        gram_ref[64 + piece * 4 : 68 + piece * 4, :64] = cross[:4, piece * 64 : piece * 64 + 64]
    gram_ref[96:100, :64] = squares[:4, :64]

    for half in range(2):
        for number, (i, j) in enumerate(BLOCKS[half][:4]):
            lanes = slice(j * 128, j * 128 + 128)
            for part in range(16):
                row = i * 128 + part * 8
                half_ref[half, number * 16 + part, :8, :] = gram_ref[row : row + 8, lanes]
        i, j = BLOCKS[half][4]
        for part in range(CHIPS):
            row = i * 128 + part * 2
            half_ref[half, part, 8:, :] = gram_ref[row : row + 2, j * 128 : j * 128 + 128]
    pair = pltpu.make_async_remote_copy(
        src_ref=half_ref.at[1 - core],
        dst_ref=half_in_ref,
        send_sem=core_sems.at[0],
        recv_sem=core_sems.at[1],
        device_id=other_core,
        device_id_type=MESH,
    )
    pair.start()
    pair.wait()
    half_in_ref[...] = half_in_ref[...] + half_ref[core]
    pl.semaphore_wait(ready_sems.at[1], 3)
    own = chips.chip(0)
    for d in PARTNERS:
        pltpu.make_async_remote_copy(
            src_ref=half_in_ref.at[chips.chip(d)],
            dst_ref=parts_in_ref.at[d],
            send_sem=part_sems.at[0],
            recv_sem=part_sems.at[1],
            device_id=chips.device(d),
            device_id_type=MESH,
        ).start()
    parts_in_ref[0] = half_in_ref[own]
    received = parts_in_ref.at[pl.ds(1, CHIPS - 1)]
    pltpu.make_async_copy(received, received, part_sems.at[1]).wait()
    done_ref[core, own] = jnp.sum(parts_in_ref[...], axis=0)
    for d in PARTNERS:
        pltpu.make_async_remote_copy(
            src_ref=done_ref.at[core, own],
            dst_ref=done_ref.at[core, own],
            send_sem=done_sems.at[0],
            recv_sem=done_sems.at[1],
            device_id=chips.device(d),
            device_id_type=MESH,
        ).start()
    pltpu.make_async_copy(received, received, part_sems.at[0]).wait()
    pltpu.make_async_copy(received, received, done_sems.at[1]).wait()
    pltpu.make_async_copy(received, received, done_sems.at[0]).wait()
    swap = pltpu.make_async_remote_copy(
        src_ref=done_ref.at[core],
        dst_ref=done_ref.at[core],
        send_sem=other_sems.at[0],
        recv_sem=other_sems.at[1],
        device_id=other_core,
        device_id_type=MESH,
    )
    swap.start()
    swap.wait()
    for half in range(2):
        for number, (i, j) in enumerate(BLOCKS[half][:4]):
            lanes = slice(j * 128, j * 128 + 128)
            for part in range(16):
                row = i * 128 + part * 8
                gram_ref[row : row + 8, lanes] = done_ref[half, number * 16 + part, :8, :]
        i, j = BLOCKS[half][4]
        for part in range(CHIPS):
            row = i * 128 + part * 2
            gram_ref[row : row + 2, j * 128 : j * 128 + 128] = done_ref[half, part, 8:, :]
    cross_sum = jnp.concatenate(
        [
            jnp.concatenate(
                [gram_ref[64 + piece * 4 : 68 + piece * 4, :64] for piece in range(8)], axis=1
            ),
            jnp.zeros((4, TERMS), f32),
        ],
        axis=0,
    )
    square_sum = jnp.concatenate([gram_ref[96:100, :1], jnp.zeros((4, 1), f32)], axis=0)
    gram_ref[64:128, :64] = gram_ref[:64, 64:128].T
    for i in range(4):
        for j in range(i):
            gram_ref[i * 128 : i * 128 + 128, j * 128 : j * 128 + 128] = gram_ref[
                j * 128 : j * 128 + 128, i * 128 : i * 128 + 128
            ].T
    solve(
        gram_ref, normal_ref, lib_ref, cross_sum, square_sum, lib, result_ref, spot_ref
    )


def split_result(result_ref, coef_ref, fit_ref):
    coef_ref[...] = result_ref[:4]
    fit_ref[...] = result_ref[8:12]


def local(snap_start, snap_end, exponents):
    vmem = pl.BlockSpec(memory_space=pltpu.VMEM)
    anywhere = pl.BlockSpec(memory_space=pl.ANY)
    result = pl.pallas_call(
        kernel,
        out_shape=jax.ShapeDtypeStruct((16, TESTS), f32),
        in_specs=[anywhere] * 6,
        out_specs=vmem,
        scratch_shapes=[
            pltpu.VMEM((7, 128), jnp.int32),
            pltpu.VMEM((1, KEYS), f32),
            pltpu.VMEM((4, CELLS_X, CELLS_Y, WIDTH_Z), bf16),
            pltpu.VMEM((4, CELLS_X, CELLS_Y, WIDTH_Z), bf16),
            pltpu.VMEM((2, 2, 2 * CENTERS_Y * PAD, MAIN), bf16),
            pltpu.VMEM((CENTERS_Y * WIDTH_Z, 3 * TESTS), bf16),
            pltpu.VMEM((8, CELLS_XY, WIDTH_Z), f32),
            pltpu.VMEM((PRODUCTS // 2, MAIN, 2 * WIDTH_Z), bf16),
            pltpu.VMEM((PRODUCTS // 4 + 1, 4 * REST, WIDTH_Z), bf16),
            pltpu.VMEM(((PRODUCTS // 4 + 1) * 4 * PAD, WIDTH_Z), f32),
            pltpu.VMEM((2, TABLE, CENTERS_Y * WIDTH_Z), bf16),
            pltpu.VMEM((KEYS, 2 * TESTS), bf16),
            pltpu.VMEM((5, 8, 128), f32),
            pltpu.VMEM((PICKED, KEYS), bf16),
            pltpu.VMEM((PICKED, TESTS), bf16),
            pltpu.VMEM((PICKED, TESTS), bf16),
            pltpu.VMEM((PICKED, TESTS), f32),
            pltpu.VMEM((TERMS, TERMS), f32),
            pltpu.VMEM((2, CHIPS, CHUNK, 128), f32),
            pltpu.VMEM((CHIPS, CHUNK, 128), f32),
            pltpu.VMEM((CHIPS, CHUNK, 128), f32),
            pltpu.VMEM((2, CHIPS, CHUNK, 128), f32),
            pltpu.VMEM((TERMS, 2 * TERMS), bf16),
            pltpu.VMEM((8, TERMS), f32),
            pltpu.SemaphoreType.DMA((6,)),
            pltpu.SemaphoreType.DMA((6,)),
            pltpu.SemaphoreType.DMA((10,)),
            pltpu.SemaphoreType.DMA((2,)),
            pltpu.SemaphoreType.DMA((2,)),
            pltpu.SemaphoreType.DMA((2,)),
            pltpu.SemaphoreType.DMA((2,)),
            pltpu.SemaphoreType.REGULAR((2,)),
        ],
        compiler_params=pltpu.CompilerParams(
            collective_id=0, has_side_effects=True, vmem_limit_bytes=56 << 20
        ),
        name="weak_form_fit",
    )(
        exponents.T,
        jnp.asarray(column_codes()),
        snap_start,
        snap_end,
        jnp.asarray(plane_weights()),
        jnp.asarray(depth_weights()),
    )
    return pl.pallas_call(
        split_result,
        out_shape=(
            jax.ShapeDtypeStruct((4, TERMS // 4), f32),
            jax.ShapeDtypeStruct((4, TESTS), f32),
        ),
        in_specs=[vmem],
        out_specs=(vmem, vmem),
        name="split_result",
    )(result)


def solution(mesh):
    placed = (P(None, "sub", None, None), P(None, "sub", None, None), P("lib", None))
    return jax.shard_map(
        local,
        mesh=mesh,
        in_specs=placed,
        out_specs=(P(None, "lib"), P(None, ("sub", "lib"))),
        check_vma=False,
    )
```

```python
import functools

import jax
import jax.numpy as jnp
import ml_dtypes
import numpy as np
from jax import lax
from jax.experimental import pallas as pl
from jax.experimental.pallas import tpu as pltpu
from jax.sharding import PartitionSpec as P

STRIDE = 8
RADIUS = 8
POWER = 6
ITERS = 10
TERMS = 512
ROWS = 16384
RIDGE = 0.1
SHRINK = 0.05
EPSILON = 1e-06

CELLS_X = 8
CELLS_Y = 40
CELLS_XY = CELLS_X * CELLS_Y
MAIN_Y = 32
MAIN = CELLS_X * MAIN_Y
REST = CELLS_XY - MAIN
WIDTH_Z = 256
CENTERS_Y = 4
CENTERS_Z = 32
TESTS = CENTERS_Y * CENTERS_Z

POWERS = [
    (a, b, c, e)
    for a in range(3)
    for b in range(3)
    for c in range(3)
    for e in range(3)
    if 1 <= a + b + c + e <= 3
]
PRODUCTS = len(POWERS) + 4
PAD = 16
TABLE = PRODUCTS * PAD
KEYS = 3 * TABLE
PICKED = TERMS + 16
TARGET_CODE = 4000

CHUNK = 10
CHIPS = 64
BLOCKS = (
    ((0, 0), (0, 1), (0, 2), (0, 3), (3, 3)),
    ((1, 1), (1, 2), (1, 3), (2, 2), (2, 3)),
)
HOPS = (0, 1, 2, 1)
PARTNERS = sorted(
    range(1, CHIPS), key=lambda d: -(HOPS[d // 16] + HOPS[d // 4 % 4] + HOPS[d % 4])
)

MESH = pl.DeviceIdType.MESH
f32 = jnp.float32
bf16 = jnp.bfloat16


def tap(order, offset):
    s = np.asarray(offset, np.float64) / RADIUS
    base = 1.0 - s * s
    value = (base**3, 6.0 * s * base**2, -6.0 * base * (1.0 - 5.0 * s * s))[order]
    return np.where(np.abs(s) <= 1.0, value, 0.0)


def split_pieces(values):
    high = values.astype(ml_dtypes.bfloat16)
    low = (values - high.astype(np.float64)).astype(ml_dtypes.bfloat16)
    return high, low


def plane_weights():
    x = np.arange(CELLS_X)[:, None]
    y = np.arange(CELLS_Y)[None, :]
    both = []
    for shift in (0, STRIDE):
        full = np.zeros((2, CENTERS_Y, PAD, CELLS_X, CELLS_Y))
        for side in range(2):
            for center in range(CENTERS_Y):
                for order_x in range(3):
                    for order_y in range(3):
                        full[side, center, order_x * 3 + order_y] = tap(
                            order_x, x - STRIDE * side
                        ) * tap(order_y, y - STRIDE * center - shift)
        wide = full[..., :MAIN_Y].reshape(2, CENTERS_Y * PAD, MAIN)
        edge = full[:, CENTERS_Y - 1, :, :, MAIN_Y:].reshape(2, PAD, REST)
        apart = np.zeros((2, 4, PAD, 4, REST))
        for member in range(4):
            apart[:, member, :, member, :] = edge
        groups = (wide, apart.reshape(2, 4 * PAD, 4 * REST))
        both.append(np.stack([np.concatenate(split_pieces(g), axis=1) for g in groups]))
    return np.stack(both)


def depth_weights():
    z = np.arange(WIDTH_Z)[:, None]
    centers = STRIDE * np.arange(CENTERS_Z)[None, :]
    full = np.zeros((CENTERS_Y, WIDTH_Z, 3, CENTERS_Y, CENTERS_Z))
    for order in range(3):
        for center in range(CENTERS_Y):
            full[center, :, order, center, :] = tap(order, z - centers)
    return full.reshape(CENTERS_Y * WIDTH_Z, 3 * TESTS).astype(ml_dtypes.bfloat16)


def column_codes():
    codes = np.full((3, PRODUCTS, PAD), -2.0, np.float32)
    for index, (a, b, c, e) in enumerate(POWERS):
        for order_z in range(3):
            for plane in range(9):
                codes[order_z, index, plane] = (
                    (((a * 3 + b) * 3 + c) * 3 + e) * 27 + plane * 3 + order_z
                )
    for field in range(4):
        codes[0, len(POWERS) + field, 0] = TARGET_CODE + field
    return codes.reshape(1, KEYS)


def others(value):
    return value, value + 1 - 2 * (value % 2), (value + 2) % 4, 3 - value


class Chips:
    def __init__(self):
        sub = lax.axis_index("sub")
        lib = lax.axis_index("lib")
        self.core = lib % 2
        self.x = others(sub // 8)
        self.y = others((sub // 4) % 2 * 2 + lib // 2)
        self.z = others(sub % 4)
        self.sub_x = [8 * v for v in self.x]
        self.sub_y = [v // 2 * 4 for v in self.y]
        self.lib_y = [v % 2 * 2 + self.core for v in self.y]
        self.chip_xy = [[16 * v + 4 * w for w in self.y] for v in self.x]

    def chip(self, d):
        return self.chip_xy[d // 16][d // 4 % 4] + self.z[d % 4]

    def device(self, d):
        return {
            "sub": self.sub_x[d // 16] + self.sub_y[d // 4 % 4] + self.z[d % 4],
            "lib": self.lib_y[d // 4 % 4],
        }


def products(fields_ref, later_ref, wide_ref, theta_ref, rest_ref):
    for field in range(4):
        for x in range(CELLS_X):
            for base, source in ((0, fields_ref), (4, later_ref)):
                plane = source[field, x].astype(f32)
                wide_ref[base + field, x * MAIN_Y : x * MAIN_Y + MAIN_Y, :] = plane[:MAIN_Y]
                wide_ref[base + field, MAIN + x * 8 : MAIN + x * 8 + 8, :] = plane[MAIN_Y:]

    def some(at, lanes, put):
        value = [wide_ref[field, pl.ds(at, 16), lanes] for field in range(4)]
        square = [v * v for v in value]
        pairs = {}
        for index, powers in enumerate(POWERS):
            result = None
            key = ()
            for field, power in enumerate(powers):
                if power == 0:
                    continue
                factor = value[field] if power == 1 else square[field]
                key = key + ((field, power),)
                if result is None:
                    result = factor
                elif key in pairs:
                    result = pairs[key]
                else:
                    result = result * factor
                    pairs[key] = result
            put(index, result.astype(bf16))
        for field in range(4):
            change = wide_ref[4 + field, pl.ds(at, 16), lanes] - value[field]
            put(len(POWERS) + field, change.astype(bf16))

    def main_rows(step, carry):
        at = pl.multiple_of(step * 16, 16)
        for half in range(2):

            def put(index, value, half=half):
                lane = index % 2 * WIDTH_Z + half * 128
                theta_ref[index // 2, pl.ds(at, 16), lane : lane + 128] = value

            some(at, slice(half * 128, half * 128 + 128), put)
        return carry

    def rest_rows(step, carry):
        at = pl.multiple_of(step * 16, 16)
        for half in range(2):
            lanes = slice(half * 128, half * 128 + 128)

            def put(index, value, lanes=lanes):
                rest_ref[index // 4, pl.ds(index % 4 * REST + at, 16), lanes] = value

            some(MAIN + at, lanes, put)
        return carry

    lax.fori_loop(0, MAIN // 16, main_rows, 0)
    lax.fori_loop(0, REST // 16, rest_rows, 0)
    used = PRODUCTS % 4 * REST
    rest_ref[PRODUCTS // 4, used:, :] = jnp.zeros((4 * REST - used, WIDTH_Z), bf16)


def plane_sums(weights_ref, theta_ref, rest_ref, rest_sum_ref, plane_ref, side):
    half = CENTERS_Y * PAD

    def leftover(index, carry):
        both = jnp.dot(weights_ref[1, side], rest_ref[index], preferred_element_type=f32)
        at = pl.multiple_of(index * half, half)
        rest_sum_ref[pl.ds(at, half), :] = both[:half] + both[half:]
        return carry

    def pair(index, carry):
        both = jnp.dot(weights_ref[0, side], theta_ref[index], preferred_element_type=f32)
        total = both[:half] + both[half:]
        for member in range(2):
            at = pl.multiple_of((index * 2 + member) * PAD, PAD)
            for center in range(CENTERS_Y):
                part = total[center * PAD : center * PAD + PAD, member * WIDTH_Z :][:, :WIDTH_Z]
                if center == CENTERS_Y - 1:
                    part = part + rest_sum_ref[pl.ds(at, PAD), :]
                lanes = slice(center * WIDTH_Z, (center + 1) * WIDTH_Z)
                high = part.astype(bf16)
                plane_ref[0, pl.ds(at, PAD), lanes] = high
                plane_ref[1, pl.ds(at, PAD), lanes] = (part - high.astype(f32)).astype(bf16)
        return carry

    lax.fori_loop(0, PRODUCTS // 4 + 1, leftover, 0, unroll=9)
    lax.fori_loop(0, PRODUCTS // 2, pair, 0, unroll=PRODUCTS // 2)


def depth_sums(plane_ref, depth_ref, table_ref, keep_low):
    size = TABLE // 2
    for start in range(0, TABLE, size):
        total = jnp.dot(
            plane_ref[0, start : start + size], depth_ref[...], preferred_element_type=f32
        )
        total = total + jnp.dot(
            plane_ref[1, start : start + size], depth_ref[...], preferred_element_type=f32
        )
        top = total.astype(bf16)
        rest = (total - top.astype(f32)).astype(bf16)
        for order in range(3):
            lanes = slice(order * TESTS, (order + 1) * TESTS)
            rows = slice(order * TABLE + start, order * TABLE + start + size)
            table_ref[rows, :TESTS] = top[:, lanes]
            if keep_low:
                table_ref[rows, TESTS:] = rest[:, lanes]


def pick_rows(code, keys_ref, pick_ref, start, count):
    spread = jnp.broadcast_to(code, (128, 128)).T
    for row in range(0, count, 16):
        for column in range(0, KEYS, 128):
            width = min(128, KEYS - column)
            same = spread[row : row + 16, :width] == keys_ref[:, column : column + width]
            pick_ref[pl.ds(start + row, 16), column : column + width] = jnp.where(
                same, 1.0, 0.0
            ).astype(bf16)


def whole_dot(left, right, contract):
    return lax.dot_general(
        left,
        right,
        (((1,), (contract,)), ((), ())),
        precision=lax.Precision.HIGHEST,
        preferred_element_type=f32,
    )


def solve(gram_ref, normal_ref, lib_ref, cross, target_squares, lib, result_ref, spot_ref):
    total = float(ROWS)
    diagonal_row = []
    diagonal_column = []
    same = lax.broadcasted_iota(jnp.int32, (128, 128), 0) == lax.broadcasted_iota(
        jnp.int32, (128, 128), 1
    )
    for block in range(4):
        at = slice(block * 128, block * 128 + 128)
        spread = jnp.where(same, gram_ref[at, at], 0.0)
        diagonal_row.append(jnp.sum(spread, axis=0, keepdims=True))
        diagonal_column.append(jnp.sum(spread, axis=1, keepdims=True))
    inverse_row = [1.0 / jnp.sqrt(d / total + EPSILON) for d in diagonal_row]
    inverse_column = [1.0 / jnp.sqrt(d / total + EPSILON) for d in diagonal_column]
    for i in range(4):
        for j in range(4):
            rows, lanes = slice(i * 128, i * 128 + 128), slice(j * 128, j * 128 + 128)
            block = gram_ref[rows, lanes] * (inverse_column[i] / total) * inverse_row[j]
            if i == j:
                block = block + jnp.where(same, RIDGE, 0.0)
            gram_ref[rows, lanes] = block
            high = block.astype(bf16)
            normal_ref[rows, lanes] = high
            normal_ref[rows, slice(TERMS + j * 128, TERMS + j * 128 + 128)] = (
                block - high.astype(f32)
            ).astype(bf16)
    inverse = jnp.concatenate(inverse_row, axis=1)
    target_scale = 1.0 / jnp.sqrt(target_squares / total + EPSILON)
    normal_cross = cross * inverse * (target_scale / total)

    def apply(rows):
        high = rows.astype(bf16)
        low = (rows - high.astype(f32)).astype(bf16)
        stacked = jnp.concatenate([high, low], axis=0)
        both = jnp.dot(stacked, normal_ref[...], preferred_element_type=f32)
        return both[:8, :TERMS] + both[:8, TERMS:] + both[8:, :TERMS]

    def fold(column):
        sums = [jnp.zeros((8, TERMS), f32) for _ in range(4)]
        for tile in range(TERMS // 8):
            rows = gram_ref[tile * 8 : tile * 8 + 8, :]
            if column is not None:
                rows = rows * column[tile]
            sums[tile % 4] = sums[tile % 4] + rows
        return jnp.sum((sums[0] + sums[1]) + (sums[2] + sums[3]), axis=0, keepdims=True)

    def spread(row):
        row = jnp.broadcast_to(row, (8, TERMS))
        return [
            jnp.sum(gram_ref[tile * 8 : tile * 8 + 8, :] * row, axis=1, keepdims=True)
            for tile in range(TERMS // 8)
        ]

    column = None
    for sweep in range(POWER // 2):
        row = fold(column)
        if sweep == 0:
            row = row * TERMS**-0.5
        column = spread(row)
    before = jnp.sum(row * row, axis=1, keepdims=True)
    after = column[0] * column[0]
    for tile in range(1, TERMS // 8):
        after = after + column[tile] * column[tile]
    after = jnp.sum(after, axis=0, keepdims=True)
    step_size = jnp.sqrt(before) / jnp.sqrt(after)
    bound = step_size * SHRINK
    coeffs = None
    for sweep in range(ITERS):
        if sweep == 0:
            moved = step_size * normal_cross
        else:
            moved = coeffs - step_size * (apply(coeffs) - normal_cross)
        coeffs = jnp.maximum(moved - bound, 0.0) - jnp.maximum(-moved - bound, 0.0)
    spot_ref[...] = coeffs
    own = pl.multiple_of(lib * 128, 128)
    result_ref[:8, :] = spot_ref[:, pl.ds(own, 128)]
    result_ref[8:, :] = whole_dot(coeffs * inverse, lib_ref[:TERMS], 0)


def kernel(
    exponents_hbm_ref,
    keys_hbm_ref,
    start_ref,
    end_ref,
    plane_weight_ref,
    depth_weight_ref,
    result_ref,
    exponents_ref,
    keys_ref,
    fields_ref,
    later_ref,
    weights_ref,
    depth_ref,
    wide_ref,
    theta_ref,
    rest_ref,
    rest_sum_ref,
    plane_ref,
    table_ref,
    codes_ref,
    pick_ref,
    edge_out_ref,
    edge_in_ref,
    lib_ref,
    gram_ref,
    half_ref,
    half_in_ref,
    parts_in_ref,
    done_ref,
    normal_ref,
    spot_ref,
    local_sems,
    code_sems,
    edge_sems,
    core_sems,
    part_sems,
    done_sems,
    other_sems,
    ready_sems,
):
    sub = lax.axis_index("sub")
    lib = lax.axis_index("lib")
    chips = Chips()
    core = chips.core
    next_sub = {"sub": (sub + 1) % 32, "lib": lib}
    last_sub = {"sub": (sub + 31) % 32, "lib": lib}
    other_core = {"sub": sub, "lib": lib + 1 - 2 * core}
    window = pl.ds(pl.multiple_of(jnp.maximum(lib * 32 - 8, 0), 8), CELLS_Y)
    load_exponents = pltpu.make_async_copy(exponents_hbm_ref, exponents_ref, local_sems.at[4])
    load_exponents.start()
    for field in range(4):
        for number, (source, target) in enumerate(
            ((start_ref, fields_ref), (end_ref, later_ref))
        ):
            pltpu.make_async_copy(
                source.at[field, :, window, :], target.at[field], local_sems.at[number]
            ).start()
    load_weights = pltpu.make_async_copy(
        plane_weight_ref.at[jnp.minimum(lib, 1)], weights_ref, local_sems.at[2]
    )
    load_depth = pltpu.make_async_copy(depth_weight_ref, depth_ref, local_sems.at[3])
    load_keys = pltpu.make_async_copy(keys_hbm_ref, keys_ref, local_sems.at[5])

    barrier = pltpu.get_barrier_semaphore()

    near = [chips.device(d) for d in (1, 2, 3, 4, 8, 12, 16, 32, 48)]
    near += [{"sub": sub, "lib": (lib + step) % 4} for step in (1, 2, 3)]
    for device in near:
        pl.semaphore_signal(barrier, inc=1, device_id=device, device_id_type=MESH)
    sends = sub < 31
    receives = sub > 0

    @pl.when(sends)
    def _():
        pl.semaphore_signal(barrier, inc=1, device_id=next_sub, device_id_type=MESH)

    @pl.when(receives)
    def _():
        pl.semaphore_signal(barrier, inc=1, device_id=last_sub, device_id_type=MESH)

    load_weights.start()
    load_depth.start()
    load_keys.start()
    load_exponents.wait()
    code = jnp.zeros((1, 128), f32)
    for place in range(7):
        code = code * 3.0 + exponents_ref[place : place + 1, :].astype(f32)
    codes_ref[lib] = jnp.broadcast_to(code, (8, 128))
    lane = lax.broadcasted_iota(jnp.int32, (8, 128), 1)
    codes_ref[4] = jnp.where(lane < 4, TARGET_CODE + lane, -1).astype(f32)

    pltpu.make_async_copy(fields_ref, fields_ref, local_sems.at[0]).wait()
    pltpu.make_async_copy(later_ref, later_ref, local_sems.at[1]).wait()
    products(fields_ref, later_ref, wide_ref, theta_ref, rest_ref)
    pl.semaphore_wait(barrier, len(near) + jnp.minimum(sub, 1) + jnp.minimum(31 - sub, 1))
    for device in near[6:9]:
        pl.semaphore_signal(ready_sems.at[0], inc=1, device_id=device, device_id_type=MESH)
    code_copies = [
        pltpu.make_async_remote_copy(
            src_ref=codes_ref.at[lib],
            dst_ref=codes_ref.at[lib],
            send_sem=code_sems.at[step],
            recv_sem=code_sems.at[3 + step],
            device_id={"sub": sub, "lib": (lib + 1 + step) % 4},
            device_id_type=MESH,
        )
        for step in range(3)
    ]
    for copy in code_copies:
        copy.start()
    load_weights.wait()
    plane_sums(weights_ref, theta_ref, rest_ref, rest_sum_ref, plane_ref, 1)
    pl.semaphore_wait(ready_sems.at[0], 3)
    for device in near[3:6]:
        pl.semaphore_signal(ready_sems.at[1], inc=1, device_id=device, device_id_type=MESH)
    load_depth.wait()
    load_keys.wait()
    depth_sums(plane_ref, depth_ref, table_ref, False)
    edges = []

    def send_edge(number, code_row, start, count):
        rows = pl.ds(start, count)
        pick_rows(code_row, keys_ref, pick_ref, start, count)
        edge_out_ref[rows, :] = jnp.dot(
            pick_ref[rows, :], table_ref[:, :TESTS], preferred_element_type=f32
        ).astype(bf16)
        edge = pltpu.make_async_remote_copy(
            src_ref=edge_out_ref.at[rows],
            dst_ref=edge_in_ref.at[rows],
            send_sem=edge_sems.at[number],
            recv_sem=edge_sems.at[5 + number],
            device_id=next_sub,
            device_id_type=MESH,
        )
        edges.append(edge)

        @pl.when(sends)
        def _():
            edge.start()

    send_edge(0, code, pl.multiple_of(lib * 128, 128), 128)
    send_edge(1, codes_ref[4, :1, :], TERMS, 16)
    for step, copy in enumerate(code_copies):
        copy.wait()
        part = (lib + 3 - step) % 4
        send_edge(2 + step, codes_ref[part, :1, :], pl.multiple_of(part * 128, 128), 128)
    plane_sums(weights_ref, theta_ref, rest_ref, rest_sum_ref, plane_ref, 0)
    depth_sums(plane_ref, depth_ref, table_ref, True)
    both = jnp.dot(pick_ref[...], table_ref[...], preferred_element_type=f32)
    lib_ref[...] = both[:, :TESTS] + both[:, TESTS:]
    @pl.when(sends)
    def _():
        for edge in edges:
            edge.wait_send()

    @pl.when(receives)
    def _():
        for edge in edges:
            edge.wait_recv()
        lib_ref[...] = lib_ref[...] + edge_in_ref[...].astype(f32)

    high = lib_ref[...].astype(bf16)
    low = (lib_ref[...] - high.astype(f32)).astype(bf16)
    product = lax.dot_general(
        jnp.concatenate([high, low, high], axis=1),
        jnp.concatenate([high[:TERMS], high[:TERMS], low[:TERMS]], axis=1),
        (((1,), (1,)), ((), ())),
        preferred_element_type=f32,
    )
    cross = product[TERMS : TERMS + 8]
    target = lib_ref[TERMS : TERMS + 8]
    squares = jnp.sum(target * target, axis=1, keepdims=True)
    pairs = []
    for group in range(2):
        first = group * CHIPS // 2
        for half in range(2):
            for number in range(group * 2, group * 2 + 2):
                i, j = BLOCKS[half][number]
                lanes = slice(j * 128, j * 128 + 128)
                for part in range(16):
                    row = i * 128 + part * 8
                    half_ref[half, number * 16 + part, :8, :] = product[row : row + 8, lanes]
            i, j = BLOCKS[half][4]
            for part in range(first, first + CHIPS // 2):
                row = i * 128 + part * 2
                half_ref[half, part, 8:, :] = product[row : row + 2, j * 128 : j * 128 + 128]
        if group == 0:
            for piece in range(8):
                half_ref[0, 8 + piece // 2, piece % 2 * 4 : piece % 2 * 4 + 4, :64] = cross[
                    :4, piece * 64 : piece * 64 + 64
                ]
            half_ref[0, 12, :4, :64] = jnp.broadcast_to(squares[:4], (4, 64))
        chunks = pl.ds(first, CHIPS // 2)
        pair = pltpu.make_async_remote_copy(
            src_ref=half_ref.at[1 - core, chunks],
            dst_ref=half_in_ref.at[chunks],
            send_sem=core_sems.at[group],
            recv_sem=core_sems.at[2 + group],
            device_id=other_core,
            device_id_type=MESH,
        )
        pair.start()
        pairs.append(pair)
    for pair in pairs:
        pair.wait()
    half_in_ref[...] = half_in_ref[...] + half_ref[core]
    pl.semaphore_wait(ready_sems.at[1], 3)
    own = chips.chip(0)
    for d in PARTNERS:
        pltpu.make_async_remote_copy(
            src_ref=half_in_ref.at[chips.chip(d)],
            dst_ref=parts_in_ref.at[d],
            send_sem=part_sems.at[0],
            recv_sem=part_sems.at[1],
            device_id=chips.device(d),
            device_id_type=MESH,
        ).start()
    parts_in_ref[0] = half_in_ref[own]
    received = parts_in_ref.at[pl.ds(1, CHIPS - 1)]
    pltpu.make_async_copy(received, received, part_sems.at[1]).wait()
    done_ref[core, own] = jnp.sum(parts_in_ref[...], axis=0)
    for d in PARTNERS:
        pltpu.make_async_remote_copy(
            src_ref=done_ref.at[core, own],
            dst_ref=done_ref.at[core, own],
            send_sem=done_sems.at[0],
            recv_sem=done_sems.at[1],
            device_id=chips.device(d),
            device_id_type=MESH,
        ).start()
    pltpu.make_async_copy(received, received, part_sems.at[0]).wait()
    pltpu.make_async_copy(received, received, done_sems.at[1]).wait()
    pltpu.make_async_copy(received, received, done_sems.at[0]).wait()
    swap = pltpu.make_async_remote_copy(
        src_ref=done_ref.at[core],
        dst_ref=done_ref.at[core],
        send_sem=other_sems.at[0],
        recv_sem=other_sems.at[1],
        device_id=other_core,
        device_id_type=MESH,
    )
    swap.start()
    swap.wait()
    for half in range(2):
        for number, (i, j) in enumerate(BLOCKS[half][:4]):
            lanes = slice(j * 128, j * 128 + 128)
            for part in range(16):
                row = i * 128 + part * 8
                gram_ref[row : row + 8, lanes] = done_ref[half, number * 16 + part, :8, :]
        i, j = BLOCKS[half][4]
        for part in range(CHIPS):
            row = i * 128 + part * 2
            gram_ref[row : row + 2, j * 128 : j * 128 + 128] = done_ref[half, part, 8:, :]
    cross_sum = jnp.concatenate(
        [
            jnp.concatenate(
                [gram_ref[64 + piece * 4 : 68 + piece * 4, :64] for piece in range(8)], axis=1
            ),
            jnp.zeros((4, TERMS), f32),
        ],
        axis=0,
    )
    square_sum = jnp.concatenate([gram_ref[96:100, :1], jnp.zeros((4, 1), f32)], axis=0)
    gram_ref[64:128, :64] = gram_ref[:64, 64:128].T
    for i in range(4):
        for j in range(i):
            gram_ref[i * 128 : i * 128 + 128, j * 128 : j * 128 + 128] = gram_ref[
                j * 128 : j * 128 + 128, i * 128 : i * 128 + 128
            ].T
    solve(
        gram_ref, normal_ref, lib_ref, cross_sum, square_sum, lib, result_ref, spot_ref
    )


def split_result(result_ref, coef_ref, fit_ref):
    coef_ref[...] = result_ref[:4]
    fit_ref[...] = result_ref[8:12]


def local(snap_start, snap_end, exponents):
    vmem = pl.BlockSpec(memory_space=pltpu.VMEM)
    anywhere = pl.BlockSpec(memory_space=pl.ANY)
    result = pl.pallas_call(
        kernel,
        out_shape=jax.ShapeDtypeStruct((16, TESTS), f32),
        in_specs=[anywhere] * 6,
        out_specs=vmem,
        scratch_shapes=[
            pltpu.VMEM((7, 128), jnp.int32),
            pltpu.VMEM((1, KEYS), f32),
            pltpu.VMEM((4, CELLS_X, CELLS_Y, WIDTH_Z), bf16),
            pltpu.VMEM((4, CELLS_X, CELLS_Y, WIDTH_Z), bf16),
            pltpu.VMEM((2, 2, 2 * CENTERS_Y * PAD, MAIN), bf16),
            pltpu.VMEM((CENTERS_Y * WIDTH_Z, 3 * TESTS), bf16),
            pltpu.VMEM((8, CELLS_XY, WIDTH_Z), f32),
            pltpu.VMEM((PRODUCTS // 2, MAIN, 2 * WIDTH_Z), bf16),
            pltpu.VMEM((PRODUCTS // 4 + 1, 4 * REST, WIDTH_Z), bf16),
            pltpu.VMEM(((PRODUCTS // 4 + 1) * 4 * PAD, WIDTH_Z), f32),
            pltpu.VMEM((2, TABLE, CENTERS_Y * WIDTH_Z), bf16),
            pltpu.VMEM((KEYS, 2 * TESTS), bf16),
            pltpu.VMEM((5, 8, 128), f32),
            pltpu.VMEM((PICKED, KEYS), bf16),
            pltpu.VMEM((PICKED, TESTS), bf16),
            pltpu.VMEM((PICKED, TESTS), bf16),
            pltpu.VMEM((PICKED, TESTS), f32),
            pltpu.VMEM((TERMS, TERMS), f32),
            pltpu.VMEM((2, CHIPS, CHUNK, 128), f32),
            pltpu.VMEM((CHIPS, CHUNK, 128), f32),
            pltpu.VMEM((CHIPS, CHUNK, 128), f32),
            pltpu.VMEM((2, CHIPS, CHUNK, 128), f32),
            pltpu.VMEM((TERMS, 2 * TERMS), bf16),
            pltpu.VMEM((8, TERMS), f32),
            pltpu.SemaphoreType.DMA((6,)),
            pltpu.SemaphoreType.DMA((6,)),
            pltpu.SemaphoreType.DMA((10,)),
            pltpu.SemaphoreType.DMA((4,)),
            pltpu.SemaphoreType.DMA((2,)),
            pltpu.SemaphoreType.DMA((2,)),
            pltpu.SemaphoreType.DMA((2,)),
            pltpu.SemaphoreType.REGULAR((2,)),
        ],
        compiler_params=pltpu.CompilerParams(
            collective_id=0, has_side_effects=True, vmem_limit_bytes=56 << 20
        ),
        name="weak_form_fit",
    )(
        exponents.T,
        jnp.asarray(column_codes()),
        snap_start,
        snap_end,
        jnp.asarray(plane_weights()),
        jnp.asarray(depth_weights()),
    )
    return pl.pallas_call(
        split_result,
        out_shape=(
            jax.ShapeDtypeStruct((4, TERMS // 4), f32),
            jax.ShapeDtypeStruct((4, TESTS), f32),
        ),
        in_specs=[vmem],
        out_specs=(vmem, vmem),
        name="split_result",
    )(result)


def solution(mesh):
    placed = (P(None, "sub", None, None), P(None, "sub", None, None), P("lib", None))
    return jax.shard_map(
        local,
        mesh=mesh,
        in_specs=placed,
        out_specs=(P(None, "lib"), P(None, ("sub", "lib"))),
        check_vma=False,
    )
```

```python
import functools

import jax
import jax.numpy as jnp
import ml_dtypes
import numpy as np
from jax import lax
from jax.experimental import pallas as pl
from jax.experimental.pallas import tpu as pltpu
from jax.sharding import PartitionSpec as P

STRIDE = 8
RADIUS = 8
POWER = 6
ITERS = 10
TERMS = 512
ROWS = 16384
RIDGE = 0.1
SHRINK = 0.05
EPSILON = 1e-06

CELLS_X = 8
CELLS_Y = 40
CELLS_XY = CELLS_X * CELLS_Y
MAIN_Y = 32
MAIN = CELLS_X * MAIN_Y
REST = CELLS_XY - MAIN
WIDTH_Z = 256
CENTERS_Y = 4
CENTERS_Z = 32
TESTS = CENTERS_Y * CENTERS_Z

POWERS = [
    (a, b, c, e)
    for a in range(3)
    for b in range(3)
    for c in range(3)
    for e in range(3)
    if 1 <= a + b + c + e <= 3
]
PRODUCTS = len(POWERS) + 4
PAD = 16
TABLE = PRODUCTS * PAD
KEYS = 3 * TABLE
PICKED = TERMS + 16
TARGET_CODE = 4000

CHUNK = 10
CHIPS = 64
BLOCKS = (
    ((0, 0), (0, 1), (0, 2), (0, 3), (3, 3)),
    ((1, 1), (1, 2), (1, 3), (2, 2), (2, 3)),
)
HOPS = (0, 1, 2, 1)
PARTNERS = sorted(
    range(1, CHIPS), key=lambda d: -(HOPS[d // 16] + HOPS[d // 4 % 4] + HOPS[d % 4])
)

MESH = pl.DeviceIdType.MESH
f32 = jnp.float32
bf16 = jnp.bfloat16


def tap(order, offset):
    s = np.asarray(offset, np.float64) / RADIUS
    base = 1.0 - s * s
    value = (base**3, 6.0 * s * base**2, -6.0 * base * (1.0 - 5.0 * s * s))[order]
    return np.where(np.abs(s) <= 1.0, value, 0.0)


def split_pieces(values):
    high = values.astype(ml_dtypes.bfloat16)
    low = (values - high.astype(np.float64)).astype(ml_dtypes.bfloat16)
    return high, low


def plane_weights():
    x = np.arange(CELLS_X)[:, None]
    y = np.arange(CELLS_Y)[None, :]
    both = []
    for shift in (0, STRIDE):
        full = np.zeros((2, CENTERS_Y, PAD, CELLS_X, CELLS_Y))
        for side in range(2):
            for center in range(CENTERS_Y):
                for order_x in range(3):
                    for order_y in range(3):
                        full[side, center, order_x * 3 + order_y] = tap(
                            order_x, x - STRIDE * side
                        ) * tap(order_y, y - STRIDE * center - shift)
        wide = full[..., :MAIN_Y].reshape(2, CENTERS_Y * PAD, MAIN)
        edge = full[:, CENTERS_Y - 1, :, :, MAIN_Y:].reshape(2, PAD, REST)
        apart = np.zeros((2, 4, PAD, 4, REST))
        for member in range(4):
            apart[:, member, :, member, :] = edge
        groups = (wide, apart.reshape(2, 4 * PAD, 4 * REST))
        both.append(np.stack([np.concatenate(split_pieces(g), axis=1) for g in groups]))
    return np.stack(both)


def depth_weights():
    z = np.arange(WIDTH_Z)[:, None]
    centers = STRIDE * np.arange(CENTERS_Z)[None, :]
    full = np.zeros((CENTERS_Y, WIDTH_Z, 3, CENTERS_Y, CENTERS_Z))
    for order in range(3):
        for center in range(CENTERS_Y):
            full[center, :, order, center, :] = tap(order, z - centers)
    return full.reshape(CENTERS_Y * WIDTH_Z, 3 * TESTS).astype(ml_dtypes.bfloat16)


def column_codes():
    codes = np.full((3, PRODUCTS, PAD), -2.0, np.float32)
    for index, (a, b, c, e) in enumerate(POWERS):
        for order_z in range(3):
            for plane in range(9):
                codes[order_z, index, plane] = (
                    (((a * 3 + b) * 3 + c) * 3 + e) * 27 + plane * 3 + order_z
                )
    for field in range(4):
        codes[0, len(POWERS) + field, 0] = TARGET_CODE + field
    return codes.reshape(1, KEYS)


def others(value):
    return value, value + 1 - 2 * (value % 2), (value + 2) % 4, 3 - value


class Chips:
    def __init__(self):
        sub = lax.axis_index("sub")
        lib = lax.axis_index("lib")
        self.core = lib % 2
        self.x = others(sub // 8)
        self.y = others((sub // 4) % 2 * 2 + lib // 2)
        self.z = others(sub % 4)
        self.sub_x = [8 * v for v in self.x]
        self.sub_y = [v // 2 * 4 for v in self.y]
        self.lib_y = [v % 2 * 2 + self.core for v in self.y]
        self.chip_xy = [[16 * v + 4 * w for w in self.y] for v in self.x]

    def chip(self, d):
        return self.chip_xy[d // 16][d // 4 % 4] + self.z[d % 4]

    def device(self, d):
        return {
            "sub": self.sub_x[d // 16] + self.sub_y[d // 4 % 4] + self.z[d % 4],
            "lib": self.lib_y[d // 4 % 4],
        }


def widen(source_ref, wide_ref, base):
    for field in range(4):
        for x in range(CELLS_X):
            plane = source_ref[field, x].astype(f32)
            wide_ref[base + field, x * MAIN_Y : x * MAIN_Y + MAIN_Y, :] = plane[:MAIN_Y]
            wide_ref[base + field, MAIN + x * 8 : MAIN + x * 8 + 8, :] = plane[MAIN_Y:]


def products(wide_ref, theta_ref, rest_ref, changes):

    def some(at, lanes, put):
        value = [wide_ref[field, pl.ds(at, 16), lanes] for field in range(4)]
        if changes:
            for field in range(4):
                change = wide_ref[4 + field, pl.ds(at, 16), lanes] - value[field]
                put(len(POWERS) + field, change.astype(bf16))
            return
        square = [v * v for v in value]
        pairs = {}
        for index, powers in enumerate(POWERS):
            result = None
            key = ()
            for field, power in enumerate(powers):
                if power == 0:
                    continue
                factor = value[field] if power == 1 else square[field]
                key = key + ((field, power),)
                if result is None:
                    result = factor
                elif key in pairs:
                    result = pairs[key]
                else:
                    result = result * factor
                    pairs[key] = result
            put(index, result.astype(bf16))

    def main_rows(step, carry):
        at = pl.multiple_of(step * 16, 16)
        for half in range(2):

            def put(index, value, half=half):
                lane = index % 2 * WIDTH_Z + half * 128
                theta_ref[index // 2, pl.ds(at, 16), lane : lane + 128] = value

            some(at, slice(half * 128, half * 128 + 128), put)
        return carry

    def rest_rows(step, carry):
        at = pl.multiple_of(step * 16, 16)
        for half in range(2):
            lanes = slice(half * 128, half * 128 + 128)

            def put(index, value, lanes=lanes):
                rest_ref[index // 4, pl.ds(index % 4 * REST + at, 16), lanes] = value

            some(MAIN + at, lanes, put)
        return carry

    lax.fori_loop(0, MAIN // 16, main_rows, 0)
    lax.fori_loop(0, REST // 16, rest_rows, 0)
    used = PRODUCTS % 4 * REST
    rest_ref[PRODUCTS // 4, used:, :] = jnp.zeros((4 * REST - used, WIDTH_Z), bf16)


def plane_sums(weights_ref, theta_ref, rest_ref, rest_sum_ref, plane_ref, side):
    half = CENTERS_Y * PAD

    def leftover(index, carry):
        both = jnp.dot(weights_ref[1, side], rest_ref[index], preferred_element_type=f32)
        at = pl.multiple_of(index * half, half)
        rest_sum_ref[pl.ds(at, half), :] = both[:half] + both[half:]
        return carry

    def pair(index, carry):
        both = jnp.dot(weights_ref[0, side], theta_ref[index], preferred_element_type=f32)
        total = both[:half] + both[half:]
        for member in range(2):
            at = pl.multiple_of((index * 2 + member) * PAD, PAD)
            for center in range(CENTERS_Y):
                part = total[center * PAD : center * PAD + PAD, member * WIDTH_Z :][:, :WIDTH_Z]
                if center == CENTERS_Y - 1:
                    part = part + rest_sum_ref[pl.ds(at, PAD), :]
                lanes = slice(center * WIDTH_Z, (center + 1) * WIDTH_Z)
                high = part.astype(bf16)
                plane_ref[0, pl.ds(at, PAD), lanes] = high
                plane_ref[1, pl.ds(at, PAD), lanes] = (part - high.astype(f32)).astype(bf16)
        return carry

    lax.fori_loop(0, PRODUCTS // 4 + 1, leftover, 0, unroll=9)
    lax.fori_loop(0, PRODUCTS // 2, pair, 0, unroll=PRODUCTS // 2)


def depth_sums(plane_ref, depth_ref, table_ref, keep_low):
    size = TABLE // 2
    for start in range(0, TABLE, size):
        total = jnp.dot(
            plane_ref[0, start : start + size], depth_ref[...], preferred_element_type=f32
        )
        total = total + jnp.dot(
            plane_ref[1, start : start + size], depth_ref[...], preferred_element_type=f32
        )
        top = total.astype(bf16)
        rest = (total - top.astype(f32)).astype(bf16)
        for order in range(3):
            lanes = slice(order * TESTS, (order + 1) * TESTS)
            rows = slice(order * TABLE + start, order * TABLE + start + size)
            table_ref[rows, :TESTS] = top[:, lanes]
            if keep_low:
                table_ref[rows, TESTS:] = rest[:, lanes]


def pick_rows(code, keys_ref, pick_ref, start, count):
    spread = jnp.broadcast_to(code, (128, 128)).T
    for row in range(0, count, 16):
        for column in range(0, KEYS, 128):
            width = min(128, KEYS - column)
            same = spread[row : row + 16, :width] == keys_ref[:, column : column + width]
            pick_ref[pl.ds(start + row, 16), column : column + width] = jnp.where(
                same, 1.0, 0.0
            ).astype(bf16)


def whole_dot(left, right, contract):
    return lax.dot_general(
        left,
        right,
        (((1,), (contract,)), ((), ())),
        precision=lax.Precision.HIGHEST,
        preferred_element_type=f32,
    )


def solve(gram_ref, normal_ref, lib_ref, cross, target_squares, lib, result_ref, spot_ref):
    total = float(ROWS)
    diagonal_row = []
    diagonal_column = []
    same = lax.broadcasted_iota(jnp.int32, (128, 128), 0) == lax.broadcasted_iota(
        jnp.int32, (128, 128), 1
    )
    for block in range(4):
        at = slice(block * 128, block * 128 + 128)
        spread = jnp.where(same, gram_ref[at, at], 0.0)
        diagonal_row.append(jnp.sum(spread, axis=0, keepdims=True))
        diagonal_column.append(jnp.sum(spread, axis=1, keepdims=True))
    inverse_row = [1.0 / jnp.sqrt(d / total + EPSILON) for d in diagonal_row]
    inverse_column = [1.0 / jnp.sqrt(d / total + EPSILON) for d in diagonal_column]
    for i in range(4):
        for j in range(4):
            rows, lanes = slice(i * 128, i * 128 + 128), slice(j * 128, j * 128 + 128)
            block = gram_ref[rows, lanes] * (inverse_column[i] / total) * inverse_row[j]
            if i == j:
                block = block + jnp.where(same, RIDGE, 0.0)
            gram_ref[rows, lanes] = block
            high = block.astype(bf16)
            normal_ref[rows, lanes] = high
            normal_ref[rows, slice(TERMS + j * 128, TERMS + j * 128 + 128)] = (
                block - high.astype(f32)
            ).astype(bf16)
    inverse = jnp.concatenate(inverse_row, axis=1)
    target_scale = 1.0 / jnp.sqrt(target_squares / total + EPSILON)
    normal_cross = cross * inverse * (target_scale / total)

    def apply(rows):
        high = rows.astype(bf16)
        low = (rows - high.astype(f32)).astype(bf16)
        stacked = jnp.concatenate([high, low], axis=0)
        both = jnp.dot(stacked, normal_ref[...], preferred_element_type=f32)
        return both[:8, :TERMS] + both[:8, TERMS:] + both[8:, :TERMS]

    def fold(column):
        sums = [jnp.zeros((8, TERMS), f32) for _ in range(4)]
        for tile in range(TERMS // 8):
            rows = gram_ref[tile * 8 : tile * 8 + 8, :]
            if column is not None:
                rows = rows * column[tile]
            sums[tile % 4] = sums[tile % 4] + rows
        return jnp.sum((sums[0] + sums[1]) + (sums[2] + sums[3]), axis=0, keepdims=True)

    def spread(row):
        row = jnp.broadcast_to(row, (8, TERMS))
        return [
            jnp.sum(gram_ref[tile * 8 : tile * 8 + 8, :] * row, axis=1, keepdims=True)
            for tile in range(TERMS // 8)
        ]

    column = None
    for sweep in range(POWER // 2):
        row = fold(column)
        if sweep == 0:
            row = row * TERMS**-0.5
        column = spread(row)
    before = jnp.sum(row * row, axis=1, keepdims=True)
    after = column[0] * column[0]
    for tile in range(1, TERMS // 8):
        after = after + column[tile] * column[tile]
    after = jnp.sum(after, axis=0, keepdims=True)
    step_size = jnp.sqrt(before) / jnp.sqrt(after)
    bound = step_size * SHRINK
    coeffs = None
    for sweep in range(ITERS):
        if sweep == 0:
            moved = step_size * normal_cross
        else:
            moved = coeffs - step_size * (apply(coeffs) - normal_cross)
        coeffs = jnp.maximum(moved - bound, 0.0) - jnp.maximum(-moved - bound, 0.0)
    spot_ref[...] = coeffs
    own = pl.multiple_of(lib * 128, 128)
    result_ref[:8, :] = spot_ref[:, pl.ds(own, 128)]
    result_ref[8:, :] = whole_dot(coeffs * inverse, lib_ref[:TERMS], 0)


def kernel(
    exponents_hbm_ref,
    keys_hbm_ref,
    start_ref,
    end_ref,
    plane_weight_ref,
    depth_weight_ref,
    result_ref,
    exponents_ref,
    keys_ref,
    fields_ref,
    later_ref,
    own_fields_ref,
    own_later_ref,
    weights_ref,
    depth_ref,
    wide_ref,
    theta_ref,
    rest_ref,
    rest_sum_ref,
    plane_ref,
    table_ref,
    codes_ref,
    pick_ref,
    edge_out_ref,
    edge_in_ref,
    lib_ref,
    gram_ref,
    half_ref,
    half_in_ref,
    parts_in_ref,
    done_ref,
    normal_ref,
    spot_ref,
    local_sems,
    code_sems,
    edge_sems,
    core_sems,
    part_sems,
    done_sems,
    other_sems,
    ready_sems,
):
    sub = lax.axis_index("sub")
    lib = lax.axis_index("lib")
    chips = Chips()
    core = chips.core
    z = chips.z[0]
    edge_lib = (lib + 2 * ((z + 1) // 4)) % 4
    next_sub = {"sub": (sub + 1) % 32, "lib": edge_lib}
    last_sub = {"sub": (sub + 31) % 32, "lib": (lib + 2 * ((4 - z) // 4)) % 4}
    other_core = {"sub": sub, "lib": lib + 1 - 2 * core}
    def load(source_ref, target_ref, part, sem):
        rows = pl.ds(pl.multiple_of(jnp.maximum(part * 32 - 8, 0), 8), CELLS_Y)
        for field in range(4):
            pltpu.make_async_copy(
                source_ref.at[field, :, rows, :], target_ref.at[field], local_sems.at[sem]
            ).start()

    def loaded(target_ref, sem):
        pltpu.make_async_copy(target_ref, target_ref, local_sems.at[sem]).wait()

    load_exponents = pltpu.make_async_copy(exponents_hbm_ref, exponents_ref, local_sems.at[4])
    load_exponents.start()
    load(start_ref, fields_ref, edge_lib, 0)
    load_edge_weights = pltpu.make_async_copy(
        plane_weight_ref.at[jnp.minimum(edge_lib, 1), :, 1], weights_ref.at[:, 1], local_sems.at[2]
    )
    load_own_weights = pltpu.make_async_copy(
        plane_weight_ref.at[jnp.minimum(lib, 1), :, 0], weights_ref.at[:, 0], local_sems.at[8]
    )
    load_depth = pltpu.make_async_copy(depth_weight_ref, depth_ref, local_sems.at[3])
    load_keys = pltpu.make_async_copy(keys_hbm_ref, keys_ref, local_sems.at[5])

    barrier = pltpu.get_barrier_semaphore()

    near = [chips.device(d) for d in (1, 2, 3, 4, 8, 12, 16, 32, 48)]
    near += [{"sub": sub, "lib": (lib + step) % 4} for step in (1, 2, 3)]
    sends = sub < 31
    receives = sub > 0

    @pl.when(receives)
    def _():
        pl.semaphore_signal(barrier, inc=1, device_id=last_sub, device_id_type=MESH)

    for device in near:
        pl.semaphore_signal(barrier, inc=1, device_id=device, device_id_type=MESH)
    load(end_ref, later_ref, edge_lib, 1)
    load_edge_weights.start()
    load_depth.start()
    load_keys.start()
    load(start_ref, own_fields_ref, lib, 6)
    load(end_ref, own_later_ref, lib, 7)
    load_own_weights.start()
    load_exponents.wait()
    code = jnp.zeros((1, 128), f32)
    for place in range(7):
        code = code * 3.0 + exponents_ref[place : place + 1, :].astype(f32)
    codes_ref[lib] = jnp.broadcast_to(code, (8, 128))
    lane = lax.broadcasted_iota(jnp.int32, (8, 128), 1)
    codes_ref[4] = jnp.where(lane < 4, TARGET_CODE + lane, -1).astype(f32)

    loaded(fields_ref, 0)
    widen(fields_ref, wide_ref, 0)
    products(wide_ref, theta_ref, rest_ref, False)
    loaded(later_ref, 1)
    widen(later_ref, wide_ref, 4)
    products(wide_ref, theta_ref, rest_ref, True)
    pl.semaphore_wait(barrier, len(near) + jnp.minimum(31 - sub, 1))
    for device in near[6:9]:
        pl.semaphore_signal(ready_sems.at[0], inc=1, device_id=device, device_id_type=MESH)
    code_copies = [
        pltpu.make_async_remote_copy(
            src_ref=codes_ref.at[lib],
            dst_ref=codes_ref.at[lib],
            send_sem=code_sems.at[step],
            recv_sem=code_sems.at[3 + step],
            device_id={"sub": sub, "lib": (lib + 1 + step) % 4},
            device_id_type=MESH,
        )
        for step in range(3)
    ]
    for copy in code_copies:
        copy.start()
    load_edge_weights.wait()
    plane_sums(weights_ref, theta_ref, rest_ref, rest_sum_ref, plane_ref, 1)
    pl.semaphore_wait(ready_sems.at[0], 3)
    for device in near[3:6]:
        pl.semaphore_signal(ready_sems.at[1], inc=1, device_id=device, device_id_type=MESH)
    load_depth.wait()
    load_keys.wait()
    depth_sums(plane_ref, depth_ref, table_ref, False)
    edges = []

    def send_edge(number, code_row, start, count):
        rows = pl.ds(start, count)
        pick_rows(code_row, keys_ref, pick_ref, start, count)
        edge_out_ref[rows, :] = jnp.dot(
            pick_ref[rows, :], table_ref[:, :TESTS], preferred_element_type=f32
        ).astype(bf16)
        edge = pltpu.make_async_remote_copy(
            src_ref=edge_out_ref.at[rows],
            dst_ref=edge_in_ref.at[rows],
            send_sem=edge_sems.at[number],
            recv_sem=edge_sems.at[5 + number],
            device_id=next_sub,
            device_id_type=MESH,
        )
        edges.append(edge)

        @pl.when(sends)
        def _():
            edge.start()

    send_edge(0, code, pl.multiple_of(lib * 128, 128), 128)
    send_edge(1, codes_ref[4, :1, :], TERMS, 16)
    for step, copy in enumerate(code_copies):
        copy.wait()
        part = (lib + 3 - step) % 4
        send_edge(2 + step, codes_ref[part, :1, :], pl.multiple_of(part * 128, 128), 128)
    loaded(own_fields_ref, 6)
    widen(own_fields_ref, wide_ref, 0)
    products(wide_ref, theta_ref, rest_ref, False)
    loaded(own_later_ref, 7)
    widen(own_later_ref, wide_ref, 4)
    products(wide_ref, theta_ref, rest_ref, True)
    load_own_weights.wait()
    plane_sums(weights_ref, theta_ref, rest_ref, rest_sum_ref, plane_ref, 0)
    depth_sums(plane_ref, depth_ref, table_ref, True)
    both = jnp.dot(pick_ref[...], table_ref[...], preferred_element_type=f32)
    lib_ref[...] = both[:, :TESTS] + both[:, TESTS:]
    @pl.when(sends)
    def _():
        for edge in edges:
            edge.wait_send()

    @pl.when(receives)
    def _():
        for edge in edges:
            edge.wait_recv()
        lib_ref[...] = lib_ref[...] + edge_in_ref[...].astype(f32)

    high = lib_ref[...].astype(bf16)
    low = (lib_ref[...] - high.astype(f32)).astype(bf16)
    product = lax.dot_general(
        jnp.concatenate([high, low, high], axis=1),
        jnp.concatenate([high[:TERMS], high[:TERMS], low[:TERMS]], axis=1),
        (((1,), (1,)), ((), ())),
        preferred_element_type=f32,
    )
    cross = product[TERMS : TERMS + 8]
    target = lib_ref[TERMS : TERMS + 8]
    squares = jnp.sum(target * target, axis=1, keepdims=True)
    pairs = []
    for group in range(2):
        first = group * CHIPS // 2
        for half in range(2):
            for number in range(group * 2, group * 2 + 2):
                i, j = BLOCKS[half][number]
                lanes = slice(j * 128, j * 128 + 128)
                for part in range(16):
                    row = i * 128 + part * 8
                    half_ref[half, number * 16 + part, :8, :] = product[row : row + 8, lanes]
            i, j = BLOCKS[half][4]
            for part in range(first, first + CHIPS // 2):
                row = i * 128 + part * 2
                half_ref[half, part, 8:, :] = product[row : row + 2, j * 128 : j * 128 + 128]
        if group == 0:
            for piece in range(8):
                half_ref[0, 8 + piece // 2, piece % 2 * 4 : piece % 2 * 4 + 4, :64] = cross[
                    :4, piece * 64 : piece * 64 + 64
                ]
            half_ref[0, 12, :4, :64] = jnp.broadcast_to(squares[:4], (4, 64))
        chunks = pl.ds(first, CHIPS // 2)
        pair = pltpu.make_async_remote_copy(
            src_ref=half_ref.at[1 - core, chunks],
            dst_ref=half_in_ref.at[chunks],
            send_sem=core_sems.at[group],
            recv_sem=core_sems.at[2 + group],
            device_id=other_core,
            device_id_type=MESH,
        )
        pair.start()
        pairs.append(pair)
    for pair in pairs:
        pair.wait()
    half_in_ref[...] = half_in_ref[...] + half_ref[core]
    pl.semaphore_wait(ready_sems.at[1], 3)
    own = chips.chip(0)
    for d in PARTNERS:
        pltpu.make_async_remote_copy(
            src_ref=half_in_ref.at[chips.chip(d)],
            dst_ref=parts_in_ref.at[d],
            send_sem=part_sems.at[0],
            recv_sem=part_sems.at[1],
            device_id=chips.device(d),
            device_id_type=MESH,
        ).start()
    parts_in_ref[0] = half_in_ref[own]
    received = parts_in_ref.at[pl.ds(1, CHIPS - 1)]
    pltpu.make_async_copy(received, received, part_sems.at[1]).wait()
    done_ref[core, own] = jnp.sum(parts_in_ref[...], axis=0)
    for d in PARTNERS:
        pltpu.make_async_remote_copy(
            src_ref=done_ref.at[core, own],
            dst_ref=done_ref.at[core, own],
            send_sem=done_sems.at[0],
            recv_sem=done_sems.at[1],
            device_id=chips.device(d),
            device_id_type=MESH,
        ).start()
    pltpu.make_async_copy(received, received, part_sems.at[0]).wait()
    pltpu.make_async_copy(received, received, done_sems.at[1]).wait()
    pltpu.make_async_copy(received, received, done_sems.at[0]).wait()
    swap = pltpu.make_async_remote_copy(
        src_ref=done_ref.at[core],
        dst_ref=done_ref.at[core],
        send_sem=other_sems.at[0],
        recv_sem=other_sems.at[1],
        device_id=other_core,
        device_id_type=MESH,
    )
    swap.start()
    swap.wait()
    for half in range(2):
        for number, (i, j) in enumerate(BLOCKS[half][:4]):
            lanes = slice(j * 128, j * 128 + 128)
            for part in range(16):
                row = i * 128 + part * 8
                gram_ref[row : row + 8, lanes] = done_ref[half, number * 16 + part, :8, :]
        i, j = BLOCKS[half][4]
        for part in range(CHIPS):
            row = i * 128 + part * 2
            gram_ref[row : row + 2, j * 128 : j * 128 + 128] = done_ref[half, part, 8:, :]
    cross_sum = jnp.concatenate(
        [
            jnp.concatenate(
                [gram_ref[64 + piece * 4 : 68 + piece * 4, :64] for piece in range(8)], axis=1
            ),
            jnp.zeros((4, TERMS), f32),
        ],
        axis=0,
    )
    square_sum = jnp.concatenate([gram_ref[96:100, :1], jnp.zeros((4, 1), f32)], axis=0)
    gram_ref[64:128, :64] = gram_ref[:64, 64:128].T
    for i in range(4):
        for j in range(i):
            gram_ref[i * 128 : i * 128 + 128, j * 128 : j * 128 + 128] = gram_ref[
                j * 128 : j * 128 + 128, i * 128 : i * 128 + 128
            ].T
    solve(
        gram_ref, normal_ref, lib_ref, cross_sum, square_sum, lib, result_ref, spot_ref
    )


def local(snap_start, snap_end, exponents):
    vmem = pl.BlockSpec(memory_space=pltpu.VMEM)
    anywhere = pl.BlockSpec(memory_space=pl.ANY)
    result = pl.pallas_call(
        kernel,
        out_shape=jax.ShapeDtypeStruct((16, TESTS), f32),
        in_specs=[anywhere] * 6,
        out_specs=vmem,
        scratch_shapes=[
            pltpu.VMEM((7, 128), jnp.int32),
            pltpu.VMEM((1, KEYS), f32),
            pltpu.VMEM((4, CELLS_X, CELLS_Y, WIDTH_Z), bf16),
            pltpu.VMEM((4, CELLS_X, CELLS_Y, WIDTH_Z), bf16),
            pltpu.VMEM((4, CELLS_X, CELLS_Y, WIDTH_Z), bf16),
            pltpu.VMEM((4, CELLS_X, CELLS_Y, WIDTH_Z), bf16),
            pltpu.VMEM((2, 2, 2 * CENTERS_Y * PAD, MAIN), bf16),
            pltpu.VMEM((CENTERS_Y * WIDTH_Z, 3 * TESTS), bf16),
            pltpu.VMEM((8, CELLS_XY, WIDTH_Z), f32),
            pltpu.VMEM((PRODUCTS // 2, MAIN, 2 * WIDTH_Z), bf16),
            pltpu.VMEM((PRODUCTS // 4 + 1, 4 * REST, WIDTH_Z), bf16),
            pltpu.VMEM(((PRODUCTS // 4 + 1) * 4 * PAD, WIDTH_Z), f32),
            pltpu.VMEM((2, TABLE, CENTERS_Y * WIDTH_Z), bf16),
            pltpu.VMEM((KEYS, 2 * TESTS), bf16),
            pltpu.VMEM((5, 8, 128), f32),
            pltpu.VMEM((PICKED, KEYS), bf16),
            pltpu.VMEM((PICKED, TESTS), bf16),
            pltpu.VMEM((PICKED, TESTS), bf16),
            pltpu.VMEM((PICKED, TESTS), f32),
            pltpu.VMEM((TERMS, TERMS), f32),
            pltpu.VMEM((2, CHIPS, CHUNK, 128), f32),
            pltpu.VMEM((CHIPS, CHUNK, 128), f32),
            pltpu.VMEM((CHIPS, CHUNK, 128), f32),
            pltpu.VMEM((2, CHIPS, CHUNK, 128), f32),
            pltpu.VMEM((TERMS, 2 * TERMS), bf16),
            pltpu.VMEM((8, TERMS), f32),
            pltpu.SemaphoreType.DMA((9,)),
            pltpu.SemaphoreType.DMA((6,)),
            pltpu.SemaphoreType.DMA((10,)),
            pltpu.SemaphoreType.DMA((4,)),
            pltpu.SemaphoreType.DMA((2,)),
            pltpu.SemaphoreType.DMA((2,)),
            pltpu.SemaphoreType.DMA((2,)),
            pltpu.SemaphoreType.REGULAR((2,)),
        ],
        compiler_params=pltpu.CompilerParams(
            collective_id=0, has_side_effects=True, vmem_limit_bytes=56 << 20
        ),
        name="weak_form_fit",
    )(
        exponents.T,
        jnp.asarray(column_codes()),
        snap_start,
        snap_end,
        jnp.asarray(plane_weights()),
        jnp.asarray(depth_weights()),
    )
    return result[:4], result[8:12]


def solution(mesh):
    placed = (P(None, "sub", None, None), P(None, "sub", None, None), P("lib", None))
    return jax.shard_map(
        local,
        mesh=mesh,
        in_specs=placed,
        out_specs=(P(None, "lib"), P(None, ("sub", "lib"))),
        check_vma=False,
    )
```

```python
import functools

import jax
import jax.numpy as jnp
import ml_dtypes
import numpy as np
from jax import lax
from jax.experimental import pallas as pl
from jax.experimental.pallas import tpu as pltpu
from jax.sharding import PartitionSpec as P

STRIDE = 8
RADIUS = 8
POWER = 6
ITERS = 10
TERMS = 512
ROWS = 16384
RIDGE = 0.1
SHRINK = 0.05
EPSILON = 1e-06

CELLS_X = 8
CELLS_Y = 40
CELLS_XY = CELLS_X * CELLS_Y
MAIN_Y = 32
MAIN = CELLS_X * MAIN_Y
REST = CELLS_XY - MAIN
WIDTH_Z = 256
CENTERS_Y = 4
CENTERS_Z = 32
TESTS = CENTERS_Y * CENTERS_Z

POWERS = [
    (a, b, c, e)
    for a in range(3)
    for b in range(3)
    for c in range(3)
    for e in range(3)
    if 1 <= a + b + c + e <= 3
]
PRODUCTS = len(POWERS) + 4
PAD = 16
TABLE = PRODUCTS * PAD
KEYS = 3 * TABLE
PICKED = TERMS + 16
TARGET_CODE = 4000

CHUNK = 10
CHIPS = 64
BLOCKS = (
    ((0, 0), (0, 1), (0, 2), (0, 3), (3, 3)),
    ((1, 1), (1, 2), (1, 3), (2, 2), (2, 3)),
)
HOPS = (0, 1, 2, 1)
PARTNERS = sorted(
    range(1, CHIPS), key=lambda d: -(HOPS[d // 16] + HOPS[d // 4 % 4] + HOPS[d % 4])
)

MESH = pl.DeviceIdType.MESH
f32 = jnp.float32
bf16 = jnp.bfloat16


def tap(order, offset):
    s = np.asarray(offset, np.float64) / RADIUS
    base = 1.0 - s * s
    value = (base**3, 6.0 * s * base**2, -6.0 * base * (1.0 - 5.0 * s * s))[order]
    return np.where(np.abs(s) <= 1.0, value, 0.0)


def split_pieces(values):
    high = values.astype(ml_dtypes.bfloat16)
    low = (values - high.astype(np.float64)).astype(ml_dtypes.bfloat16)
    return high, low


def plane_weights():
    x = np.arange(CELLS_X)[:, None]
    y = np.arange(CELLS_Y)[None, :]
    both = []
    for shift in (0, STRIDE):
        full = np.zeros((2, CENTERS_Y, PAD, CELLS_X, CELLS_Y))
        for side in range(2):
            for center in range(CENTERS_Y):
                for order_x in range(3):
                    for order_y in range(3):
                        full[side, center, order_x * 3 + order_y] = tap(
                            order_x, x - STRIDE * side
                        ) * tap(order_y, y - STRIDE * center - shift)
        wide = full[..., :MAIN_Y].reshape(2, CENTERS_Y * PAD, MAIN)
        edge = full[:, CENTERS_Y - 1, :, :, MAIN_Y:].reshape(2, PAD, REST)
        apart = np.zeros((2, 4, PAD, 4, REST))
        for member in range(4):
            apart[:, member, :, member, :] = edge
        groups = (wide, apart.reshape(2, 4 * PAD, 4 * REST))
        both.append(np.stack([np.concatenate(split_pieces(g), axis=1) for g in groups]))
    return np.stack(both)


def depth_weights():
    z = np.arange(WIDTH_Z)[:, None]
    centers = STRIDE * np.arange(CENTERS_Z)[None, :]
    full = np.zeros((CENTERS_Y, WIDTH_Z, 3, CENTERS_Y, CENTERS_Z))
    for order in range(3):
        for center in range(CENTERS_Y):
            full[center, :, order, center, :] = tap(order, z - centers)
    return full.reshape(CENTERS_Y * WIDTH_Z, 3 * TESTS).astype(ml_dtypes.bfloat16)


def column_codes():
    codes = np.full((3, PRODUCTS, PAD), -2.0, np.float32)
    for index, (a, b, c, e) in enumerate(POWERS):
        for order_z in range(3):
            for plane in range(9):
                codes[order_z, index, plane] = (
                    (((a * 3 + b) * 3 + c) * 3 + e) * 27 + plane * 3 + order_z
                )
    for field in range(4):
        codes[0, len(POWERS) + field, 0] = TARGET_CODE + field
    return codes.reshape(1, KEYS)


def others(value):
    return value, value + 1 - 2 * (value % 2), (value + 2) % 4, 3 - value


class Chips:
    def __init__(self):
        sub = lax.axis_index("sub")
        lib = lax.axis_index("lib")
        self.core = lib % 2
        self.x = others(sub // 8)
        self.y = others((sub // 4) % 2 * 2 + lib // 2)
        self.z = others(sub % 4)
        self.sub_x = [8 * v for v in self.x]
        self.sub_y = [v // 2 * 4 for v in self.y]
        self.lib_y = [v % 2 * 2 + self.core for v in self.y]
        self.chip_xy = [[16 * v + 4 * w for w in self.y] for v in self.x]

    def chip(self, d):
        return self.chip_xy[d // 16][d // 4 % 4] + self.z[d % 4]

    def device(self, d):
        return {
            "sub": self.sub_x[d // 16] + self.sub_y[d // 4 % 4] + self.z[d % 4],
            "lib": self.lib_y[d // 4 % 4],
        }


def widen(source_ref, wide_ref, base):
    for field in range(4):
        for x in range(CELLS_X):
            plane = source_ref[field, x].astype(f32)
            wide_ref[base + field, x * MAIN_Y : x * MAIN_Y + MAIN_Y, :] = plane[:MAIN_Y]
            wide_ref[base + field, MAIN + x * 8 : MAIN + x * 8 + 8, :] = plane[MAIN_Y:]


def products(wide_ref, theta_ref, rest_ref, changes):

    def some(at, lanes, put):
        value = [wide_ref[field, pl.ds(at, 16), lanes] for field in range(4)]
        if changes:
            for field in range(4):
                change = wide_ref[4 + field, pl.ds(at, 16), lanes] - value[field]
                put(len(POWERS) + field, change.astype(bf16))
            return
        square = [v * v for v in value]
        pairs = {}
        for index, powers in enumerate(POWERS):
            result = None
            key = ()
            for field, power in enumerate(powers):
                if power == 0:
                    continue
                factor = value[field] if power == 1 else square[field]
                key = key + ((field, power),)
                if result is None:
                    result = factor
                elif key in pairs:
                    result = pairs[key]
                else:
                    result = result * factor
                    pairs[key] = result
            put(index, result.astype(bf16))

    def main_rows(step, carry):
        at = pl.multiple_of(step * 16, 16)
        for half in range(2):

            def put(index, value, half=half):
                lane = index % 2 * WIDTH_Z + half * 128
                theta_ref[index // 2, pl.ds(at, 16), lane : lane + 128] = value

            some(at, slice(half * 128, half * 128 + 128), put)
        return carry

    def rest_rows(step, carry):
        at = pl.multiple_of(step * 16, 16)
        for half in range(2):
            lanes = slice(half * 128, half * 128 + 128)

            def put(index, value, lanes=lanes):
                rest_ref[index // 4, pl.ds(index % 4 * REST + at, 16), lanes] = value

            some(MAIN + at, lanes, put)
        return carry

    lax.fori_loop(0, MAIN // 16, main_rows, 0)
    lax.fori_loop(0, REST // 16, rest_rows, 0)
    used = PRODUCTS % 4 * REST
    rest_ref[PRODUCTS // 4, used:, :] = jnp.zeros((4 * REST - used, WIDTH_Z), bf16)


def plane_sums(weights_ref, theta_ref, rest_ref, rest_sum_ref, plane_ref, side):
    half = CENTERS_Y * PAD

    def leftover(index, carry):
        both = jnp.dot(weights_ref[1, side], rest_ref[index], preferred_element_type=f32)
        at = pl.multiple_of(index * half, half)
        rest_sum_ref[pl.ds(at, half), :] = both[:half] + both[half:]
        return carry

    def pair(index, carry):
        both = jnp.dot(weights_ref[0, side], theta_ref[index], preferred_element_type=f32)
        total = both[:half] + both[half:]
        for member in range(2):
            at = pl.multiple_of((index * 2 + member) * PAD, PAD)
            for center in range(CENTERS_Y):
                part = total[center * PAD : center * PAD + PAD, member * WIDTH_Z :][:, :WIDTH_Z]
                if center == CENTERS_Y - 1:
                    part = part + rest_sum_ref[pl.ds(at, PAD), :]
                lanes = slice(center * WIDTH_Z, (center + 1) * WIDTH_Z)
                high = part.astype(bf16)
                plane_ref[0, pl.ds(at, PAD), lanes] = high
                plane_ref[1, pl.ds(at, PAD), lanes] = (part - high.astype(f32)).astype(bf16)
        return carry

    lax.fori_loop(0, PRODUCTS // 4 + 1, leftover, 0, unroll=9)
    lax.fori_loop(0, PRODUCTS // 2, pair, 0, unroll=PRODUCTS // 2)


def depth_sums(plane_ref, depth_ref, table_ref, keep_low):
    size = TABLE // 2
    for start in range(0, TABLE, size):
        total = jnp.dot(
            plane_ref[0, start : start + size], depth_ref[...], preferred_element_type=f32
        )
        total = total + jnp.dot(
            plane_ref[1, start : start + size], depth_ref[...], preferred_element_type=f32
        )
        top = total.astype(bf16)
        rest = (total - top.astype(f32)).astype(bf16)
        for order in range(3):
            lanes = slice(order * TESTS, (order + 1) * TESTS)
            rows = slice(order * TABLE + start, order * TABLE + start + size)
            table_ref[rows, :TESTS] = top[:, lanes]
            if keep_low:
                table_ref[rows, TESTS:] = rest[:, lanes]


def pick_rows(code, keys_ref, pick_ref, start, count):
    spread = jnp.broadcast_to(code, (128, 128)).T
    for row in range(0, count, 16):
        for column in range(0, KEYS, 128):
            width = min(128, KEYS - column)
            same = spread[row : row + 16, :width] == keys_ref[:, column : column + width]
            pick_ref[pl.ds(start + row, 16), column : column + width] = jnp.where(
                same, 1.0, 0.0
            ).astype(bf16)


def whole_dot(left, right, contract):
    return lax.dot_general(
        left,
        right,
        (((1,), (contract,)), ((), ())),
        precision=lax.Precision.HIGHEST,
        preferred_element_type=f32,
    )


def solve(gram_ref, normal_ref, lib_ref, cross, target_squares, lib, result_ref, spot_ref):
    total = float(ROWS)
    diagonal_row = []
    diagonal_column = []
    same = lax.broadcasted_iota(jnp.int32, (128, 128), 0) == lax.broadcasted_iota(
        jnp.int32, (128, 128), 1
    )
    for block in range(4):
        at = slice(block * 128, block * 128 + 128)
        spread = jnp.where(same, gram_ref[at, at], 0.0)
        diagonal_row.append(jnp.sum(spread, axis=0, keepdims=True))
        diagonal_column.append(jnp.sum(spread, axis=1, keepdims=True))
    inverse_row = [1.0 / jnp.sqrt(d / total + EPSILON) for d in diagonal_row]
    inverse_column = [1.0 / jnp.sqrt(d / total + EPSILON) for d in diagonal_column]
    for i in range(4):
        for j in range(4):
            rows, lanes = slice(i * 128, i * 128 + 128), slice(j * 128, j * 128 + 128)
            block = gram_ref[rows, lanes] * (inverse_column[i] / total) * inverse_row[j]
            if i == j:
                block = block + jnp.where(same, RIDGE, 0.0)
            gram_ref[rows, lanes] = block
            high = block.astype(bf16)
            normal_ref[rows, lanes] = high
            normal_ref[rows, slice(TERMS + j * 128, TERMS + j * 128 + 128)] = (
                block - high.astype(f32)
            ).astype(bf16)
    inverse = jnp.concatenate(inverse_row, axis=1)
    target_scale = 1.0 / jnp.sqrt(target_squares / total + EPSILON)
    normal_cross = cross * inverse * (target_scale / total)

    def apply(rows):
        high = rows.astype(bf16)
        low = (rows - high.astype(f32)).astype(bf16)
        stacked = jnp.concatenate([high, low], axis=0)
        first = jnp.dot(stacked, normal_ref[:, :TERMS], preferred_element_type=f32)
        second = jnp.dot(high, normal_ref[:, TERMS:], preferred_element_type=f32)
        return first[:8] + first[8:] + second

    def fold(column):
        sums = [jnp.zeros((8, TERMS), f32) for _ in range(4)]
        for tile in range(TERMS // 8):
            rows = gram_ref[tile * 8 : tile * 8 + 8, :]
            if column is not None:
                rows = rows * column[tile]
            sums[tile % 4] = sums[tile % 4] + rows
        return jnp.sum((sums[0] + sums[1]) + (sums[2] + sums[3]), axis=0, keepdims=True)

    def spread(row):
        row = jnp.broadcast_to(row, (8, TERMS))
        return [
            jnp.sum(gram_ref[tile * 8 : tile * 8 + 8, :] * row, axis=1, keepdims=True)
            for tile in range(TERMS // 8)
        ]

    column = None
    for sweep in range(POWER // 2):
        row = fold(column)
        if sweep == 0:
            row = row * TERMS**-0.5
        column = spread(row)
    before = jnp.sum(row * row, axis=1, keepdims=True)
    after = column[0] * column[0]
    for tile in range(1, TERMS // 8):
        after = after + column[tile] * column[tile]
    after = jnp.sum(after, axis=0, keepdims=True)
    step_size = jnp.sqrt(before) / jnp.sqrt(after)
    bound = step_size * SHRINK
    coeffs = None
    for sweep in range(ITERS):
        if sweep == 0:
            moved = step_size * normal_cross
        else:
            moved = coeffs - step_size * (apply(coeffs) - normal_cross)
        coeffs = jnp.maximum(moved - bound, 0.0) - jnp.maximum(-moved - bound, 0.0)
    spot_ref[...] = coeffs
    own = pl.multiple_of(lib * 128, 128)
    result_ref[:8, :] = spot_ref[:, pl.ds(own, 128)]
    result_ref[8:, :] = whole_dot(coeffs * inverse, lib_ref[:TERMS], 0)


def kernel(
    exponents_hbm_ref,
    keys_hbm_ref,
    start_ref,
    end_ref,
    plane_weight_ref,
    depth_weight_ref,
    result_ref,
    exponents_ref,
    keys_ref,
    fields_ref,
    later_ref,
    own_fields_ref,
    own_later_ref,
    weights_ref,
    depth_ref,
    wide_ref,
    theta_ref,
    rest_ref,
    rest_sum_ref,
    plane_ref,
    table_ref,
    codes_ref,
    pick_ref,
    edge_out_ref,
    edge_in_ref,
    lib_ref,
    gram_ref,
    half_ref,
    half_in_ref,
    parts_in_ref,
    done_ref,
    normal_ref,
    spot_ref,
    local_sems,
    code_sems,
    edge_sems,
    core_sems,
    part_sems,
    done_sems,
    other_sems,
    ready_sems,
):
    sub = lax.axis_index("sub")
    lib = lax.axis_index("lib")
    chips = Chips()
    core = chips.core
    z = chips.z[0]
    edge_lib = (lib + 2 * ((z + 1) // 4)) % 4
    next_sub = {"sub": (sub + 1) % 32, "lib": edge_lib}
    last_sub = {"sub": (sub + 31) % 32, "lib": (lib + 2 * ((4 - z) // 4)) % 4}
    other_core = {"sub": sub, "lib": lib + 1 - 2 * core}
    def load(source_ref, target_ref, part, sem):
        rows = pl.ds(pl.multiple_of(jnp.maximum(part * 32 - 8, 0), 8), CELLS_Y)
        for field in range(4):
            pltpu.make_async_copy(
                source_ref.at[field, :, rows, :], target_ref.at[field], local_sems.at[sem]
            ).start()

    def loaded(target_ref, sem):
        pltpu.make_async_copy(target_ref, target_ref, local_sems.at[sem]).wait()

    load_exponents = pltpu.make_async_copy(exponents_hbm_ref, exponents_ref, local_sems.at[4])
    load_exponents.start()
    load(start_ref, fields_ref, edge_lib, 0)
    load_edge_weights = pltpu.make_async_copy(
        plane_weight_ref.at[jnp.minimum(edge_lib, 1), :, 1], weights_ref.at[:, 1], local_sems.at[2]
    )
    load_own_weights = pltpu.make_async_copy(
        plane_weight_ref.at[jnp.minimum(lib, 1), :, 0], weights_ref.at[:, 0], local_sems.at[8]
    )
    load_depth = pltpu.make_async_copy(depth_weight_ref, depth_ref, local_sems.at[3])
    load_keys = pltpu.make_async_copy(keys_hbm_ref, keys_ref, local_sems.at[5])

    barrier = pltpu.get_barrier_semaphore()

    near = [chips.device(d) for d in (1, 2, 3, 4, 8, 12, 16, 32, 48)]
    near += [{"sub": sub, "lib": (lib + step) % 4} for step in (1, 2, 3)]
    sends = sub < 31
    receives = sub > 0

    @pl.when(receives)
    def _():
        pl.semaphore_signal(barrier, inc=1, device_id=last_sub, device_id_type=MESH)

    for device in near:
        pl.semaphore_signal(barrier, inc=1, device_id=device, device_id_type=MESH)
    load(end_ref, later_ref, edge_lib, 1)
    load_edge_weights.start()
    load_depth.start()
    load_keys.start()
    load(start_ref, own_fields_ref, lib, 6)
    load(end_ref, own_later_ref, lib, 7)
    load_own_weights.start()
    load_exponents.wait()
    code = jnp.zeros((1, 128), f32)
    for place in range(7):
        code = code * 3.0 + exponents_ref[place : place + 1, :].astype(f32)
    codes_ref[lib] = jnp.broadcast_to(code, (8, 128))
    lane = lax.broadcasted_iota(jnp.int32, (8, 128), 1)
    codes_ref[4] = jnp.where(lane < 4, TARGET_CODE + lane, -1).astype(f32)

    loaded(fields_ref, 0)
    widen(fields_ref, wide_ref, 0)
    products(wide_ref, theta_ref, rest_ref, False)
    loaded(later_ref, 1)
    widen(later_ref, wide_ref, 4)
    products(wide_ref, theta_ref, rest_ref, True)
    pl.semaphore_wait(barrier, len(near) + jnp.minimum(31 - sub, 1))
    for device in near[6:9]:
        pl.semaphore_signal(ready_sems.at[0], inc=1, device_id=device, device_id_type=MESH)
    code_copies = [
        pltpu.make_async_remote_copy(
            src_ref=codes_ref.at[lib],
            dst_ref=codes_ref.at[lib],
            send_sem=code_sems.at[step],
            recv_sem=code_sems.at[3 + step],
            device_id={"sub": sub, "lib": (lib + 1 + step) % 4},
            device_id_type=MESH,
        )
        for step in range(3)
    ]
    for copy in code_copies:
        copy.start()
    load_edge_weights.wait()
    plane_sums(weights_ref, theta_ref, rest_ref, rest_sum_ref, plane_ref, 1)
    pl.semaphore_wait(ready_sems.at[0], 3)
    for device in near[3:6]:
        pl.semaphore_signal(ready_sems.at[1], inc=1, device_id=device, device_id_type=MESH)
    load_depth.wait()
    load_keys.wait()
    depth_sums(plane_ref, depth_ref, table_ref, False)
    edges = []

    def send_edge(number, code_row, start, count):
        rows = pl.ds(start, count)
        pick_rows(code_row, keys_ref, pick_ref, start, count)
        edge_out_ref[rows, :] = jnp.dot(
            pick_ref[rows, :], table_ref[:, :TESTS], preferred_element_type=f32
        ).astype(bf16)
        edge = pltpu.make_async_remote_copy(
            src_ref=edge_out_ref.at[rows],
            dst_ref=edge_in_ref.at[rows],
            send_sem=edge_sems.at[number],
            recv_sem=edge_sems.at[5 + number],
            device_id=next_sub,
            device_id_type=MESH,
        )
        edges.append(edge)

        @pl.when(sends)
        def _():
            edge.start()

    send_edge(0, code, pl.multiple_of(lib * 128, 128), 128)
    send_edge(1, codes_ref[4, :1, :], TERMS, 16)
    for step, copy in enumerate(code_copies):
        copy.wait_recv()
        part = (lib + 3 - step) % 4
        send_edge(2 + step, codes_ref[part, :1, :], pl.multiple_of(part * 128, 128), 128)
    loaded(own_fields_ref, 6)
    widen(own_fields_ref, wide_ref, 0)
    products(wide_ref, theta_ref, rest_ref, False)
    loaded(own_later_ref, 7)
    widen(own_later_ref, wide_ref, 4)
    products(wide_ref, theta_ref, rest_ref, True)
    load_own_weights.wait()
    plane_sums(weights_ref, theta_ref, rest_ref, rest_sum_ref, plane_ref, 0)
    depth_sums(plane_ref, depth_ref, table_ref, True)
    both = jnp.dot(pick_ref[...], table_ref[...], preferred_element_type=f32)
    lib_ref[...] = both[:, :TESTS] + both[:, TESTS:]
    @pl.when(receives)
    def _():
        for edge in edges:
            edge.wait_recv()
        lib_ref[...] = lib_ref[...] + edge_in_ref[...].astype(f32)

    high = lib_ref[...].astype(bf16)
    low = (lib_ref[...] - high.astype(f32)).astype(bf16)
    product = lax.dot_general(
        jnp.concatenate([high, low, high], axis=1),
        jnp.concatenate([high[:TERMS], high[:TERMS], low[:TERMS]], axis=1),
        (((1,), (1,)), ((), ())),
        preferred_element_type=f32,
    )
    cross = product[TERMS : TERMS + 8]
    target = lib_ref[TERMS : TERMS + 8]
    squares = jnp.sum(target * target, axis=1, keepdims=True)
    pairs = []
    for group in range(2):
        first = group * CHIPS // 2
        for half in range(2):
            for number in range(group * 2, group * 2 + 2):
                i, j = BLOCKS[half][number]
                lanes = slice(j * 128, j * 128 + 128)
                for part in range(16):
                    row = i * 128 + part * 8
                    half_ref[half, number * 16 + part, :8, :] = product[row : row + 8, lanes]
            i, j = BLOCKS[half][4]
            for part in range(first, first + CHIPS // 2):
                row = i * 128 + part * 2
                half_ref[half, part, 8:, :] = product[row : row + 2, j * 128 : j * 128 + 128]
        if group == 0:
            for piece in range(8):
                half_ref[0, 8 + piece // 2, piece % 2 * 4 : piece % 2 * 4 + 4, :64] = cross[
                    :4, piece * 64 : piece * 64 + 64
                ]
            half_ref[0, 12, :4, :64] = jnp.broadcast_to(squares[:4], (4, 64))
        chunks = pl.ds(first, CHIPS // 2)
        pair = pltpu.make_async_remote_copy(
            src_ref=half_ref.at[1 - core, chunks],
            dst_ref=half_in_ref.at[chunks],
            send_sem=core_sems.at[group],
            recv_sem=core_sems.at[2 + group],
            device_id=other_core,
            device_id_type=MESH,
        )
        pair.start()
        pairs.append(pair)
    for pair in pairs:
        pair.wait_recv()
    half_in_ref[...] = half_in_ref[...] + half_ref[core]
    pl.semaphore_wait(ready_sems.at[1], 3)
    own = chips.chip(0)
    for d in PARTNERS:
        pltpu.make_async_remote_copy(
            src_ref=half_in_ref.at[chips.chip(d)],
            dst_ref=parts_in_ref.at[d],
            send_sem=part_sems.at[0],
            recv_sem=part_sems.at[1],
            device_id=chips.device(d),
            device_id_type=MESH,
        ).start()
    parts_in_ref[0] = half_in_ref[own]
    received = parts_in_ref.at[pl.ds(1, CHIPS - 1)]
    pltpu.make_async_copy(received, received, part_sems.at[1]).wait()
    done_ref[core, own] = jnp.sum(parts_in_ref[...], axis=0)
    for d in PARTNERS:
        pltpu.make_async_remote_copy(
            src_ref=done_ref.at[core, own],
            dst_ref=done_ref.at[core, own],
            send_sem=done_sems.at[0],
            recv_sem=done_sems.at[1],
            device_id=chips.device(d),
            device_id_type=MESH,
        ).start()
    pltpu.make_async_copy(received, received, done_sems.at[1]).wait()
    swap = pltpu.make_async_remote_copy(
        src_ref=done_ref.at[core],
        dst_ref=done_ref.at[core],
        send_sem=other_sems.at[0],
        recv_sem=other_sems.at[1],
        device_id=other_core,
        device_id_type=MESH,
    )
    swap.start()
    swap.wait_recv()
    for half in range(2):
        for number, (i, j) in enumerate(BLOCKS[half][:4]):
            lanes = slice(j * 128, j * 128 + 128)
            for part in range(16):
                row = i * 128 + part * 8
                gram_ref[row : row + 8, lanes] = done_ref[half, number * 16 + part, :8, :]
        i, j = BLOCKS[half][4]
        for part in range(CHIPS):
            row = i * 128 + part * 2
            gram_ref[row : row + 2, j * 128 : j * 128 + 128] = done_ref[half, part, 8:, :]
    cross_sum = jnp.concatenate(
        [
            jnp.concatenate(
                [gram_ref[64 + piece * 4 : 68 + piece * 4, :64] for piece in range(8)], axis=1
            ),
            jnp.zeros((4, TERMS), f32),
        ],
        axis=0,
    )
    square_sum = jnp.concatenate([gram_ref[96:100, :1], jnp.zeros((4, 1), f32)], axis=0)
    gram_ref[64:128, :64] = gram_ref[:64, 64:128].T
    for i in range(4):
        for j in range(i):
            gram_ref[i * 128 : i * 128 + 128, j * 128 : j * 128 + 128] = gram_ref[
                j * 128 : j * 128 + 128, i * 128 : i * 128 + 128
            ].T
    solve(
        gram_ref, normal_ref, lib_ref, cross_sum, square_sum, lib, result_ref, spot_ref
    )
    for copy in code_copies:
        copy.wait_send()
    for pair in pairs:
        pair.wait_send()
    pltpu.make_async_copy(received, received, part_sems.at[0]).wait()
    pltpu.make_async_copy(received, received, done_sems.at[0]).wait()
    swap.wait_send()

    @pl.when(sends)
    def _():
        for edge in edges:
            edge.wait_send()


def local(snap_start, snap_end, exponents):
    vmem = pl.BlockSpec(memory_space=pltpu.VMEM)
    anywhere = pl.BlockSpec(memory_space=pl.ANY)
    result = pl.pallas_call(
        kernel,
        out_shape=jax.ShapeDtypeStruct((16, TESTS), f32),
        in_specs=[anywhere] * 6,
        out_specs=vmem,
        scratch_shapes=[
            pltpu.VMEM((7, 128), jnp.int32),
            pltpu.VMEM((1, KEYS), f32),
            pltpu.VMEM((4, CELLS_X, CELLS_Y, WIDTH_Z), bf16),
            pltpu.VMEM((4, CELLS_X, CELLS_Y, WIDTH_Z), bf16),
            pltpu.VMEM((4, CELLS_X, CELLS_Y, WIDTH_Z), bf16),
            pltpu.VMEM((4, CELLS_X, CELLS_Y, WIDTH_Z), bf16),
            pltpu.VMEM((2, 2, 2 * CENTERS_Y * PAD, MAIN), bf16),
            pltpu.VMEM((CENTERS_Y * WIDTH_Z, 3 * TESTS), bf16),
            pltpu.VMEM((8, CELLS_XY, WIDTH_Z), f32),
            pltpu.VMEM((PRODUCTS // 2, MAIN, 2 * WIDTH_Z), bf16),
            pltpu.VMEM((PRODUCTS // 4 + 1, 4 * REST, WIDTH_Z), bf16),
            pltpu.VMEM(((PRODUCTS // 4 + 1) * 4 * PAD, WIDTH_Z), f32),
            pltpu.VMEM((2, TABLE, CENTERS_Y * WIDTH_Z), bf16),
            pltpu.VMEM((KEYS, 2 * TESTS), bf16),
            pltpu.VMEM((5, 8, 128), f32),
            pltpu.VMEM((PICKED, KEYS), bf16),
            pltpu.VMEM((PICKED, TESTS), bf16),
            pltpu.VMEM((PICKED, TESTS), bf16),
            pltpu.VMEM((PICKED, TESTS), f32),
            pltpu.VMEM((TERMS, TERMS), f32),
            pltpu.VMEM((2, CHIPS, CHUNK, 128), f32),
            pltpu.VMEM((CHIPS, CHUNK, 128), f32),
            pltpu.VMEM((CHIPS, CHUNK, 128), f32),
            pltpu.VMEM((2, CHIPS, CHUNK, 128), f32),
            pltpu.VMEM((TERMS, 2 * TERMS), bf16),
            pltpu.VMEM((8, TERMS), f32),
            pltpu.SemaphoreType.DMA((9,)),
            pltpu.SemaphoreType.DMA((6,)),
            pltpu.SemaphoreType.DMA((10,)),
            pltpu.SemaphoreType.DMA((4,)),
            pltpu.SemaphoreType.DMA((2,)),
            pltpu.SemaphoreType.DMA((2,)),
            pltpu.SemaphoreType.DMA((2,)),
            pltpu.SemaphoreType.REGULAR((2,)),
        ],
        compiler_params=pltpu.CompilerParams(
            collective_id=0, has_side_effects=True, vmem_limit_bytes=56 << 20
        ),
        name="weak_form_fit",
    )(
        exponents.T,
        jnp.asarray(column_codes()),
        snap_start,
        snap_end,
        jnp.asarray(plane_weights()),
        jnp.asarray(depth_weights()),
    )
    return result[:4], result[8:12]


def solution(mesh):
    placed = (P(None, "sub", None, None), P(None, "sub", None, None), P("lib", None))
    return jax.shard_map(
        local,
        mesh=mesh,
        in_specs=placed,
        out_specs=(P(None, "lib"), P(None, ("sub", "lib"))),
        check_vma=False,
    )
```

```python
import functools

import jax
import jax.numpy as jnp
import ml_dtypes
import numpy as np
from jax import lax
from jax.experimental import pallas as pl
from jax.experimental.pallas import tpu as pltpu
from jax.sharding import PartitionSpec as P

STRIDE = 8
RADIUS = 8
POWER = 6
ITERS = 10
TERMS = 512
ROWS = 16384
RIDGE = 0.1
SHRINK = 0.05
EPSILON = 1e-06

CELLS_X = 8
CELLS_Y = 40
CELLS_XY = CELLS_X * CELLS_Y
MAIN_Y = 32
MAIN = CELLS_X * MAIN_Y
REST = CELLS_XY - MAIN
WIDTH_Z = 256
CENTERS_Y = 4
CENTERS_Z = 32
TESTS = CENTERS_Y * CENTERS_Z

POWERS = [
    (a, b, c, e)
    for a in range(3)
    for b in range(3)
    for c in range(3)
    for e in range(3)
    if 1 <= a + b + c + e <= 3
]
PRODUCTS = len(POWERS) + 4
PAD = 16
TABLE = PRODUCTS * PAD
KEYS = 3 * TABLE
PICKED = TERMS + 16
TARGET_CODE = 4000

CHUNK = 10
CHIPS = 64
BLOCKS = (
    ((0, 0), (0, 1), (0, 2), (0, 3), (3, 3)),
    ((1, 1), (1, 2), (1, 3), (2, 2), (2, 3)),
)
HOPS = (0, 1, 2, 1)
PARTNERS = sorted(
    range(1, CHIPS), key=lambda d: -(HOPS[d // 16] + HOPS[d // 4 % 4] + HOPS[d % 4])
)

MESH = pl.DeviceIdType.MESH
f32 = jnp.float32
bf16 = jnp.bfloat16


def tap(order, offset):
    s = np.asarray(offset, np.float64) / RADIUS
    base = 1.0 - s * s
    value = (base**3, 6.0 * s * base**2, -6.0 * base * (1.0 - 5.0 * s * s))[order]
    return np.where(np.abs(s) <= 1.0, value, 0.0)


def split_pieces(values):
    high = values.astype(ml_dtypes.bfloat16)
    low = (values - high.astype(np.float64)).astype(ml_dtypes.bfloat16)
    return high, low


def plane_weights():
    x = np.arange(CELLS_X)[:, None]
    y = np.arange(CELLS_Y)[None, :]
    both = []
    for shift in (0, STRIDE):
        full = np.zeros((2, CENTERS_Y, PAD, CELLS_X, CELLS_Y))
        for side in range(2):
            for center in range(CENTERS_Y):
                for order_x in range(3):
                    for order_y in range(3):
                        full[side, center, order_x * 3 + order_y] = tap(
                            order_x, x - STRIDE * side
                        ) * tap(order_y, y - STRIDE * center - shift)
        wide = full[..., :MAIN_Y].reshape(2, CENTERS_Y * PAD, MAIN)
        edge = full[:, CENTERS_Y - 1, :, :, MAIN_Y:].reshape(2, PAD, REST)
        apart = np.zeros((2, 4, PAD, 4, REST))
        for member in range(4):
            apart[:, member, :, member, :] = edge
        groups = (wide, apart.reshape(2, 4 * PAD, 4 * REST))
        both.append(np.stack([np.concatenate(split_pieces(g), axis=1) for g in groups]))
    return np.stack(both)


def depth_weights():
    z = np.arange(WIDTH_Z)[:, None]
    centers = STRIDE * np.arange(CENTERS_Z)[None, :]
    full = np.zeros((CENTERS_Y, WIDTH_Z, 3, CENTERS_Y, CENTERS_Z))
    for order in range(3):
        for center in range(CENTERS_Y):
            full[center, :, order, center, :] = tap(order, z - centers)
    return full.reshape(CENTERS_Y * WIDTH_Z, 3 * TESTS).astype(ml_dtypes.bfloat16)


def column_codes():
    codes = np.full((3, PRODUCTS, PAD), -2.0, np.float32)
    for index, (a, b, c, e) in enumerate(POWERS):
        for order_z in range(3):
            for plane in range(9):
                codes[order_z, index, plane] = (
                    (((a * 3 + b) * 3 + c) * 3 + e) * 27 + plane * 3 + order_z
                )
    for field in range(4):
        codes[0, len(POWERS) + field, 0] = TARGET_CODE + field
    return codes.reshape(1, KEYS)


def others(value):
    return value, value + 1 - 2 * (value % 2), (value + 2) % 4, 3 - value


class Chips:
    def __init__(self):
        sub = lax.axis_index("sub")
        lib = lax.axis_index("lib")
        self.core = lib % 2
        self.x = others(sub // 8)
        self.y = others((sub // 4) % 2 * 2 + lib // 2)
        self.z = others(sub % 4)
        self.sub_x = [8 * v for v in self.x]
        self.sub_y = [v // 2 * 4 for v in self.y]
        self.lib_y = [v % 2 * 2 + self.core for v in self.y]
        self.chip_xy = [[16 * v + 4 * w for w in self.y] for v in self.x]

    def chip(self, d):
        return self.chip_xy[d // 16][d // 4 % 4] + self.z[d % 4]

    def device(self, d):
        return {
            "sub": self.sub_x[d // 16] + self.sub_y[d // 4 % 4] + self.z[d % 4],
            "lib": self.lib_y[d // 4 % 4],
        }


def widen(source_ref, wide_ref, base):
    for field in range(4):
        for x in range(CELLS_X):
            plane = source_ref[field, x].astype(f32)
            wide_ref[base + field, x * MAIN_Y : x * MAIN_Y + MAIN_Y, :] = plane[:MAIN_Y]
            wide_ref[base + field, MAIN + x * 8 : MAIN + x * 8 + 8, :] = plane[MAIN_Y:]


def products(wide_ref, theta_ref, rest_ref, changes):

    def some(at, lanes, put):
        value = [wide_ref[field, pl.ds(at, 16), lanes] for field in range(4)]
        if changes:
            for field in range(4):
                change = wide_ref[4 + field, pl.ds(at, 16), lanes] - value[field]
                put(len(POWERS) + field, change.astype(bf16))
            return
        square = [v * v for v in value]
        pairs = {}
        for index, powers in enumerate(POWERS):
            result = None
            key = ()
            for field, power in enumerate(powers):
                if power == 0:
                    continue
                factor = value[field] if power == 1 else square[field]
                key = key + ((field, power),)
                if result is None:
                    result = factor
                elif key in pairs:
                    result = pairs[key]
                else:
                    result = result * factor
                    pairs[key] = result
            put(index, result.astype(bf16))

    def main_rows(step, carry):
        at = pl.multiple_of(step * 16, 16)
        for half in range(2):

            def put(index, value, half=half):
                lane = index % 2 * WIDTH_Z + half * 128
                theta_ref[index // 2, pl.ds(at, 16), lane : lane + 128] = value

            some(at, slice(half * 128, half * 128 + 128), put)
        return carry

    def rest_rows(step, carry):
        at = pl.multiple_of(step * 16, 16)
        for half in range(2):
            lanes = slice(half * 128, half * 128 + 128)

            def put(index, value, lanes=lanes):
                rest_ref[index // 4, pl.ds(index % 4 * REST + at, 16), lanes] = value

            some(MAIN + at, lanes, put)
        return carry

    lax.fori_loop(0, MAIN // 16, main_rows, 0, unroll=4 if changes else 2)
    lax.fori_loop(0, REST // 16, rest_rows, 0, unroll=4 if changes else 2)
    used = PRODUCTS % 4 * REST
    rest_ref[PRODUCTS // 4, used:, :] = jnp.zeros((4 * REST - used, WIDTH_Z), bf16)


def plane_sums(weights_ref, theta_ref, rest_ref, rest_sum_ref, plane_ref, side):
    half = CENTERS_Y * PAD

    def leftover(index, carry):
        both = jnp.dot(weights_ref[1, side], rest_ref[index], preferred_element_type=f32)
        at = pl.multiple_of(index * half, half)
        rest_sum_ref[pl.ds(at, half), :] = both[:half] + both[half:]
        return carry

    def pair(index, carry):
        both = jnp.dot(weights_ref[0, side], theta_ref[index], preferred_element_type=f32)
        total = both[:half] + both[half:]
        for member in range(2):
            at = pl.multiple_of((index * 2 + member) * PAD, PAD)
            for center in range(CENTERS_Y):
                part = total[center * PAD : center * PAD + PAD, member * WIDTH_Z :][:, :WIDTH_Z]
                if center == CENTERS_Y - 1:
                    part = part + rest_sum_ref[pl.ds(at, PAD), :]
                lanes = slice(center * WIDTH_Z, (center + 1) * WIDTH_Z)
                high = part.astype(bf16)
                plane_ref[0, pl.ds(at, PAD), lanes] = high
                plane_ref[1, pl.ds(at, PAD), lanes] = (part - high.astype(f32)).astype(bf16)
        return carry

    lax.fori_loop(0, PRODUCTS // 4 + 1, leftover, 0, unroll=9)
    lax.fori_loop(0, PRODUCTS // 2, pair, 0, unroll=PRODUCTS // 2)


def depth_sums(plane_ref, depth_ref, table_ref, keep_low):
    size = TABLE // 2
    for start in range(0, TABLE, size):
        total = jnp.dot(
            plane_ref[0, start : start + size], depth_ref[...], preferred_element_type=f32
        )
        total = total + jnp.dot(
            plane_ref[1, start : start + size], depth_ref[...], preferred_element_type=f32
        )
        top = total.astype(bf16)
        rest = (total - top.astype(f32)).astype(bf16)
        for order in range(3):
            lanes = slice(order * TESTS, (order + 1) * TESTS)
            rows = slice(order * TABLE + start, order * TABLE + start + size)
            table_ref[rows, :TESTS] = top[:, lanes]
            if keep_low:
                table_ref[rows, TESTS:] = rest[:, lanes]


def pick_rows(code, keys_ref, pick_ref, start, count):
    spread = jnp.broadcast_to(code, (128, 128)).T
    for row in range(0, count, 16):
        for column in range(0, KEYS, 128):
            width = min(128, KEYS - column)
            same = spread[row : row + 16, :width] == keys_ref[:, column : column + width]
            pick_ref[pl.ds(start + row, 16), column : column + width] = jnp.where(
                same, 1.0, 0.0
            ).astype(bf16)


def whole_dot(left, right, contract):
    return lax.dot_general(
        left,
        right,
        (((1,), (contract,)), ((), ())),
        precision=lax.Precision.HIGHEST,
        preferred_element_type=f32,
    )


def solve(gram_ref, normal_ref, lib_ref, cross, target_squares, lib, result_ref, spot_ref):
    total = float(ROWS)
    diagonal_row = []
    diagonal_column = []
    same = lax.broadcasted_iota(jnp.int32, (128, 128), 0) == lax.broadcasted_iota(
        jnp.int32, (128, 128), 1
    )
    for block in range(4):
        at = slice(block * 128, block * 128 + 128)
        spread = jnp.where(same, gram_ref[at, at], 0.0)
        diagonal_row.append(jnp.sum(spread, axis=0, keepdims=True))
        diagonal_column.append(jnp.sum(spread, axis=1, keepdims=True))
    inverse_row = [1.0 / jnp.sqrt(d / total + EPSILON) for d in diagonal_row]
    inverse_column = [1.0 / jnp.sqrt(d / total + EPSILON) for d in diagonal_column]
    for i in range(4):
        for j in range(4):
            rows, lanes = slice(i * 128, i * 128 + 128), slice(j * 128, j * 128 + 128)
            block = gram_ref[rows, lanes] * (inverse_column[i] / total) * inverse_row[j]
            if i == j:
                block = block + jnp.where(same, RIDGE, 0.0)
            gram_ref[rows, lanes] = block
            high = block.astype(bf16)
            normal_ref[rows, lanes] = high
            normal_ref[rows, slice(TERMS + j * 128, TERMS + j * 128 + 128)] = (
                block - high.astype(f32)
            ).astype(bf16)
    inverse = jnp.concatenate(inverse_row, axis=1)
    target_scale = 1.0 / jnp.sqrt(target_squares / total + EPSILON)
    normal_cross = cross * inverse * (target_scale / total)

    def apply(rows):
        high = rows.astype(bf16)
        low = (rows - high.astype(f32)).astype(bf16)
        stacked = jnp.concatenate([high, low], axis=0)
        first = jnp.dot(stacked, normal_ref[:, :TERMS], preferred_element_type=f32)
        second = jnp.dot(high, normal_ref[:, TERMS:], preferred_element_type=f32)
        return first[:8] + first[8:] + second

    def fold(column):
        sums = [jnp.zeros((8, TERMS), f32) for _ in range(4)]
        for tile in range(TERMS // 8):
            rows = gram_ref[tile * 8 : tile * 8 + 8, :]
            if column is not None:
                rows = rows * column[tile]
            sums[tile % 4] = sums[tile % 4] + rows
        return jnp.sum((sums[0] + sums[1]) + (sums[2] + sums[3]), axis=0, keepdims=True)

    def spread(row):
        row = jnp.broadcast_to(row, (8, TERMS))
        return [
            jnp.sum(gram_ref[tile * 8 : tile * 8 + 8, :] * row, axis=1, keepdims=True)
            for tile in range(TERMS // 8)
        ]

    column = None
    for sweep in range(POWER // 2):
        row = fold(column)
        if sweep == 0:
            row = row * TERMS**-0.5
        column = spread(row)
    before = jnp.sum(row * row, axis=1, keepdims=True)
    after = column[0] * column[0]
    for tile in range(1, TERMS // 8):
        after = after + column[tile] * column[tile]
    after = jnp.sum(after, axis=0, keepdims=True)
    step_size = jnp.sqrt(before) / jnp.sqrt(after)
    bound = step_size * SHRINK
    coeffs = None
    for sweep in range(ITERS):
        if sweep == 0:
            moved = step_size * normal_cross
        else:
            moved = coeffs - step_size * (apply(coeffs) - normal_cross)
        coeffs = jnp.maximum(moved - bound, 0.0) - jnp.maximum(-moved - bound, 0.0)
    spot_ref[...] = coeffs
    own = pl.multiple_of(lib * 128, 128)
    result_ref[:8, :] = spot_ref[:, pl.ds(own, 128)]
    result_ref[8:, :] = whole_dot(coeffs * inverse, lib_ref[:TERMS], 0)


def kernel(
    exponents_hbm_ref,
    keys_hbm_ref,
    start_ref,
    end_ref,
    plane_weight_ref,
    depth_weight_ref,
    result_ref,
    exponents_ref,
    keys_ref,
    fields_ref,
    later_ref,
    own_fields_ref,
    own_later_ref,
    weights_ref,
    depth_ref,
    wide_ref,
    theta_ref,
    rest_ref,
    rest_sum_ref,
    plane_ref,
    table_ref,
    codes_ref,
    pick_ref,
    edge_out_ref,
    edge_in_ref,
    lib_ref,
    gram_ref,
    half_ref,
    half_in_ref,
    parts_in_ref,
    done_ref,
    normal_ref,
    spot_ref,
    local_sems,
    code_sems,
    edge_sems,
    core_sems,
    part_sems,
    done_sems,
    other_sems,
    ready_sems,
):
    sub = lax.axis_index("sub")
    lib = lax.axis_index("lib")
    chips = Chips()
    core = chips.core
    z = chips.z[0]
    edge_lib = (lib + 2 * ((z + 1) // 4)) % 4
    next_sub = {"sub": (sub + 1) % 32, "lib": edge_lib}
    last_sub = {"sub": (sub + 31) % 32, "lib": (lib + 2 * ((4 - z) // 4)) % 4}
    other_core = {"sub": sub, "lib": lib + 1 - 2 * core}
    def load(source_ref, target_ref, part, sem):
        rows = pl.ds(pl.multiple_of(jnp.maximum(part * 32 - 8, 0), 8), CELLS_Y)
        for field in range(4):
            pltpu.make_async_copy(
                source_ref.at[field, :, rows, :], target_ref.at[field], local_sems.at[sem]
            ).start()

    def loaded(target_ref, sem):
        pltpu.make_async_copy(target_ref, target_ref, local_sems.at[sem]).wait()

    load_exponents = pltpu.make_async_copy(exponents_hbm_ref, exponents_ref, local_sems.at[4])
    load_exponents.start()
    load(start_ref, fields_ref, edge_lib, 0)
    load_edge_weights = pltpu.make_async_copy(
        plane_weight_ref.at[jnp.minimum(edge_lib, 1), :, 1], weights_ref.at[:, 1], local_sems.at[2]
    )
    load_own_weights = pltpu.make_async_copy(
        plane_weight_ref.at[jnp.minimum(lib, 1), :, 0], weights_ref.at[:, 0], local_sems.at[8]
    )
    load_depth = pltpu.make_async_copy(depth_weight_ref, depth_ref, local_sems.at[3])
    load_keys = pltpu.make_async_copy(keys_hbm_ref, keys_ref, local_sems.at[5])

    barrier = pltpu.get_barrier_semaphore()

    near = [chips.device(d) for d in (1, 2, 3, 4, 8, 12, 16, 32, 48)]
    near += [{"sub": sub, "lib": (lib + step) % 4} for step in (1, 2, 3)]
    sends = sub < 31
    receives = sub > 0

    @pl.when(receives)
    def _():
        pl.semaphore_signal(barrier, inc=1, device_id=last_sub, device_id_type=MESH)

    for device in near:
        pl.semaphore_signal(barrier, inc=1, device_id=device, device_id_type=MESH)
    load(end_ref, later_ref, edge_lib, 1)
    load_edge_weights.start()
    load_depth.start()
    load_keys.start()
    load(start_ref, own_fields_ref, lib, 6)
    load(end_ref, own_later_ref, lib, 7)
    load_own_weights.start()
    load_exponents.wait()
    code = jnp.zeros((1, 128), f32)
    for place in range(7):
        code = code * 3.0 + exponents_ref[place : place + 1, :].astype(f32)
    codes_ref[lib] = jnp.broadcast_to(code, (8, 128))
    lane = lax.broadcasted_iota(jnp.int32, (8, 128), 1)
    codes_ref[4] = jnp.where(lane < 4, TARGET_CODE + lane, -1).astype(f32)

    loaded(fields_ref, 0)
    widen(fields_ref, wide_ref, 0)
    products(wide_ref, theta_ref, rest_ref, False)
    loaded(later_ref, 1)
    widen(later_ref, wide_ref, 4)
    products(wide_ref, theta_ref, rest_ref, True)
    pl.semaphore_wait(barrier, len(near) + jnp.minimum(31 - sub, 1))
    for device in near[6:9]:
        pl.semaphore_signal(ready_sems.at[0], inc=1, device_id=device, device_id_type=MESH)
    code_copies = [
        pltpu.make_async_remote_copy(
            src_ref=codes_ref.at[lib],
            dst_ref=codes_ref.at[lib],
            send_sem=code_sems.at[step],
            recv_sem=code_sems.at[3 + step],
            device_id={"sub": sub, "lib": (lib + 1 + step) % 4},
            device_id_type=MESH,
        )
        for step in range(3)
    ]
    for copy in code_copies:
        copy.start()
    load_edge_weights.wait()
    plane_sums(weights_ref, theta_ref, rest_ref, rest_sum_ref, plane_ref, 1)
    pl.semaphore_wait(ready_sems.at[0], 3)
    for device in near[3:6]:
        pl.semaphore_signal(ready_sems.at[1], inc=1, device_id=device, device_id_type=MESH)
    load_depth.wait()
    load_keys.wait()
    depth_sums(plane_ref, depth_ref, table_ref, False)
    edges = []

    def send_edge(number, code_row, start, count):
        rows = pl.ds(start, count)
        pick_rows(code_row, keys_ref, pick_ref, start, count)
        edge_out_ref[rows, :] = jnp.dot(
            pick_ref[rows, :], table_ref[:, :TESTS], preferred_element_type=f32
        ).astype(bf16)
        edge = pltpu.make_async_remote_copy(
            src_ref=edge_out_ref.at[rows],
            dst_ref=edge_in_ref.at[rows],
            send_sem=edge_sems.at[number],
            recv_sem=edge_sems.at[5 + number],
            device_id=next_sub,
            device_id_type=MESH,
        )
        edges.append(edge)

        @pl.when(sends)
        def _():
            edge.start()

    send_edge(0, code, pl.multiple_of(lib * 128, 128), 128)
    send_edge(1, codes_ref[4, :1, :], TERMS, 16)
    for step, copy in enumerate(code_copies):
        copy.wait_recv()
        part = (lib + 3 - step) % 4
        send_edge(2 + step, codes_ref[part, :1, :], pl.multiple_of(part * 128, 128), 128)
    loaded(own_fields_ref, 6)
    widen(own_fields_ref, wide_ref, 0)
    products(wide_ref, theta_ref, rest_ref, False)
    loaded(own_later_ref, 7)
    widen(own_later_ref, wide_ref, 4)
    products(wide_ref, theta_ref, rest_ref, True)
    load_own_weights.wait()
    plane_sums(weights_ref, theta_ref, rest_ref, rest_sum_ref, plane_ref, 0)
    depth_sums(plane_ref, depth_ref, table_ref, True)
    both = jnp.dot(pick_ref[...], table_ref[...], preferred_element_type=f32)
    lib_ref[...] = both[:, :TESTS] + both[:, TESTS:]
    @pl.when(receives)
    def _():
        for edge in edges:
            edge.wait_recv()
        lib_ref[...] = lib_ref[...] + edge_in_ref[...].astype(f32)

    high = lib_ref[...].astype(bf16)
    low = (lib_ref[...] - high.astype(f32)).astype(bf16)
    product = lax.dot_general(
        jnp.concatenate([high, low, high], axis=1),
        jnp.concatenate([high[:TERMS], high[:TERMS], low[:TERMS]], axis=1),
        (((1,), (1,)), ((), ())),
        preferred_element_type=f32,
    )
    cross = product[TERMS : TERMS + 8]
    target = lib_ref[TERMS : TERMS + 8]
    squares = jnp.sum(target * target, axis=1, keepdims=True)
    pairs = []
    for group in range(2):
        first = group * CHIPS // 2
        for half in range(2):
            for number in range(group * 2, group * 2 + 2):
                i, j = BLOCKS[half][number]
                lanes = slice(j * 128, j * 128 + 128)
                for part in range(16):
                    row = i * 128 + part * 8
                    half_ref[half, number * 16 + part, :8, :] = product[row : row + 8, lanes]
            i, j = BLOCKS[half][4]
            for part in range(first, first + CHIPS // 2):
                row = i * 128 + part * 2
                half_ref[half, part, 8:, :] = product[row : row + 2, j * 128 : j * 128 + 128]
        if group == 0:
            for piece in range(8):
                half_ref[0, 8 + piece // 2, piece % 2 * 4 : piece % 2 * 4 + 4, :64] = cross[
                    :4, piece * 64 : piece * 64 + 64
                ]
            half_ref[0, 12, :4, :64] = jnp.broadcast_to(squares[:4], (4, 64))
        chunks = pl.ds(first, CHIPS // 2)
        pair = pltpu.make_async_remote_copy(
            src_ref=half_ref.at[1 - core, chunks],
            dst_ref=half_in_ref.at[chunks],
            send_sem=core_sems.at[group],
            recv_sem=core_sems.at[2 + group],
            device_id=other_core,
            device_id_type=MESH,
        )
        pair.start()
        pairs.append(pair)
    for group, pair in enumerate(pairs):
        pair.wait_recv()
        chunks = pl.ds(group * CHIPS // 2, CHIPS // 2)
        half_in_ref[chunks] = half_in_ref[chunks] + half_ref[core, chunks]
    pl.semaphore_wait(ready_sems.at[1], 3)
    own = chips.chip(0)
    for d in PARTNERS:
        pltpu.make_async_remote_copy(
            src_ref=half_in_ref.at[chips.chip(d)],
            dst_ref=parts_in_ref.at[d],
            send_sem=part_sems.at[0],
            recv_sem=part_sems.at[1],
            device_id=chips.device(d),
            device_id_type=MESH,
        ).start()
    parts_in_ref[0] = half_in_ref[own]
    received = parts_in_ref.at[pl.ds(1, CHIPS - 1)]
    pltpu.make_async_copy(received, received, part_sems.at[1]).wait()
    done_ref[core, own] = jnp.sum(parts_in_ref[...], axis=0)
    for d in PARTNERS:
        pltpu.make_async_remote_copy(
            src_ref=done_ref.at[core, own],
            dst_ref=done_ref.at[core, own],
            send_sem=done_sems.at[0],
            recv_sem=done_sems.at[1],
            device_id=chips.device(d),
            device_id_type=MESH,
        ).start()
    pltpu.make_async_copy(received, received, done_sems.at[1]).wait()
    swap = pltpu.make_async_remote_copy(
        src_ref=done_ref.at[core],
        dst_ref=done_ref.at[core],
        send_sem=other_sems.at[0],
        recv_sem=other_sems.at[1],
        device_id=other_core,
        device_id_type=MESH,
    )
    swap.start()
    swap.wait_recv()
    for half in range(2):
        for number, (i, j) in enumerate(BLOCKS[half][:4]):
            lanes = slice(j * 128, j * 128 + 128)
            for part in range(16):
                row = i * 128 + part * 8
                gram_ref[row : row + 8, lanes] = done_ref[half, number * 16 + part, :8, :]
        i, j = BLOCKS[half][4]
        for part in range(CHIPS):
            row = i * 128 + part * 2
            gram_ref[row : row + 2, j * 128 : j * 128 + 128] = done_ref[half, part, 8:, :]
    cross_sum = jnp.concatenate(
        [
            jnp.concatenate(
                [gram_ref[64 + piece * 4 : 68 + piece * 4, :64] for piece in range(8)], axis=1
            ),
            jnp.zeros((4, TERMS), f32),
        ],
        axis=0,
    )
    square_sum = jnp.concatenate([gram_ref[96:100, :1], jnp.zeros((4, 1), f32)], axis=0)
    gram_ref[64:128, :64] = gram_ref[:64, 64:128].T
    for i in range(4):
        for j in range(i):
            gram_ref[i * 128 : i * 128 + 128, j * 128 : j * 128 + 128] = gram_ref[
                j * 128 : j * 128 + 128, i * 128 : i * 128 + 128
            ].T
    solve(
        gram_ref, normal_ref, lib_ref, cross_sum, square_sum, lib, result_ref, spot_ref
    )
    for copy in code_copies:
        copy.wait_send()
    for pair in pairs:
        pair.wait_send()
    pltpu.make_async_copy(received, received, part_sems.at[0]).wait()
    pltpu.make_async_copy(received, received, done_sems.at[0]).wait()
    swap.wait_send()

    @pl.when(sends)
    def _():
        for edge in edges:
            edge.wait_send()


def local(snap_start, snap_end, exponents):
    vmem = pl.BlockSpec(memory_space=pltpu.VMEM)
    anywhere = pl.BlockSpec(memory_space=pl.ANY)
    result = pl.pallas_call(
        kernel,
        out_shape=jax.ShapeDtypeStruct((16, TESTS), f32),
        in_specs=[anywhere] * 6,
        out_specs=vmem,
        scratch_shapes=[
            pltpu.VMEM((7, 128), jnp.int32),
            pltpu.VMEM((1, KEYS), f32),
            pltpu.VMEM((4, CELLS_X, CELLS_Y, WIDTH_Z), bf16),
            pltpu.VMEM((4, CELLS_X, CELLS_Y, WIDTH_Z), bf16),
            pltpu.VMEM((4, CELLS_X, CELLS_Y, WIDTH_Z), bf16),
            pltpu.VMEM((4, CELLS_X, CELLS_Y, WIDTH_Z), bf16),
            pltpu.VMEM((2, 2, 2 * CENTERS_Y * PAD, MAIN), bf16),
            pltpu.VMEM((CENTERS_Y * WIDTH_Z, 3 * TESTS), bf16),
            pltpu.VMEM((8, CELLS_XY, WIDTH_Z), f32),
            pltpu.VMEM((PRODUCTS // 2, MAIN, 2 * WIDTH_Z), bf16),
            pltpu.VMEM((PRODUCTS // 4 + 1, 4 * REST, WIDTH_Z), bf16),
            pltpu.VMEM(((PRODUCTS // 4 + 1) * 4 * PAD, WIDTH_Z), f32),
            pltpu.VMEM((2, TABLE, CENTERS_Y * WIDTH_Z), bf16),
            pltpu.VMEM((KEYS, 2 * TESTS), bf16),
            pltpu.VMEM((5, 8, 128), f32),
            pltpu.VMEM((PICKED, KEYS), bf16),
            pltpu.VMEM((PICKED, TESTS), bf16),
            pltpu.VMEM((PICKED, TESTS), bf16),
            pltpu.VMEM((PICKED, TESTS), f32),
            pltpu.VMEM((TERMS, TERMS), f32),
            pltpu.VMEM((2, CHIPS, CHUNK, 128), f32),
            pltpu.VMEM((CHIPS, CHUNK, 128), f32),
            pltpu.VMEM((CHIPS, CHUNK, 128), f32),
            pltpu.VMEM((2, CHIPS, CHUNK, 128), f32),
            pltpu.VMEM((TERMS, 2 * TERMS), bf16),
            pltpu.VMEM((8, TERMS), f32),
            pltpu.SemaphoreType.DMA((9,)),
            pltpu.SemaphoreType.DMA((6,)),
            pltpu.SemaphoreType.DMA((10,)),
            pltpu.SemaphoreType.DMA((4,)),
            pltpu.SemaphoreType.DMA((2,)),
            pltpu.SemaphoreType.DMA((2,)),
            pltpu.SemaphoreType.DMA((2,)),
            pltpu.SemaphoreType.REGULAR((2,)),
        ],
        compiler_params=pltpu.CompilerParams(
            collective_id=0, has_side_effects=True, vmem_limit_bytes=56 << 20
        ),
        name="weak_form_fit",
    )(
        exponents.T,
        jnp.asarray(column_codes()),
        snap_start,
        snap_end,
        jnp.asarray(plane_weights()),
        jnp.asarray(depth_weights()),
    )
    return result[:4], result[8:12]


def solution(mesh):
    placed = (P(None, "sub", None, None), P(None, "sub", None, None), P("lib", None))
    return jax.shard_map(
        local,
        mesh=mesh,
        in_specs=placed,
        out_specs=(P(None, "lib"), P(None, ("sub", "lib"))),
        check_vma=False,
    )
```
